128 devices in a mesh: role: 2 (over core), seq: 16 (over z, x), tp: 4 (over y).
Axes of the slice: x: 4, y: 4, z: 4, core: 2. Of those that a mesh axis runs over, the one named last changes fastest.
Arguments:
- merger_hidden: bfloat16 [2048, 5120], P(('role', 'seq'), 'tp'), may hold values from -6 to 6
- merger_out: bfloat16 [5120, 8192], P('tp', ('role', 'seq')), may hold values from -0.078125 to 0.078125
- row_position: int32 [2048], P(('role', 'seq')), may hold values from -1 to 8191, as said below
- prompt_embeds: bfloat16 [8192, 8192], P(('role', 'seq'), 'tp'), may hold values from -300 to 300
- norm_gain: bfloat16 [8192], P('tp'), may hold values from 0.099609375 to 1.8984375
- query_weight: bfloat16 [8192, 4096], P(None, 'tp'), may hold values from -2.762136 to 2.762136
- key_weight: bfloat16 [8192, 512], P(None, 'tp'), may hold values from -0.06629126 to 0.06629126
- value_weight: bfloat16 [8192, 512], P(None, 'tp'), may hold values from -0.0625 to 0.0625
Outputs:
- stream: bfloat16 [8192, 8192], P(('role', 'seq'), 'tp')
- context: bfloat16 [8192, 4096], P(('role', 'seq'), 'tp')
The draws below stay inside these ranges and needn't reach their ends.
Inputs may be any that keep to these rules, and one draw needn't show every extreme that they name: `row_position`: the live slots of each device's 64 come first and hold distinct prompt positions, distinct over all devices; the other slots hold -1. Of one device's slots at most 4 hold positions of one owner's block (positions j * 256 to (j + 1) * 256 - 1); every device has 4 or more live slots.
All inputs are finite; a program needn't handle non-finite values.
Results may differ from the reference program's by a relative error of at most 0.012.
The reference program's roundings to bfloat16 on the way (of `embeds`, `normed` and `rounded`) count: a program that leaves them out, or rounds other values in their place, can miss the bound.
Values may be sent and summed in bfloat16 or wider, within the bound.
A program may use at most 192 MiB of HBM per device.

```python
import math
import jax
import jax.numpy as jnp
from jax import lax

D = 8192
MH = 5120
HEAD_DIM = 128
HEADS = 32
KV_HEADS = 4
TOK_DEV = 256
ROW_DEV = 64
TOKENS = 8192
ROWS = 2048
CAP = 4


def draw_row_position(key, part):
    groups = ROWS // ROW_DEV
    capacity = CAP
    items = groups * capacity
    base_key = jax.random.fold_in(key, 11)
    subkeys = jax.random.split(base_key, 4)
    shared_owner = jax.random.randint(subkeys[0], (), 0, groups)
    full_device = jax.random.randint(subkeys[1], (), 0, groups)
    exponent = jax.random.randint(subkeys[2], (groups,), 0, 4)
    divisor = jnp.array([1, 2, 4, 8], jnp.int32)[exponent]
    live_count = jnp.maximum(capacity, ROW_DEV // divisor)
    live_count = jnp.where(jnp.arange(groups) == full_device, ROW_DEV, live_count)
    device_keys = jax.random.split(subkeys[3], groups)

    def one_device(device_key, device, count):
        pick_key, order_key = jax.random.split(device_key)
        entries = jnp.arange(items, dtype=jnp.int32)
        owners = entries // capacity
        offsets = entries % capacity
        ranking = jax.random.randint(pick_key, (items,), 0, 1 << 20) * items + entries
        ranking = jnp.where(owners == shared_owner, entries - items, ranking)
        chosen = jnp.argsort(ranking)[:ROW_DEV]
        spots = owners[chosen] * TOK_DEV + device * capacity + offsets[chosen]
        slots_all = jnp.arange(ROW_DEV, dtype=jnp.int32)
        shuffle = jax.random.randint(order_key, (ROW_DEV,), 0, 1 << 20) * ROW_DEV + slots_all
        shuffle = jnp.where(slots_all < count, shuffle, (1 << 30) + slots_all)
        spots = spots[jnp.argsort(shuffle)]
        return jnp.where(slots_all < count, spots, -1)
    result = jax.vmap(one_device)(device_keys, jnp.arange(groups, dtype=jnp.int32), live_count)
    return result.reshape(ROWS).astype(jnp.int32)


def draw_prompt_embeds(key, part):
    subkeys = jax.random.split(jax.random.fold_in(key, 23), 3)
    lift = jnp.arange(D, dtype=jnp.float32) / D
    column = 0.3 * jnp.exp(jnp.log(10.0) * lift) * jnp.exp(jax.random.uniform(subkeys[0], (D,), minval=-0.2, maxval=0.2))
    row_scale = jnp.exp(jax.random.uniform(subkeys[1], (TOKENS, 1), minval=0.0, maxval=jnp.log(10.0)))
    values = jnp.clip(jax.random.normal(subkeys[2], (TOKENS, D)), -6.0, 6.0) * column[None, :] * row_scale
    return values.astype(jnp.bfloat16)


def key_table(key):
    noise = jnp.clip(jax.random.normal(jax.random.fold_in(key, 41), (D, KV_HEADS * HEAD_DIM)), -6.0, 6.0)
    return noise * D ** (-0.5)


def draw_key_weight(key, part):
    return key_table(key).astype(jnp.bfloat16)


def draw_query_weight(key, part):
    noise = jnp.clip(jax.random.normal(jax.random.fold_in(key, 43), (D, HEADS * HEAD_DIM)), -6.0, 6.0) * D ** (-0.5)
    values = 3.0 * noise
    return values.astype(jnp.bfloat16)


def level_of(stream_key, shape, cuts, smallest, top_value):
    gain, own = 1.0, jax.random.fold_in(stream_key, 6)
    for dim, shards_of in cuts:
        draws = jnp.exp(jax.random.uniform(jax.random.fold_in(own, dim), (shards_of,), jnp.float32, smallest / len(cuts), top_value / len(cuts)))
        gain = gain * jnp.repeat(draws, shape[dim] // shards_of).reshape([-1 if axis == dim else 1 for axis in range(len(shape))])
    return gain


def centred(rng, extent, width, bound, cuts=(), kind=jnp.bfloat16):
    values = jax.random.normal(rng, extent, jnp.float32) * width
    if len(cuts) > 0:
        values = level_of(rng, extent, cuts, -0.22, 0.18) * values
    return jnp.clip(values, min=-bound, max=bound).astype(kind)


def setup_inputs(seed: int = 0) -> dict:
    key_of = jax.random.split(jax.random.key(seed), 9)
    merger_hidden = centred(key_of[0], (ROWS, MH), 1.0, 6.0, ((0, 32), (1, 4)))
    merger_out = centred(key_of[1], (MH, D), MH ** -0.5, 0.078125, ((0, 4), (1, 32)))
    row_position = draw_row_position(jax.random.fold_in(key_of[8], 71), 0)
    prompt_embeds = draw_prompt_embeds(jax.random.fold_in(key_of[8], 71), 0)
    norm_gain = jnp.clip(1.0 + 0.18 * jax.random.normal(key_of[4], (D,), jnp.float32), 0.099609375, 1.8984375).astype(jnp.bfloat16)
    query_weight = draw_query_weight(jax.random.fold_in(key_of[8], 71), 0)
    key_weight = draw_key_weight(jax.random.fold_in(key_of[8], 71), 0)
    value_weight = centred(key_of[7], (D, KV_HEADS * HEAD_DIM), D ** -0.5, 0.0625, ((1, 4),))
    return {"merger_hidden": merger_hidden, "merger_out": merger_out, "row_position": row_position, "prompt_embeds": prompt_embeds, "norm_gain": norm_gain, "query_weight": query_weight, "key_weight": key_weight, "value_weight": value_weight}


def rotate(vectors, positions):
    half_dim = vectors.shape[-1] // 2
    frequency = 1000000.0 ** (-jnp.arange(half_dim, dtype=jnp.float32) / half_dim)
    angles = positions.astype(jnp.float32)[:, None, None] * frequency[None, None, :]
    cosine = jnp.cos(angles)
    sine_part = jnp.sin(angles)
    lower_half = vectors[..., :half_dim]
    upper_half = vectors[..., half_dim:]
    return jnp.concatenate([lower_half * cosine - upper_half * sine_part, upper_half * cosine + lower_half * sine_part], axis=-1)

def reference(merger_hidden, merger_out, row_position, prompt_embeds, norm_gain, query_weight, key_weight, value_weight):
    embeds = jnp.dot(merger_hidden, merger_out, preferred_element_type=jnp.float32).astype(jnp.bfloat16)
    target = jnp.where(row_position >= 0, row_position, TOKENS).astype(jnp.int32)
    stream = prompt_embeds.at[target].set(embeds, mode='drop')
    widened = stream.astype(jnp.float32)
    inverse = lax.rsqrt(lax.optimization_barrier(jnp.sum(widened * widened, axis=1, keepdims=True)) / D + 1e-06)
    normed = (widened * inverse * norm_gain.astype(jnp.float32)[None, :]).astype(jnp.bfloat16)
    positions = jnp.arange(TOKENS, dtype=jnp.int32)
    query_sum = jnp.dot(normed, query_weight, preferred_element_type=jnp.float32)
    key_sum = jnp.dot(normed, key_weight, preferred_element_type=jnp.float32)
    value_sum = jnp.dot(normed, value_weight, preferred_element_type=jnp.float32)
    queries = rotate(query_sum.reshape(TOKENS, HEADS, HEAD_DIM), positions).astype(jnp.bfloat16)
    key_rows = rotate(key_sum.reshape(TOKENS, KV_HEADS, HEAD_DIM), positions).astype(jnp.bfloat16)
    value_rows = value_sum.astype(jnp.bfloat16).reshape(TOKENS, KV_HEADS, HEAD_DIM)
    group_size = HEADS // KV_HEADS
    block = math.gcd(TOKENS, 512)
    block_count = TOKENS // block
    score_scale = 1.0 / math.sqrt(HEAD_DIM)
    every_key = jnp.arange(TOKENS, dtype=jnp.int32)

    def one_block(block_id):
        kv_head = (block_id // block_count).astype(jnp.int32)
        first_row = (block_id % block_count * block).astype(jnp.int32)
        zero_index = jnp.zeros((), jnp.int32)
        query_block = lax.dynamic_slice(queries, (first_row, kv_head * group_size, zero_index), (block, group_size, HEAD_DIM)).astype(jnp.float32)
        key_block = lax.dynamic_slice(key_rows, (zero_index, kv_head, zero_index), (TOKENS, 1, HEAD_DIM))[:, 0].astype(jnp.float32)
        value_block = lax.dynamic_slice(value_rows, (zero_index, kv_head, zero_index), (TOKENS, 1, HEAD_DIM))[:, 0].astype(jnp.float32)
        scores = jnp.einsum('qgd,kd->gqk', query_block, key_block) * score_scale
        query_pos = first_row + jnp.arange(block, dtype=jnp.int32)
        visible = every_key[None, :] <= query_pos[:, None]
        scores = jnp.where(visible[None], scores, -jnp.inf)
        row_max = lax.optimization_barrier(jnp.max(scores, axis=2, keepdims=True))
        probability = jnp.exp(scores - row_max)
        row_sum = lax.optimization_barrier(jnp.sum(probability, axis=2))
        rounded = lax.optimization_barrier(probability.astype(jnp.bfloat16))
        mixed = jnp.einsum('gqk,kd->qgd', rounded.astype(jnp.float32), value_block)
        return (mixed / jnp.transpose(row_sum)[:, :, None]).astype(jnp.bfloat16)
    blocks = lax.map(one_block, jnp.arange(KV_HEADS * block_count, dtype=jnp.int32))
    context = blocks.reshape(KV_HEADS, block_count, block, group_size, HEAD_DIM)
    context = jnp.transpose(context, (1, 2, 0, 3, 4)).reshape(TOKENS, HEADS * HEAD_DIM)
    return (stream, context)
```

```python
import functools
import math

import jax
import jax.numpy as jnp
from jax import lax
from jax.experimental import pallas as pl
from jax.experimental.pallas import tpu as pltpu
from jax.sharding import PartitionSpec as P

HEAD_DIM = 128


def split_up(x, dim, length):
    before, after = (x.shape[:dim], x.shape[dim + 1 :])
    return jnp.moveaxis(x.reshape(*before, length, -1, *after), dim, 0)


def in_order(blocks, dim):
    lengths = list(blocks.shape[1:])
    lengths[dim] *= blocks.shape[0]
    return jnp.moveaxis(blocks, 0, dim).reshape(lengths)


def exchange_both(x, axis, axes, splits, concats):
    sizes = [lax.axis_size(a) for a in axes]
    blocks = split_up(x, splits[0], sizes[0])
    blocks = jnp.moveaxis(split_up(blocks, splits[1] + 1, sizes[1]), 0, 1)
    inside = blocks.shape[2:]
    blocks = blocks.reshape(-1, *inside)
    blocks = lax.all_to_all(blocks, axis, split_axis=0, concat_axis=0, tiled=True)
    blocks = in_order(blocks.reshape(*sizes, *inside), concats[0] + 1)
    return in_order(blocks, concats[1])


def sent_together(arrays, axis, dim, along):
    widths = [a.shape[along] for a in arrays]
    both = jnp.concatenate(arrays, axis=along)
    filled = lax.all_gather(both, axis, axis=dim, tiled=True)
    return tuple(jnp.split(filled, [sum(widths[:k]) for k in range(1, len(widths))], axis=along))


def rotate(vectors, positions):
    half_dim = vectors.shape[-1] // 2
    frequency = 1000000.0 ** (-jnp.arange(half_dim, dtype=jnp.float32) / half_dim)
    angles = positions.astype(jnp.float32)[:, None, None] * frequency[None, None, :]
    cosine = jnp.cos(angles)
    sine_part = jnp.sin(angles)
    lower_half = vectors[..., :half_dim]
    upper_half = vectors[..., half_dim:]
    return jnp.concatenate(
        [
            lower_half * cosine - upper_half * sine_part,
            upper_half * cosine + lower_half * sine_part,
        ],
        axis=-1,
    )


def sum_hidden(partial_value):
    return lax.psum_scatter(partial_value, "tp", scatter_dimension=1, tiled=True).astype(
        jnp.bfloat16
    )


def project_strips(merger_hidden, merger_out):
    return jnp.dot(
        lax.all_gather(merger_hidden, ("role", "seq"), axis=0, tiled=True),
        merger_out,
        preferred_element_type=jnp.float32,
    )


KEY_BLOCK = 1024


def attend_kernel(heads, q_ref, k_ref, v_ref, o_ref, acc, top, total):
    rows = q_ref.shape[0]
    first = (lax.axis_index("role") * lax.axis_size("seq") + lax.axis_index("seq")) * rows
    factor = math.log2(math.e) / math.sqrt(HEAD_DIM)
    acc[...] = jnp.zeros_like(acc)
    total[...] = jnp.zeros_like(total)
    top[...] = jnp.full_like(top, -1e30)

    def block(b, masked):
        start = pl.multiple_of(b * KEY_BLOCK, KEY_BLOCK)
        k = k_ref[pl.ds(start, KEY_BLOCK), :]
        v = v_ref[pl.ds(start, KEY_BLOCK), :]
        if masked:
            key_pos = start + lax.broadcasted_iota(jnp.int32, (rows, KEY_BLOCK), 1)
            query_pos = first + lax.broadcasted_iota(jnp.int32, (rows, KEY_BLOCK), 0)
            visible = key_pos <= query_pos
        for h in range(heads):
            q = q_ref[:, h * HEAD_DIM : (h + 1) * HEAD_DIM]
            s = lax.dot_general(
                q, k, (((1,), (1,)), ((), ())), preferred_element_type=jnp.float32
            )
            if masked:
                s = jnp.where(visible, s, -1e30)
            old = top[h][:, :1]
            new = jnp.maximum(old, jnp.max(s, axis=1, keepdims=True))
            p = jnp.exp2((s - new) * factor)
            alpha = jnp.exp2((old - new) * factor)
            part = p[:, :HEAD_DIM]
            for c in range(1, KEY_BLOCK // HEAD_DIM):
                part = part + p[:, c * HEAD_DIM : (c + 1) * HEAD_DIM]
            total[h] = total[h] * alpha + part
            acc[h] = acc[h] * alpha + jnp.dot(
                p.astype(jnp.bfloat16), v, preferred_element_type=jnp.float32
            )
            top[h] = jnp.broadcast_to(new, (rows, HEAD_DIM))

    full = first // KEY_BLOCK

    @pl.loop(0, full)
    def _(b):
        block(b, False)

    block(full, True)
    for h in range(heads):
        l = jnp.sum(total[h], axis=1, keepdims=True)
        o_ref[:, h * HEAD_DIM : (h + 1) * HEAD_DIM] = (acc[h] / l).astype(o_ref.dtype)


def attend(q, k, v, heads):
    rows = q.shape[0]
    vmem = pl.BlockSpec(memory_space=pltpu.VMEM)
    return pl.pallas_call(
        functools.partial(attend_kernel, heads),
        out_shape=jax.ShapeDtypeStruct(q.shape, jnp.bfloat16),
        in_specs=[vmem] * 3,
        out_specs=vmem,
        scratch_shapes=[pltpu.VMEM((heads, rows, HEAD_DIM), jnp.float32)] * 3,
        compiler_params=pltpu.CompilerParams(vmem_limit_bytes=48 << 20),
    )(q, k, v)


def body(
    merger_hidden,
    merger_out,
    row_position,
    prompt_embeds,
    norm_gain,
    query_weight,
    key_weight,
    value_weight,
):
    groups = lax.axis_size("role") * lax.axis_size("seq")
    device_rank = lax.axis_index(("role", "seq"))
    row_count = merger_hidden.shape[0]
    tok_count = prompt_embeds.shape[0]
    columns = prompt_embeds.shape[1]
    model_width = columns * lax.axis_size("tp")
    capacity = 2 * row_count // groups
    strips = project_strips(merger_hidden, merger_out)
    partial_value = lax.all_to_all(strips, ("role", "seq"), split_axis=0, concat_axis=1, tiled=True)
    embeds = sum_hidden(partial_value)
    owners = jnp.where(row_position >= 0, row_position // tok_count, groups)
    onehot = (owners[:, None] == jnp.arange(groups, dtype=jnp.int32)[None, :]).astype(jnp.int32)
    earlier = jnp.sum((jnp.cumsum(onehot, axis=0) - onehot) * onehot, axis=1)
    buffer_slot = jnp.where(owners < groups, owners * capacity + earlier, groups * capacity)
    source = (
        jnp.full((groups * capacity,), row_count, jnp.int32)
        .at[buffer_slot]
        .set(jnp.arange(row_count, dtype=jnp.int32), mode="drop")
    )
    padded = jnp.concatenate([embeds, jnp.zeros((1, columns), jnp.bfloat16)], axis=0)
    outgoing = padded[source].reshape(groups, capacity, columns)
    outgoing_pos = jnp.concatenate([row_position, jnp.full((1,), -1, jnp.int32)])[source].reshape(
        groups, capacity
    )
    role_count = lax.axis_size("role")
    seq_count = lax.axis_size("seq")
    arrived, arrived_pos = (
        exchange_both(
            outgoing.reshape(role_count, seq_count, capacity, columns),
            ("role", "seq"),
            ("role", "seq"),
            (0, 1),
            (0, 1),
        ),
        exchange_both(
            outgoing_pos.reshape(role_count, seq_count, capacity),
            ("role", "seq"),
            ("role", "seq"),
            (0, 1),
            (0, 1),
        ),
    )
    arrived_pos = arrived_pos.reshape(-1)
    local_row = jnp.where(arrived_pos >= 0, arrived_pos - device_rank * tok_count, tok_count)
    stream = prompt_embeds.at[local_row].set(arrived.reshape(-1, columns), mode="drop")
    widened = stream.astype(jnp.float32)
    squares = lax.psum(jnp.sum(widened * widened, axis=1), "tp")
    inverse = lax.rsqrt(squares / model_width + 1e-06)[:, None]
    normed = (widened * inverse * norm_gain.astype(jnp.float32)[None, :]).astype(jnp.bfloat16)
    tables = (query_weight, key_weight, value_weight)
    shard_piece = lax.all_gather(normed, "tp", axis=1, tiled=True)
    query_sum, key_sum, value_sum = tuple(
        (jnp.dot(shard_piece, table, preferred_element_type=jnp.float32) for table in tables)
    )
    local_heads = query_weight.shape[1] // HEAD_DIM
    local_kv = key_weight.shape[1] // HEAD_DIM
    positions = device_rank * tok_count + jnp.arange(tok_count, dtype=jnp.int32)
    queries = rotate(query_sum.reshape(tok_count, local_heads, HEAD_DIM), positions).astype(
        jnp.bfloat16
    )
    key_rows = rotate(key_sum.reshape(tok_count, local_kv, HEAD_DIM), positions).astype(
        jnp.bfloat16
    )
    value_rows = value_sum.astype(jnp.bfloat16).reshape(tok_count, local_kv, HEAD_DIM)
    key_piece, value_piece = sent_together((key_rows, value_rows), ("role", "seq"), 0, 1)
    context = attend(
        queries.reshape(tok_count, local_heads * HEAD_DIM),
        key_piece.reshape(-1, HEAD_DIM),
        value_piece.reshape(-1, HEAD_DIM),
        local_heads,
    )
    return (stream, context)


def solution(mesh):
    in_specs = (
        P(("role", "seq"), "tp"),
        P("tp", ("role", "seq")),
        P(("role", "seq")),
        P(("role", "seq"), "tp"),
        P("tp"),
        P(None, "tp"),
        P(None, "tp"),
        P(None, "tp"),
    )
    out_specs = (P(("role", "seq"), "tp"), P(("role", "seq"), "tp"))
    return jax.shard_map(body, mesh=mesh, in_specs=in_specs, out_specs=out_specs, check_vma=False)
```

```python
import functools
import math

import jax
import jax.numpy as jnp
from jax import lax
from jax.experimental import pallas as pl
from jax.experimental.pallas import tpu as pltpu
from jax.sharding import PartitionSpec as P

HEAD_DIM = 128


def sent_together(arrays, axis, dim, along):
    widths = [a.shape[along] for a in arrays]
    both = jnp.concatenate(arrays, axis=along)
    filled = lax.all_gather(both, axis, axis=dim, tiled=True)
    return tuple(jnp.split(filled, [sum(widths[:k]) for k in range(1, len(widths))], axis=along))


def rotate(vectors, positions):
    half_dim = vectors.shape[-1] // 2
    frequency = 1000000.0 ** (-jnp.arange(half_dim, dtype=jnp.float32) / half_dim)
    angles = positions.astype(jnp.float32)[:, None, None] * frequency[None, None, :]
    cosine = jnp.cos(angles)
    sine_part = jnp.sin(angles)
    lower_half = vectors[..., :half_dim]
    upper_half = vectors[..., half_dim:]
    return jnp.concatenate(
        [
            lower_half * cosine - upper_half * sine_part,
            upper_half * cosine + lower_half * sine_part,
        ],
        axis=-1,
    )


MESH = pl.DeviceIdType.MESH
SIDE = 4


def remote(src, dst, send_sem, recv_sem, role, seq, tp):
    return pltpu.make_async_remote_copy(
        src_ref=src,
        dst_ref=dst,
        send_sem=send_sem,
        recv_sem=recv_sem,
        device_id=(role, seq, tp),
        device_id_type=MESH,
    )


def plane_gather(buf, full_sem, half_sem, send_sem, between=()):
    role, seq, tp = lax.axis_index("role"), lax.axis_index("seq"), lax.axis_index("tp")
    step_a, step_b = 1 + 3 * role, 4 - 3 * role
    z, x = seq // SIDE, seq % SIDE
    ca = x + role * (z - x)
    cb = z + role * (x - z)
    half = buf.shape[1] // 2
    sent = []

    def seq_of(a, b):
        return ((ca + a + SIDE) % SIDE) * step_a + ((cb + b + SIDE) % SIDE) * step_b

    def slot_of(a, b):
        return role * (SIDE * SIDE) + seq_of(a, b)

    def whole(slot, to_role, to_seq):
        copy = remote(
            buf.at[slot], buf.at[slot], send_sem.at[len(sent)], full_sem.at[slot], to_role, to_seq, tp
        )
        copy.start()
        sent.append(copy)

    def part(slot, k, to_seq):
        piece = buf.at[slot, pl.ds(k * half, half)]
        copy = remote(
            piece, piece, send_sem.at[len(sent)], half_sem.at[slot, k], role, to_seq, tp
        )
        copy.start()
        sent.append(copy)

    def wait_whole(slot):
        pltpu.make_async_copy(buf.at[slot], buf.at[slot], full_sem.at[slot]).wait()

    def wait_parts(slot):
        for k in range(2):
            piece = buf.at[slot, pl.ds(k * half, half)]
            pltpu.make_async_copy(piece, piece, half_sem.at[slot, k]).wait()

    def spread_b(slot):
        whole(slot, role, seq_of(0, 1))
        whole(slot, role, seq_of(0, -1))
        whole(slot, 1 - role, seq)

    own = slot_of(0, 0)
    whole(own, role, seq_of(1, 0))
    whole(own, role, seq_of(-1, 0))
    spread_b(own)
    for a, k in ((-1, 0), (1, 1)):
        wait_whole(slot_of(a, 0))
        part(slot_of(a, 0), k, seq_of(-a, 0))
        spread_b(slot_of(a, 0))

    def pass_b(a):
        for b, k in ((-1, 0), (1, 1)):
            wait_whole(slot_of(a, b))
            part(slot_of(a, b), k, seq_of(0, -b))
            whole(slot_of(a, b), 1 - role, seq)

    pass_b(0)
    wait_parts(slot_of(2, 0))
    spread_b(slot_of(2, 0))
    for a in (-1, 1, 2):
        pass_b(a)
    for a in (0, -1, 1, 2):
        wait_parts(slot_of(a, 2))
        whole(slot_of(a, 2), 1 - role, seq)
    for s in range(SIDE * SIDE):
        wait_whole((1 - role) * (SIDE * SIDE) + s)
    for copy in sent:
        copy.wait_send()


PLANE_SENDS = 2 + 3 * 4 + 2 + 8 + 12


def iota(shape, dim):
    return lax.broadcasted_iota(jnp.int32, shape, dim).astype(jnp.float32)


def merge_kernel(
    hidden,
    weight,
    position,
    prompt,
    stream,
    buf,
    full_sem,
    half_sem,
    send_sem,
    partial,
    landed,
    y_send,
    y_recv,
    table,
    place,
    packed,
    arrived,
    d_send,
    d_recv,
):
    role, seq, tp = lax.axis_index("role"), lax.axis_index("seq"), lax.axis_index("tp")
    rank = role * lax.axis_size("seq") + seq
    rows, width = hidden.shape
    tokens = prompt.shape[0]
    groups = buf.shape[0]
    columns = weight.shape[1]
    capacity = 2 * rows // groups
    lane = lax.broadcasted_iota(jnp.int32, (rows, 128), 1)
    pos = jnp.broadcast_to(position[...], (rows, 128))
    owner = jnp.where(pos >= 0, pos // tokens, -1)
    rest = jnp.where(pos >= 0, pos % tokens, 0)
    code = jnp.where(lane == 0, owner, jnp.where(lane == 1, rest, 0))
    buf[rank, :, :width] = hidden[...]
    buf[rank, :, width:] = code.astype(jnp.float32).astype(jnp.bfloat16)
    plane_gather(buf, full_sem, half_sem, send_sem)

    quarter = groups // 4
    block = quarter * rows
    copies = []
    for i, off in enumerate((2, 1, 3, 0)):
        q = (tp + off) % 4
        left = buf[pl.ds(q * quarter, quarter), :, :width].reshape(block, width)
        value = jnp.dot(left, weight[...], preferred_element_type=jnp.float32)
        if off:
            partial[i] = value.astype(jnp.bfloat16)
            copy = remote(
                partial.at[i], landed.at[off - 1], y_send.at[i], y_recv.at[off - 1], role, seq, q
            )
            copy.start()
            copies.append(copy)
    mine = value

    some = 256
    batch = some // rows
    r0 = lax.broadcasted_iota(jnp.int32, (some, some), 0)
    r1 = lax.broadcasted_iota(jnp.int32, (some, some), 1)
    lower = jnp.where((r1 < r0) & (r1 // rows == r0 // rows), 1.0, 0.0).astype(jnp.bfloat16)
    source = (lax.broadcasted_iota(jnp.int32, (some, 1), 0) // rows).astype(jnp.float32)

    def decode(first):
        got = buf[pl.ds(first, batch), :, width:].reshape(some, 128).astype(jnp.float32)
        owner, rest = got[:, 0:1], got[:, 1:2]
        onehot = jnp.where(owner == iota((some, 128), 1), 1.0, 0.0)
        before = jnp.dot(lower, onehot.astype(jnp.bfloat16), preferred_element_type=jnp.float32)
        return owner, rest, jnp.sum(before * onehot, axis=1, keepdims=True)

    for n in range(quarter // batch):
        owner, rest, earlier = decode(tp * quarter + n * batch)
        slot = owner * (quarter * capacity) + (source + n * batch) * capacity + earlier
        table[n * some : (n + 1) * some, :] = jnp.where(
            slot == iota((some, table.shape[1]), 1), 1.0, 0.0
        ).astype(jnp.bfloat16)
    place[...] = jnp.zeros_like(place)

    @pl.loop(0, groups // batch)
    def _(n):
        owner, rest, earlier = decode(n * batch)
        here = (rest == iota((some, tokens), 1)) & (owner == rank.astype(jnp.float32))
        slot = (source + (n * batch).astype(jnp.float32)) * capacity + earlier
        there = slot == iota((some, 128), 1)
        place[...] += lax.dot_general(
            jnp.where(here, 1.0, 0.0).astype(jnp.bfloat16),
            jnp.where(there, 1.0, 0.0).astype(jnp.bfloat16),
            (((0,), (0,)), ((), ())),
            preferred_element_type=jnp.float32,
        )

    for k in range(3):
        pltpu.make_async_copy(landed.at[k], landed.at[k], y_recv.at[k]).wait()
        mine = mine + landed[k].astype(jnp.float32)
    packed[...] = lax.dot_general(
        table[...],
        mine.astype(jnp.bfloat16),
        (((0,), (0,)), ((), ())),
        preferred_element_type=jnp.float32,
    ).astype(jnp.bfloat16)

    piece = quarter * capacity
    to_tp = rank // 8
    lane_group = rank % 8

    def sending(i):
        j = (rank + i) % groups
        return remote(
            packed.at[pl.ds(pl.multiple_of(j * piece, piece), piece)],
            arrived.at[lane_group, pl.ds(pl.multiple_of(tp * piece, piece), piece)],
            d_send.at[i],
            d_recv.at[lane_group * 4 + tp],
            j // 16,
            j % 16,
            to_tp,
        )

    def staying():
        return pltpu.make_async_copy(
            packed.at[pl.ds(pl.multiple_of(rank * piece, piece), piece)],
            arrived.at[lane_group, pl.ds(pl.multiple_of(tp * piece, piece), piece)],
            d_recv.at[lane_group * 4 + tp],
        )

    @pl.when(to_tp == tp)
    def _():
        staying().start()

    @pl.when(to_tp != tp)
    def _():
        sending(0).start()

    @pl.loop(1, groups)
    def _(i):
        sending(i).start()

    chosen = place[...].astype(jnp.bfloat16)
    hit = jnp.max(place[...], axis=1, keepdims=True) > 0.5
    for c in range(8):
        for k in range(4):
            got = arrived.at[c, pl.ds(k * piece, piece)]
            pltpu.make_async_copy(got, got, d_recv.at[c * 4 + k]).wait()
        rows_here = jnp.dot(chosen, arrived[c], preferred_element_type=jnp.float32)
        span = slice(c * columns, (c + 1) * columns)
        stream[:, span] = jnp.where(
            hit, rows_here, prompt[:, span].astype(jnp.float32)
        ).astype(jnp.bfloat16)
    for copy in copies:
        copy.wait_send()

    @pl.when(to_tp != tp)
    def _():
        sending(0).wait_send()

    @pl.loop(1, groups)
    def _(i):
        sending(i).wait_send()


def merge(hidden, weight, position, prompt):
    rows, width = hidden.shape
    groups = lax.axis_size("role") * lax.axis_size("seq")
    columns = weight.shape[1]
    block = groups * rows // 4
    slots = groups * (groups // 4) * (2 * rows // groups)
    dma = pltpu.SemaphoreType.DMA
    vmem = pl.BlockSpec(memory_space=pltpu.VMEM)
    return pl.pallas_call(
        merge_kernel,
        out_shape=jax.ShapeDtypeStruct(prompt.shape, jnp.bfloat16),
        in_specs=[vmem] * 4,
        out_specs=vmem,
        scratch_shapes=[
            pltpu.VMEM((groups, rows, width + 128), jnp.bfloat16),
            dma((groups,)),
            dma((groups, 2)),
            dma((PLANE_SENDS,)),
            pltpu.VMEM((3, block, columns), jnp.bfloat16),
            pltpu.VMEM((3, block, columns), jnp.bfloat16),
            dma((3,)),
            dma((3,)),
            pltpu.VMEM((block, slots), jnp.bfloat16),
            pltpu.VMEM((prompt.shape[0], 128), jnp.float32),
            pltpu.VMEM((slots, columns), jnp.bfloat16),
            pltpu.VMEM((8, slots // 8, columns), jnp.bfloat16),
            dma((groups,)),
            dma((groups,)),
        ],
        compiler_params=pltpu.CompilerParams(
            has_side_effects=True, vmem_limit_bytes=48 << 20
        ),
    )(hidden, weight, position[:, None], prompt)


KEY_BLOCK = 1024


def attend_kernel(heads, q_ref, k_ref, v_ref, o_ref, acc, top, total):
    rows = q_ref.shape[0]
    first = (lax.axis_index("role") * lax.axis_size("seq") + lax.axis_index("seq")) * rows
    factor = math.log2(math.e) / math.sqrt(HEAD_DIM)
    acc[...] = jnp.zeros_like(acc)
    total[...] = jnp.zeros_like(total)
    top[...] = jnp.full_like(top, -1e30)

    def block(b, masked):
        start = pl.multiple_of(b * KEY_BLOCK, KEY_BLOCK)
        k = k_ref[pl.ds(start, KEY_BLOCK), :]
        v = v_ref[pl.ds(start, KEY_BLOCK), :]
        if masked:
            key_pos = start + lax.broadcasted_iota(jnp.int32, (rows, KEY_BLOCK), 1)
            query_pos = first + lax.broadcasted_iota(jnp.int32, (rows, KEY_BLOCK), 0)
            visible = key_pos <= query_pos
        for h in range(heads):
            q = q_ref[:, h * HEAD_DIM : (h + 1) * HEAD_DIM]
            s = lax.dot_general(
                q, k, (((1,), (1,)), ((), ())), preferred_element_type=jnp.float32
            )
            if masked:
                s = jnp.where(visible, s, -1e30)
            old = top[h][:, :1]
            new = jnp.maximum(old, jnp.max(s, axis=1, keepdims=True))
            p = jnp.exp2((s - new) * factor)
            alpha = jnp.exp2((old - new) * factor)
            part = p[:, :HEAD_DIM]
            for c in range(1, KEY_BLOCK // HEAD_DIM):
                part = part + p[:, c * HEAD_DIM : (c + 1) * HEAD_DIM]
            total[h] = total[h] * alpha + part
            acc[h] = acc[h] * alpha + jnp.dot(
                p.astype(jnp.bfloat16), v, preferred_element_type=jnp.float32
            )
            top[h] = jnp.broadcast_to(new, (rows, HEAD_DIM))

    full = first // KEY_BLOCK

    @pl.loop(0, full)
    def _(b):
        block(b, False)

    block(full, True)
    for h in range(heads):
        l = jnp.sum(total[h], axis=1, keepdims=True)
        o_ref[:, h * HEAD_DIM : (h + 1) * HEAD_DIM] = (acc[h] / l).astype(o_ref.dtype)


def attend(q, k, v, heads):
    rows = q.shape[0]
    vmem = pl.BlockSpec(memory_space=pltpu.VMEM)
    return pl.pallas_call(
        functools.partial(attend_kernel, heads),
        out_shape=jax.ShapeDtypeStruct(q.shape, jnp.bfloat16),
        in_specs=[vmem] * 3,
        out_specs=vmem,
        scratch_shapes=[pltpu.VMEM((heads, rows, HEAD_DIM), jnp.float32)] * 3,
        compiler_params=pltpu.CompilerParams(vmem_limit_bytes=48 << 20),
    )(q, k, v)


def body(
    merger_hidden,
    merger_out,
    row_position,
    prompt_embeds,
    norm_gain,
    query_weight,
    key_weight,
    value_weight,
):
    device_rank = lax.axis_index(("role", "seq"))
    tok_count = prompt_embeds.shape[0]
    columns = prompt_embeds.shape[1]
    model_width = columns * lax.axis_size("tp")
    stream = merge(merger_hidden, merger_out, row_position, prompt_embeds)
    widened = stream.astype(jnp.float32)
    squares = lax.psum(jnp.sum(widened * widened, axis=1), "tp")
    inverse = lax.rsqrt(squares / model_width + 1e-06)[:, None]
    normed = (widened * inverse * norm_gain.astype(jnp.float32)[None, :]).astype(jnp.bfloat16)
    tables = (query_weight, key_weight, value_weight)
    shard_piece = lax.all_gather(normed, "tp", axis=1, tiled=True)
    query_sum, key_sum, value_sum = tuple(
        (jnp.dot(shard_piece, table, preferred_element_type=jnp.float32) for table in tables)
    )
    local_heads = query_weight.shape[1] // HEAD_DIM
    local_kv = key_weight.shape[1] // HEAD_DIM
    positions = device_rank * tok_count + jnp.arange(tok_count, dtype=jnp.int32)
    queries = rotate(query_sum.reshape(tok_count, local_heads, HEAD_DIM), positions).astype(
        jnp.bfloat16
    )
    key_rows = rotate(key_sum.reshape(tok_count, local_kv, HEAD_DIM), positions).astype(
        jnp.bfloat16
    )
    value_rows = value_sum.astype(jnp.bfloat16).reshape(tok_count, local_kv, HEAD_DIM)
    key_piece, value_piece = sent_together((key_rows, value_rows), ("role", "seq"), 0, 1)
    context = attend(
        queries.reshape(tok_count, local_heads * HEAD_DIM),
        key_piece.reshape(-1, HEAD_DIM),
        value_piece.reshape(-1, HEAD_DIM),
        local_heads,
    )
    return (stream, context)


def solution(mesh):
    in_specs = (
        P(("role", "seq"), "tp"),
        P("tp", ("role", "seq")),
        P(("role", "seq")),
        P(("role", "seq"), "tp"),
        P("tp"),
        P(None, "tp"),
        P(None, "tp"),
        P(None, "tp"),
    )
    out_specs = (P(("role", "seq"), "tp"), P(("role", "seq"), "tp"))
    return jax.shard_map(body, mesh=mesh, in_specs=in_specs, out_specs=out_specs, check_vma=False)
```

```python
import functools
import math

import jax
import jax.numpy as jnp
from jax import lax
from jax.experimental import pallas as pl
from jax.experimental.pallas import tpu as pltpu
from jax.sharding import PartitionSpec as P

HEAD_DIM = 128


def rotary(positions):
    half_dim = HEAD_DIM // 2
    frequency = 1000000.0 ** (-jnp.arange(half_dim, dtype=jnp.float32) / half_dim)
    angles = positions.astype(jnp.float32)[:, None] * frequency[None, :]
    cosine, sine = jnp.cos(angles), jnp.sin(angles)
    return (
        jnp.concatenate([cosine, cosine], axis=1),
        jnp.concatenate([-sine, sine], axis=1),
    )


MESH = pl.DeviceIdType.MESH
SIDE = 4


def remote(src, dst, send_sem, recv_sem, role, seq, tp):
    return pltpu.make_async_remote_copy(
        src_ref=src,
        dst_ref=dst,
        send_sem=send_sem,
        recv_sem=recv_sem,
        device_id=(role, seq, tp),
        device_id_type=MESH,
    )


def plane_gather(buf, full_sem, half_sem, send_sem, between=()):
    role, seq, tp = lax.axis_index("role"), lax.axis_index("seq"), lax.axis_index("tp")
    step_a, step_b = 1 + 3 * role, 4 - 3 * role
    z, x = seq // SIDE, seq % SIDE
    ca = x + role * (z - x)
    cb = z + role * (x - z)
    half = buf.shape[1] // 2
    sent = []

    def seq_of(a, b):
        return ((ca + a + SIDE) % SIDE) * step_a + ((cb + b + SIDE) % SIDE) * step_b

    def slot_of(a, b):
        return role * (SIDE * SIDE) + seq_of(a, b)

    def whole(slot, to_role, to_seq):
        copy = remote(
            buf.at[slot], buf.at[slot], send_sem.at[len(sent)], full_sem.at[slot], to_role, to_seq, tp
        )
        copy.start()
        sent.append(copy)

    def part(slot, k, to_seq):
        piece = buf.at[slot, pl.ds(k * half, half)]
        copy = remote(
            piece, piece, send_sem.at[len(sent)], half_sem.at[slot, k], role, to_seq, tp
        )
        copy.start()
        sent.append(copy)

    def wait_whole(slot):
        pltpu.make_async_copy(buf.at[slot], buf.at[slot], full_sem.at[slot]).wait()

    def wait_parts(slot):
        for k in range(2):
            piece = buf.at[slot, pl.ds(k * half, half)]
            pltpu.make_async_copy(piece, piece, half_sem.at[slot, k]).wait()

    def spread_b(slot):
        whole(slot, role, seq_of(0, 1))
        whole(slot, role, seq_of(0, -1))
        whole(slot, 1 - role, seq)

    own = slot_of(0, 0)
    whole(own, role, seq_of(1, 0))
    whole(own, role, seq_of(-1, 0))
    spread_b(own)
    for a, k in ((-1, 0), (1, 1)):
        wait_whole(slot_of(a, 0))
        part(slot_of(a, 0), k, seq_of(-a, 0))
        spread_b(slot_of(a, 0))

    def pass_b(a):
        for b, k in ((-1, 0), (1, 1)):
            wait_whole(slot_of(a, b))
            part(slot_of(a, b), k, seq_of(0, -b))
            whole(slot_of(a, b), 1 - role, seq)

    pass_b(0)
    wait_parts(slot_of(2, 0))
    spread_b(slot_of(2, 0))
    for a in (-1, 1, 2):
        pass_b(a)
    for a in (0, -1, 1, 2):
        wait_parts(slot_of(a, 2))
        whole(slot_of(a, 2), 1 - role, seq)
    for s in range(SIDE * SIDE):
        wait_whole((1 - role) * (SIDE * SIDE) + s)
    for copy in sent:
        copy.wait_send()


PLANE_SENDS = 2 + 3 * 4 + 2 + 8 + 12


def iota(shape, dim):
    return lax.broadcasted_iota(jnp.int32, shape, dim).astype(jnp.float32)


def merge_kernel(
    hidden,
    weight,
    position,
    prompt,
    stream,
    buf,
    full_sem,
    half_sem,
    send_sem,
    partial,
    landed,
    y_send,
    y_recv,
    table,
    place,
    packed,
    arrived,
    d_send,
    d_recv,
):
    role, seq, tp = lax.axis_index("role"), lax.axis_index("seq"), lax.axis_index("tp")
    rank = role * lax.axis_size("seq") + seq
    rows, width = hidden.shape
    tokens = prompt.shape[0]
    groups = buf.shape[0]
    columns = weight.shape[1]
    capacity = 2 * rows // groups
    lane = lax.broadcasted_iota(jnp.int32, (rows, 128), 1)
    pos = jnp.broadcast_to(position[...], (rows, 128))
    owner = jnp.where(pos >= 0, pos // tokens, -1)
    rest = jnp.where(pos >= 0, pos % tokens, 0)
    code = jnp.where(lane == 0, owner, jnp.where(lane == 1, rest, 0))
    buf[rank, :, :width] = hidden[...]
    buf[rank, :, width:] = code.astype(jnp.float32).astype(jnp.bfloat16)
    plane_gather(buf, full_sem, half_sem, send_sem)

    quarter = groups // 4
    block = quarter * rows
    copies = []
    for i, off in enumerate((2, 1, 3, 0)):
        q = (tp + off) % 4
        left = buf[pl.ds(q * quarter, quarter), :, :width].reshape(block, width)
        value = jnp.dot(left, weight[...], preferred_element_type=jnp.float32)
        if off:
            partial[i] = value.astype(jnp.bfloat16)
            copy = remote(
                partial.at[i], landed.at[off - 1], y_send.at[i], y_recv.at[off - 1], role, seq, q
            )
            copy.start()
            copies.append(copy)
    mine = value

    some = 256
    batch = some // rows
    r0 = lax.broadcasted_iota(jnp.int32, (some, some), 0)
    r1 = lax.broadcasted_iota(jnp.int32, (some, some), 1)
    lower = jnp.where((r1 < r0) & (r1 // rows == r0 // rows), 1.0, 0.0).astype(jnp.bfloat16)
    source = (lax.broadcasted_iota(jnp.int32, (some, 1), 0) // rows).astype(jnp.float32)

    def decode(first):
        got = buf[pl.ds(first, batch), :, width:].reshape(some, 128).astype(jnp.float32)
        owner, rest = got[:, 0:1], got[:, 1:2]
        onehot = jnp.where(owner == iota((some, 128), 1), 1.0, 0.0)
        before = jnp.dot(lower, onehot.astype(jnp.bfloat16), preferred_element_type=jnp.float32)
        return owner, rest, jnp.sum(before * onehot, axis=1, keepdims=True)

    for n in range(quarter // batch):
        owner, rest, earlier = decode(tp * quarter + n * batch)
        slot = owner * (quarter * capacity) + (source + n * batch) * capacity + earlier
        table[n * some : (n + 1) * some, :] = jnp.where(
            slot == iota((some, table.shape[1]), 1), 1.0, 0.0
        ).astype(jnp.bfloat16)
    place[...] = jnp.zeros_like(place)

    @pl.loop(0, groups // batch)
    def _(n):
        owner, rest, earlier = decode(n * batch)
        here = (rest == iota((some, tokens), 1)) & (owner == rank.astype(jnp.float32))
        slot = (source + (n * batch).astype(jnp.float32)) * capacity + earlier
        there = slot == iota((some, 128), 1)
        place[...] += lax.dot_general(
            jnp.where(here, 1.0, 0.0).astype(jnp.bfloat16),
            jnp.where(there, 1.0, 0.0).astype(jnp.bfloat16),
            (((0,), (0,)), ((), ())),
            preferred_element_type=jnp.float32,
        )

    for k in range(3):
        pltpu.make_async_copy(landed.at[k], landed.at[k], y_recv.at[k]).wait()
        mine = mine + landed[k].astype(jnp.float32)
    packed[...] = lax.dot_general(
        table[...],
        mine.astype(jnp.bfloat16),
        (((0,), (0,)), ((), ())),
        preferred_element_type=jnp.float32,
    ).astype(jnp.bfloat16)

    piece = quarter * capacity
    to_tp = rank // 8
    lane_group = rank % 8

    def sending(i):
        j = (rank + i) % groups
        return remote(
            packed.at[pl.ds(pl.multiple_of(j * piece, piece), piece)],
            arrived.at[lane_group, pl.ds(pl.multiple_of(tp * piece, piece), piece)],
            d_send.at[i],
            d_recv.at[lane_group * 4 + tp],
            j // 16,
            j % 16,
            to_tp,
        )

    def staying():
        return pltpu.make_async_copy(
            packed.at[pl.ds(pl.multiple_of(rank * piece, piece), piece)],
            arrived.at[lane_group, pl.ds(pl.multiple_of(tp * piece, piece), piece)],
            d_recv.at[lane_group * 4 + tp],
        )

    @pl.when(to_tp == tp)
    def _():
        staying().start()

    @pl.when(to_tp != tp)
    def _():
        sending(0).start()

    @pl.loop(1, groups)
    def _(i):
        sending(i).start()

    chosen = place[...].astype(jnp.bfloat16)
    hit = jnp.max(place[...], axis=1, keepdims=True) > 0.5
    for c in range(8):
        for k in range(4):
            got = arrived.at[c, pl.ds(k * piece, piece)]
            pltpu.make_async_copy(got, got, d_recv.at[c * 4 + k]).wait()
        rows_here = jnp.dot(chosen, arrived[c], preferred_element_type=jnp.float32)
        span = slice(c * columns, (c + 1) * columns)
        stream[:, span] = jnp.where(
            hit, rows_here, prompt[:, span].astype(jnp.float32)
        ).astype(jnp.bfloat16)
    for copy in copies:
        copy.wait_send()

    @pl.when(to_tp != tp)
    def _():
        sending(0).wait_send()

    @pl.loop(1, groups)
    def _(i):
        sending(i).wait_send()


def merge(hidden, weight, position, prompt):
    rows, width = hidden.shape
    groups = lax.axis_size("role") * lax.axis_size("seq")
    columns = weight.shape[1]
    block = groups * rows // 4
    slots = groups * (groups // 4) * (2 * rows // groups)
    dma = pltpu.SemaphoreType.DMA
    vmem = pl.BlockSpec(memory_space=pltpu.VMEM)
    return pl.pallas_call(
        merge_kernel,
        out_shape=jax.ShapeDtypeStruct(prompt.shape, jnp.bfloat16),
        in_specs=[vmem] * 4,
        out_specs=vmem,
        scratch_shapes=[
            pltpu.VMEM((groups, rows, width + 128), jnp.bfloat16),
            dma((groups,)),
            dma((groups, 2)),
            dma((PLANE_SENDS,)),
            pltpu.VMEM((3, block, columns), jnp.bfloat16),
            pltpu.VMEM((3, block, columns), jnp.bfloat16),
            dma((3,)),
            dma((3,)),
            pltpu.VMEM((block, slots), jnp.bfloat16),
            pltpu.VMEM((prompt.shape[0], 128), jnp.float32),
            pltpu.VMEM((slots, columns), jnp.bfloat16),
            pltpu.VMEM((8, slots // 8, columns), jnp.bfloat16),
            dma((groups,)),
            dma((groups,)),
        ],
        compiler_params=pltpu.CompilerParams(
            has_side_effects=True, vmem_limit_bytes=48 << 20
        ),
    )(hidden, weight, position[:, None], prompt)


CHUNKS = 4


def project_kernel(
    eps,
    stream,
    gain,
    query_weight,
    key_weight,
    value_weight,
    cosine,
    sine,
    queries,
    both,
    normed,
    weights,
    acc,
    squares,
    w_sem,
    s_send,
    s_recv,
    n_send,
    n_recv,
):
    role, seq, tp = lax.axis_index("role"), lax.axis_index("seq"), lax.axis_index("tp")
    rows, columns = stream.shape
    chunk = columns // CHUNKS
    heads = queries.shape[1] // HEAD_DIM
    parts = ((query_weight, 0), (key_weight, heads), (value_weight, heads + 1))
    fetches = {}
    for i, off in enumerate((0, -1, 1, 2)):
        t = (tp + off + 4) % 4
        for k, (table, place) in enumerate(parts):
            span = pl.ds(pl.multiple_of(t * columns, columns), columns)
            lanes = pl.ds(place * HEAD_DIM, table.shape[1])
            copy = pltpu.make_async_copy(
                table.at[span], weights.at[span, lanes], w_sem.at[i, k]
            )
            copy.start()
            fetches[off, k] = copy

    total = jnp.zeros((rows, 128), jnp.float32)
    for c in range(columns // 128):
        x = stream[:, c * 128 : (c + 1) * 128].astype(jnp.float32)
        total = total + x * x
    squares[3] = jnp.broadcast_to(
        jnp.sum(jnp.transpose(total), axis=0, keepdims=True), (8, rows)
    )
    sums = []
    for k, off in enumerate((1, 3, 2)):
        copy = remote(
            squares.at[3], squares.at[k], s_send.at[k], s_recv.at[k], role, seq, (tp + off) % 4
        )
        copy.start()
        sums.append(copy)
    for copy in sums:
        copy.wait()
    whole = squares[0] + squares[1] + (squares[2] + squares[3])
    whole = jnp.broadcast_to(whole[0:1], (128, rows))
    inverse = lax.rsqrt(jnp.transpose(whole) / (4 * columns) + eps)[:, 0:1]

    copies = []

    def send(t, c, off):
        copy = remote(
            normed.at[t, c],
            normed.at[t, c],
            n_send.at[len(copies)],
            n_recv.at[t, c],
            role,
            seq,
            (tp + off + 4) % 4,
        )
        copy.start()
        copies.append(copy)

    def arrive(t, c):
        pltpu.make_async_copy(normed.at[t, c], normed.at[t, c], n_recv.at[t, c]).wait()

    def scale(c):
        span = slice(c * chunk, (c + 1) * chunk)
        x = stream[:, span].astype(jnp.float32)
        normed[tp, c] = (x * inverse * gain[:, span].astype(jnp.float32)).astype(jnp.bfloat16)

    scale(0)
    send(tp, 0, 1)
    scale(2)
    send(tp, 2, -1)
    scale(1)
    send(tp, 1, 1)
    scale(3)
    send(tp, 3, -1)
    send(tp, 2, 1)
    send(tp, 0, -1)
    send(tp, 3, 1)
    send(tp, 1, -1)
    before, after, across = (tp + 3) % 4, (tp + 1) % 4, (tp + 2) % 4

    def multiply(t, c, first=False):
        span = pl.ds(pl.multiple_of(t * columns + c * chunk, chunk), chunk)
        value = jnp.dot(normed[t, c], weights[span, :], preferred_element_type=jnp.float32)
        if first:
            acc[...] = value
        else:
            acc[...] += value

    def fetched(off):
        for k in range(len(parts)):
            fetches[off, k].wait()

    fetched(0)
    for c in range(CHUNKS):
        multiply(tp, c, c == 0)
    fetched(-1)
    fetched(1)
    for c, d in ((0, 2), (1, 3)):
        arrive(before, c)
        send(before, c, 1)
        arrive(after, d)
        send(after, d, -1)
        multiply(before, c)
        multiply(after, d)
    for c, d in ((2, 0), (3, 1)):
        arrive(before, c)
        multiply(before, c)
        arrive(after, d)
        multiply(after, d)
    fetched(2)
    for c in (0, 2, 1, 3):
        arrive(across, c)
        multiply(across, c)

    for h in range(heads + 1):
        span = slice(h * HEAD_DIM, (h + 1) * HEAD_DIM)
        u = acc[:, span]
        turned = u * cosine[...] + pltpu.roll(u, HEAD_DIM // 2, 1) * sine[...]
        if h < heads:
            queries[:, span] = turned.astype(jnp.bfloat16)
        else:
            both[:, :HEAD_DIM] = turned.astype(jnp.bfloat16)
    both[:, HEAD_DIM:] = acc[:, (heads + 1) * HEAD_DIM :].astype(jnp.bfloat16)
    for copy in copies:
        copy.wait_send()


def project(stream, gain, query_weight, key_weight, value_weight, cosine, sine):
    rows, columns = stream.shape
    wide = query_weight.shape[1] + 2 * HEAD_DIM
    dma = pltpu.SemaphoreType.DMA
    vmem = pl.BlockSpec(memory_space=pltpu.VMEM)
    hbm = pl.BlockSpec(memory_space=pl.ANY)
    return pl.pallas_call(
        functools.partial(project_kernel, 1e-06),
        out_shape=(
            jax.ShapeDtypeStruct((rows, query_weight.shape[1]), jnp.bfloat16),
            jax.ShapeDtypeStruct((rows, 2 * HEAD_DIM), jnp.bfloat16),
        ),
        in_specs=[vmem, vmem, hbm, hbm, hbm, vmem, vmem],
        out_specs=(vmem, vmem),
        scratch_shapes=[
            pltpu.VMEM((4, CHUNKS, rows, columns // CHUNKS), jnp.bfloat16),
            pltpu.VMEM((4 * columns, wide), jnp.bfloat16),
            pltpu.VMEM((rows, wide), jnp.float32),
            pltpu.VMEM((4, 8, rows), jnp.float32),
            dma((4, 3)),
            dma((3,)),
            dma((3,)),
            dma((3 * CHUNKS,)),
            dma((4, CHUNKS)),
        ],
        compiler_params=pltpu.CompilerParams(
            has_side_effects=True, vmem_limit_bytes=56 << 20
        ),
    )(stream, gain, query_weight, key_weight, value_weight, cosine, sine)


KEY_BLOCK = 1024


def attend_kernel(
    heads, q_ref, both, o_ref, buf, full_sem, half_sem, send_sem, acc, top, total
):
    rows = q_ref.shape[0]
    rank = lax.axis_index("role") * lax.axis_size("seq") + lax.axis_index("seq")
    first = rank * rows
    several = KEY_BLOCK // rows
    factor = math.log2(math.e) / math.sqrt(HEAD_DIM)
    buf[rank] = both[...]
    plane_gather(buf, full_sem, half_sem, send_sem)
    acc[...] = jnp.zeros_like(acc)
    total[...] = jnp.zeros_like(total)
    top[...] = jnp.full_like(top, -1e30)

    def block(b, masked):
        got = pl.ds(b * several, several)
        k = buf[got, :, :HEAD_DIM].reshape(KEY_BLOCK, HEAD_DIM)
        v = buf[got, :, HEAD_DIM:].reshape(KEY_BLOCK, HEAD_DIM)
        if masked:
            key_pos = b * KEY_BLOCK + lax.broadcasted_iota(jnp.int32, (rows, KEY_BLOCK), 1)
            query_pos = first + lax.broadcasted_iota(jnp.int32, (rows, KEY_BLOCK), 0)
            visible = key_pos <= query_pos
        for h in range(heads):
            q = q_ref[:, h * HEAD_DIM : (h + 1) * HEAD_DIM]
            s = lax.dot_general(
                q, k, (((1,), (1,)), ((), ())), preferred_element_type=jnp.float32
            )
            if masked:
                s = jnp.where(visible, s, -1e30)
            old = top[h][:, :1]
            new = jnp.maximum(old, jnp.max(s, axis=1, keepdims=True))
            p = jnp.exp2((s - new) * factor)
            alpha = jnp.exp2((old - new) * factor)
            part = p[:, :HEAD_DIM]
            for c in range(1, KEY_BLOCK // HEAD_DIM):
                part = part + p[:, c * HEAD_DIM : (c + 1) * HEAD_DIM]
            total[h] = total[h] * alpha + part
            acc[h] = acc[h] * alpha + jnp.dot(
                p.astype(jnp.bfloat16), v, preferred_element_type=jnp.float32
            )
            top[h] = jnp.broadcast_to(new, (rows, HEAD_DIM))

    full = first // KEY_BLOCK

    @pl.loop(0, full)
    def _(b):
        block(b, False)

    block(full, True)
    for h in range(heads):
        l = jnp.sum(total[h], axis=1, keepdims=True)
        o_ref[:, h * HEAD_DIM : (h + 1) * HEAD_DIM] = (acc[h] / l).astype(o_ref.dtype)


def attend(q, both):
    rows = q.shape[0]
    heads = q.shape[1] // HEAD_DIM
    groups = lax.axis_size("role") * lax.axis_size("seq")
    dma = pltpu.SemaphoreType.DMA
    vmem = pl.BlockSpec(memory_space=pltpu.VMEM)
    return pl.pallas_call(
        functools.partial(attend_kernel, heads),
        out_shape=jax.ShapeDtypeStruct(q.shape, jnp.bfloat16),
        in_specs=[vmem] * 2,
        out_specs=vmem,
        scratch_shapes=[
            pltpu.VMEM((groups, rows, 2 * HEAD_DIM), jnp.bfloat16),
            dma((groups,)),
            dma((groups, 2)),
            dma((PLANE_SENDS,)),
        ]
        + [pltpu.VMEM((heads, rows, HEAD_DIM), jnp.float32)] * 3,
        compiler_params=pltpu.CompilerParams(
            has_side_effects=True, vmem_limit_bytes=48 << 20
        ),
    )(q, both)


def body(
    merger_hidden,
    merger_out,
    row_position,
    prompt_embeds,
    norm_gain,
    query_weight,
    key_weight,
    value_weight,
):
    device_rank = lax.axis_index(("role", "seq"))
    tok_count = prompt_embeds.shape[0]
    stream = merge(merger_hidden, merger_out, row_position, prompt_embeds)
    positions = device_rank * tok_count + jnp.arange(tok_count, dtype=jnp.int32)
    cosine, sine = rotary(positions)
    queries, both = project(
        stream, norm_gain[None, :], query_weight, key_weight, value_weight, cosine, sine
    )
    context = attend(queries, both)
    return (stream, context)


def solution(mesh):
    in_specs = (
        P(("role", "seq"), "tp"),
        P("tp", ("role", "seq")),
        P(("role", "seq")),
        P(("role", "seq"), "tp"),
        P("tp"),
        P(None, "tp"),
        P(None, "tp"),
        P(None, "tp"),
    )
    out_specs = (P(("role", "seq"), "tp"), P(("role", "seq"), "tp"))
    return jax.shard_map(body, mesh=mesh, in_specs=in_specs, out_specs=out_specs, check_vma=False)
```

```python
import functools
import math

import jax
import jax.numpy as jnp
from jax import lax
from jax.experimental import pallas as pl
from jax.experimental.pallas import tpu as pltpu
from jax.sharding import PartitionSpec as P

HEAD_DIM = 128


def rotary(positions):
    half_dim = HEAD_DIM // 2
    frequency = 1000000.0 ** (-jnp.arange(half_dim, dtype=jnp.float32) / half_dim)
    angles = positions.astype(jnp.float32)[:, None] * frequency[None, :]
    cosine, sine = jnp.cos(angles), jnp.sin(angles)
    return (
        jnp.concatenate([cosine, cosine], axis=1),
        jnp.concatenate([-sine, sine], axis=1),
    )


MESH = pl.DeviceIdType.MESH
SIDE = 4


def remote(src, dst, send_sem, recv_sem, role, seq, tp):
    return pltpu.make_async_remote_copy(
        src_ref=src,
        dst_ref=dst,
        send_sem=send_sem,
        recv_sem=recv_sem,
        device_id=(role, seq, tp),
        device_id_type=MESH,
    )


def plane_gather(buf, full_sem, half_sem, send_sem, on_line=None):
    role, seq, tp = lax.axis_index("role"), lax.axis_index("seq"), lax.axis_index("tp")
    step_a, step_b = 1 + 3 * role, 4 - 3 * role
    z, x = seq // SIDE, seq % SIDE
    ca = x + role * (z - x)
    cb = z + role * (x - z)
    half = buf.shape[1] // 2
    sent = []

    def seq_of(a, b):
        return ((ca + a + SIDE) % SIDE) * step_a + ((cb + b + SIDE) % SIDE) * step_b

    def slot_of(a, b):
        return role * (SIDE * SIDE) + seq_of(a, b)

    def whole(slot, to_role, to_seq):
        copy = remote(
            buf.at[slot], buf.at[slot], send_sem.at[len(sent)], full_sem.at[slot], to_role, to_seq, tp
        )
        copy.start()
        sent.append(copy)

    def part(slot, k, to_seq):
        piece = buf.at[slot, pl.ds(k * half, half)]
        copy = remote(
            piece, piece, send_sem.at[len(sent)], half_sem.at[slot, k], role, to_seq, tp
        )
        copy.start()
        sent.append(copy)

    def wait_whole(slot):
        pltpu.make_async_copy(buf.at[slot], buf.at[slot], full_sem.at[slot]).wait()

    def wait_parts(slot):
        for k in range(2):
            piece = buf.at[slot, pl.ds(k * half, half)]
            pltpu.make_async_copy(piece, piece, half_sem.at[slot, k]).wait()

    def spread_b(slot):
        whole(slot, role, seq_of(0, 1))
        whole(slot, role, seq_of(0, -1))
        whole(slot, 1 - role, seq)

    own = slot_of(0, 0)
    whole(own, role, seq_of(1, 0))
    whole(own, role, seq_of(-1, 0))
    spread_b(own)
    for a, k in ((-1, 0), (1, 1)):
        wait_whole(slot_of(a, 0))
        part(slot_of(a, 0), k, seq_of(-a, 0))
        spread_b(slot_of(a, 0))

    def pass_b(a):
        for b, k in ((-1, 0), (1, 1)):
            wait_whole(slot_of(a, b))
            part(slot_of(a, b), k, seq_of(0, -b))
            whole(slot_of(a, b), 1 - role, seq)

    def line(b):
        if on_line is not None:
            on_line(role, (cb + b + SIDE) % SIDE)

    def other_line(b):
        fixed = (ca + b + SIDE) % SIDE
        for k in range(SIDE):
            wait_whole((1 - role) * (SIDE * SIDE) + fixed * step_a + k * step_b)
        if on_line is not None:
            on_line(1 - role, fixed)

    pass_b(0)
    wait_parts(slot_of(2, 0))
    spread_b(slot_of(2, 0))
    line(0)
    for a in (-1, 1):
        pass_b(a)
    other_line(0)
    pass_b(2)
    line(-1)
    line(1)
    other_line(-1)
    other_line(1)
    for a in (0, -1, 1, 2):
        wait_parts(slot_of(a, 2))
        whole(slot_of(a, 2), 1 - role, seq)
    line(2)
    other_line(2)
    return sent


PLANE_SENDS = 2 + 3 * 4 + 2 + 8 + 12
CHUNKS = 4
KEY_BLOCK = 1024


def iota(shape, dim):
    return lax.broadcasted_iota(jnp.int32, shape, dim).astype(jnp.float32)


def greet():
    role, seq, tp = lax.axis_index("role"), lax.axis_index("seq"), lax.axis_index("tp")
    z, x = seq // SIDE, seq % SIDE
    rank = role * (SIDE * SIDE) + seq
    barrier = pltpu.get_barrier_semaphore()

    def tell(to_role, to_seq, to_tp):
        pl.semaphore_signal(
            barrier, inc=1, device_id=(to_role, to_seq, to_tp), device_id_type=MESH
        )

    tell(1 - role, seq, tp)
    for k in (1, 3):
        tell(role, z * SIDE + (x + k) % SIDE, tp)
        tell(role, ((z + k) % SIDE) * SIDE + x, tp)
    for k in (1, 2, 3):
        tell(role, seq, (tp + k) % 4)

    @pl.loop(0, 32)
    def _(i):
        source = tp * 8 + i // 4

        @pl.when((source != rank) | (i % 4 != tp))
        def _():
            tell(source // 16, source % 16, i % 4)

    self_too = jnp.where(rank // 8 == tp, 1, 0)
    pl.semaphore_wait(barrier, 40 - self_too)


def merge_part(
    hidden, weight, position, prompt, stream, weight_here, prompt_here, m
):
    (
        buf,
        full_sem,
        half_sem,
        send_sem,
        partial,
        landed,
        mine,
        y_send,
        y_recv,
        table,
        place,
        packed,
        arrived,
        d_send,
        d_recv,
    ) = m
    role, seq, tp = lax.axis_index("role"), lax.axis_index("seq"), lax.axis_index("tp")
    rank = role * lax.axis_size("seq") + seq
    rows, width = hidden.shape
    tokens = prompt.shape[0]
    groups = buf.shape[0]
    columns = weight.shape[1]
    capacity = 2 * rows // groups
    quarter = groups // 4
    some = SIDE * rows
    copies = []

    def on_line(of_role, fixed):
        n = len(copies) // 3
        if n == 0:
            weight_here.wait()
        step_a, step_b = 1 + 3 * of_role, 4 - 3 * of_role
        pieces, spots = [], []
        for d in (2, 1, 3, 0):
            along = (tp + d + SIDE - fixed) % SIDE
            slot = of_role * (SIDE * SIDE) + along * step_a + fixed * step_b
            pieces.append(buf[slot, :, :width])
            spots.append(of_role * SIDE + fixed + of_role * (along - fixed))
        value = jnp.dot(
            jnp.concatenate(pieces, axis=0), weight[...], preferred_element_type=jnp.float32
        )
        for k, d in enumerate((2, 1, 3)):
            partial[n, k] = value[k * rows : (k + 1) * rows].astype(jnp.bfloat16)
            copy = remote(
                partial.at[n, k],
                landed.at[3 - d, spots[k]],
                y_send.at[n, k],
                y_recv.at[3 - d, spots[k]],
                role,
                seq,
                (tp + d) % 4,
            )
            copy.start()
            copies.append(copy)
        mine[spots[3]] = value[3 * rows :]

    sent = plane_gather(buf, full_sem, half_sem, send_sem, on_line)

    r0 = lax.broadcasted_iota(jnp.int32, (some, some), 0)
    r1 = lax.broadcasted_iota(jnp.int32, (some, some), 1)
    lower = jnp.where((r1 < r0) & (r1 // rows == r0 // rows), 1.0, 0.0).astype(jnp.bfloat16)
    source = lax.broadcasted_iota(jnp.int32, (some, 1), 0) // rows

    def decode(got):
        got = got.astype(jnp.float32)
        owner, rest = got[:, 0:1], got[:, 1:2]
        onehot = jnp.where(owner == iota((some, 128), 1), 1.0, 0.0)
        before = jnp.dot(lower, onehot.astype(jnp.bfloat16), preferred_element_type=jnp.float32)
        return owner, rest, jnp.sum(before * onehot, axis=1, keepdims=True)

    for n in range(quarter // SIDE):
        got = jnp.concatenate(
            [buf[n * 16 + z * SIDE + (tp + SIDE - z) % SIDE, :, width:] for z in range(SIDE)],
            axis=0,
        )
        owner, rest, earlier = decode(got)
        spot = (source + n * SIDE).astype(jnp.float32)
        slot = owner * (quarter * capacity) + spot * capacity + earlier
        table[n * some : (n + 1) * some, :] = jnp.where(
            slot == iota((some, table.shape[1]), 1), 1.0, 0.0
        ).astype(jnp.bfloat16)
    place[...] = jnp.zeros_like(place)

    @pl.loop(0, groups // SIDE)
    def _(n):
        got = buf[pl.ds(n * SIDE, SIDE), :, width:].reshape(some, 128)
        owner, rest, earlier = decode(got)
        here = (rest == iota((some, tokens), 1)) & (owner == rank.astype(jnp.float32))
        spot = ((source + n % SIDE) % SIDE) * quarter + n
        slot = spot.astype(jnp.float32) * capacity + earlier
        there = slot == iota((some, 128), 1)
        place[...] += lax.dot_general(
            jnp.where(here, 1.0, 0.0).astype(jnp.bfloat16),
            jnp.where(there, 1.0, 0.0).astype(jnp.bfloat16),
            (((0,), (0,)), ((), ())),
            preferred_element_type=jnp.float32,
        )

    for i in range(quarter):
        for k in range(3):
            got = landed.at[k, i]
            pltpu.make_async_copy(got, got, y_recv.at[k, i]).wait()
            mine[i] += landed[k, i].astype(jnp.float32)
    packed[...] = lax.dot_general(
        table[...],
        mine[...].reshape(quarter * rows, columns).astype(jnp.bfloat16),
        (((0,), (0,)), ((), ())),
        preferred_element_type=jnp.float32,
    ).astype(jnp.bfloat16)

    piece = quarter * capacity
    to_tp = rank // 8
    lane_group = rank % 8

    def sending(i):
        j = (rank + i) % groups
        return remote(
            packed.at[pl.ds(pl.multiple_of(j * piece, piece), piece)],
            arrived.at[lane_group, pl.ds(pl.multiple_of(tp * piece, piece), piece)],
            d_send.at[i],
            d_recv.at[lane_group * 4 + tp],
            j // 16,
            j % 16,
            to_tp,
        )

    def staying():
        return pltpu.make_async_copy(
            packed.at[pl.ds(pl.multiple_of(rank * piece, piece), piece)],
            arrived.at[lane_group, pl.ds(pl.multiple_of(tp * piece, piece), piece)],
            d_recv.at[lane_group * 4 + tp],
        )

    @pl.when(to_tp == tp)
    def _():
        staying().start()

    @pl.when(to_tp != tp)
    def _():
        sending(0).start()

    @pl.loop(1, groups)
    def _(i):
        sending(i).start()

    chosen = place[...].astype(jnp.bfloat16)
    hit = jnp.max(place[...], axis=1, keepdims=True) > 0.5
    prompt_here.wait()
    total = jnp.zeros((tokens, 128), jnp.float32)
    for c in range(8):
        for k in range(4):
            got = arrived.at[c, pl.ds(k * piece, piece)]
            pltpu.make_async_copy(got, got, d_recv.at[c * 4 + k]).wait()
        rows_here = jnp.dot(chosen, arrived[c], preferred_element_type=jnp.float32)
        span = slice(c * columns, (c + 1) * columns)
        x = jnp.where(hit, rows_here, prompt[:, span].astype(jnp.float32))
        stream[:, span] = x.astype(jnp.bfloat16)
        for k in range(0, columns, 128):
            total = total + x[:, k : k + 128] * x[:, k : k + 128]

    def finish():
        for copy in copies + sent:
            copy.wait_send()

        @pl.when(to_tp != tp)
        def _():
            sending(0).wait_send()

        @pl.loop(1, groups)
        def _(i):
            sending(i).wait_send()

    return total, finish


def project_part(eps, total, stream, gain, tables_here, acc, m):
    normed, weights, squares, s_send, s_recv, n_send, n_recv = m
    role, seq, tp = lax.axis_index("role"), lax.axis_index("seq"), lax.axis_index("tp")
    rows, columns = stream.shape
    chunk = columns // CHUNKS
    squares[3] = jnp.broadcast_to(
        jnp.sum(jnp.transpose(total), axis=0, keepdims=True), (8, rows)
    )
    sums = []
    for k, off in enumerate((1, 3, 2)):
        copy = remote(
            squares.at[3], squares.at[k], s_send.at[k], s_recv.at[k], role, seq, (tp + off) % 4
        )
        copy.start()
        sums.append(copy)
    for copy in sums:
        copy.wait()
    whole = squares[0] + squares[1] + (squares[2] + squares[3])
    whole = jnp.broadcast_to(whole[0:1], (128, rows))
    inverse = lax.rsqrt(jnp.transpose(whole) / (4 * columns) + eps)[:, 0:1]

    copies = []

    def send(t, c, off):
        copy = remote(
            normed.at[t, c],
            normed.at[t, c],
            n_send.at[len(copies)],
            n_recv.at[t, c],
            role,
            seq,
            (tp + off + 4) % 4,
        )
        copy.start()
        copies.append(copy)

    def arrive(t, c):
        pltpu.make_async_copy(normed.at[t, c], normed.at[t, c], n_recv.at[t, c]).wait()

    def scale(c):
        span = slice(c * chunk, (c + 1) * chunk)
        x = stream[:, span].astype(jnp.float32)
        normed[tp, c] = (x * inverse * gain[:, span].astype(jnp.float32)).astype(jnp.bfloat16)

    scale(0)
    send(tp, 0, 1)
    scale(2)
    send(tp, 2, -1)
    scale(1)
    send(tp, 1, 1)
    scale(3)
    send(tp, 3, -1)
    send(tp, 2, 1)
    send(tp, 0, -1)
    send(tp, 3, 1)
    send(tp, 1, -1)
    before, after, across = (tp + 3) % 4, (tp + 1) % 4, (tp + 2) % 4

    def multiply(t, c, first=False):
        span = pl.ds(pl.multiple_of(t * columns + c * chunk, chunk), chunk)
        value = jnp.dot(normed[t, c], weights[span, :], preferred_element_type=jnp.float32)
        if first:
            acc[...] = value
        else:
            acc[...] += value

    for copy in tables_here:
        copy.wait()
    for c in range(CHUNKS):
        multiply(tp, c, c == 0)
    for c, d in ((0, 2), (1, 3)):
        arrive(before, c)
        send(before, c, 1)
        arrive(after, d)
        send(after, d, -1)
        multiply(before, c)
        multiply(after, d)
    for c, d in ((2, 0), (3, 1)):
        arrive(before, c)
        multiply(before, c)
        arrive(after, d)
        multiply(after, d)
    for c in (0, 2, 1, 3):
        arrive(across, c)
        multiply(across, c)

    def finish():
        for copy in copies:
            copy.wait_send()

    return finish


def attend_part(q_ref, buf, o_ref, acc, top, total):
    rows = q_ref.shape[0]
    heads = q_ref.shape[1] // HEAD_DIM
    rank = lax.axis_index("role") * lax.axis_size("seq") + lax.axis_index("seq")
    first = rank * rows
    several = KEY_BLOCK // rows
    factor = math.log2(math.e) / math.sqrt(HEAD_DIM)
    acc[...] = jnp.zeros_like(acc)
    total[...] = jnp.zeros_like(total)
    top[...] = jnp.full_like(top, -1e30)

    def block(b, masked):
        got = pl.ds(b * several, several)
        k = buf[got, :, :HEAD_DIM].reshape(KEY_BLOCK, HEAD_DIM)
        v = buf[got, :, HEAD_DIM:].reshape(KEY_BLOCK, HEAD_DIM)
        if masked:
            key_pos = b * KEY_BLOCK + lax.broadcasted_iota(jnp.int32, (rows, KEY_BLOCK), 1)
            query_pos = first + lax.broadcasted_iota(jnp.int32, (rows, KEY_BLOCK), 0)
            visible = key_pos <= query_pos
        for h in range(heads):
            q = q_ref[:, h * HEAD_DIM : (h + 1) * HEAD_DIM]
            s = lax.dot_general(
                q, k, (((1,), (1,)), ((), ())), preferred_element_type=jnp.float32
            )
            if masked:
                s = jnp.where(visible, s, -1e30)
            old = top[h][:, :1]
            new = jnp.maximum(old, jnp.max(s, axis=1, keepdims=True))
            p = jnp.exp2((s - new) * factor)
            alpha = jnp.exp2((old - new) * factor)
            part = p[:, :HEAD_DIM]
            for c in range(1, KEY_BLOCK // HEAD_DIM):
                part = part + p[:, c * HEAD_DIM : (c + 1) * HEAD_DIM]
            total[h] = total[h] * alpha + part
            acc[h] = acc[h] * alpha + jnp.dot(
                p.astype(jnp.bfloat16), v, preferred_element_type=jnp.float32
            )
            top[h] = jnp.broadcast_to(new, (rows, HEAD_DIM))

    full = first // KEY_BLOCK

    @pl.loop(0, full)
    def _(b):
        block(b, False)

    block(full, True)
    for h in range(heads):
        l = jnp.sum(total[h], axis=1, keepdims=True)
        o_ref[:, h * HEAD_DIM : (h + 1) * HEAD_DIM] = (acc[h] / l).astype(o_ref.dtype)


MERGE_SCRATCH = 15
PROJECT_SCRATCH = 7


def kernel(
    hidden,
    merger_out,
    position,
    prompt,
    gain,
    query_weight,
    key_weight,
    value_weight,
    cosine,
    sine,
    stream_out,
    context_out,
    merger_here,
    prompt_here,
    stream,
    queries,
    cosine_here,
    sine_here,
    sums,
    keys,
    k_full,
    k_half,
    k_send,
    acc,
    top,
    total,
    in_sem,
    w_sem,
    *more,
):
    m, p = more[:MERGE_SCRATCH], more[MERGE_SCRATCH:]
    role, seq, tp = lax.axis_index("role"), lax.axis_index("seq"), lax.axis_index("tp")
    rank = role * lax.axis_size("seq") + seq
    rows, width = hidden.shape
    tokens = prompt.shape[0]
    columns = prompt.shape[1]
    heads = query_weight.shape[1] // HEAD_DIM

    fetches = []
    for k, (src, dst) in enumerate(
        (
            (merger_out, merger_here),
            (prompt, prompt_here),
            (cosine, cosine_here),
            (sine, sine_here),
        )
    ):
        copy = pltpu.make_async_copy(src, dst, in_sem.at[k])
        copy.start()
        fetches.append(copy)
    weights = p[1]
    tables_here = []
    for i in range(4):
        for k, (table, spot) in enumerate(
            ((query_weight, 0), (key_weight, heads), (value_weight, heads + 1))
        ):
            span = pl.ds(i * columns, columns)
            lanes = pl.ds(spot * HEAD_DIM, table.shape[1])
            copy = pltpu.make_async_copy(
                table.at[span], weights.at[span, lanes], w_sem.at[i, k]
            )
            copy.start()
            tables_here.append(copy)

    lane = lax.broadcasted_iota(jnp.int32, (rows, 128), 1)
    pos = jnp.transpose(jnp.broadcast_to(position[...], (128, rows)))
    owner = jnp.where(pos >= 0, pos // tokens, -1)
    rest = jnp.where(pos >= 0, pos % tokens, 0)
    code = jnp.where(lane == 0, owner, jnp.where(lane == 1, rest, 0))
    buf = m[0]
    buf[rank, :, :width] = hidden[...]
    buf[rank, :, width:] = code.astype(jnp.float32).astype(jnp.bfloat16)
    greet()
    squares, merged = merge_part(
        hidden, merger_here, position, prompt_here, stream, fetches[0], fetches[1], m
    )
    stream_sent = pltpu.make_async_copy(stream, stream_out, in_sem.at[4])
    stream_sent.start()
    projected = project_part(1e-06, squares, stream, gain, tables_here, sums, p)
    fetches[2].wait()
    fetches[3].wait()

    def turned(h):
        u = sums[:, h * HEAD_DIM : (h + 1) * HEAD_DIM]
        u = u * cosine_here[...] + pltpu.roll(u, HEAD_DIM // 2, 1) * sine_here[...]
        return u.astype(jnp.bfloat16)

    keys[rank, :, :HEAD_DIM] = turned(heads)
    keys[rank, :, HEAD_DIM:] = sums[:, (heads + 1) * HEAD_DIM :].astype(jnp.bfloat16)
    for h in range(heads):
        queries[:, h * HEAD_DIM : (h + 1) * HEAD_DIM] = turned(h)
    k_sent = plane_gather(keys, k_full, k_half, k_send)
    attend_part(queries, keys, context_out, acc, top, total)
    stream_sent.wait()
    for copy in k_sent:
        copy.wait_send()
    projected()
    merged()


def together(hidden, merger_out, position, prompt, gain, wq, wk, wv, cosine, sine):
    rows, width = hidden.shape
    groups = lax.axis_size("role") * lax.axis_size("seq")
    tokens, columns = prompt.shape
    strip = merger_out.shape[1]
    quarter = groups // 4
    slots = groups * quarter * (2 * rows // groups)
    heads = wq.shape[1] // HEAD_DIM
    wide = wq.shape[1] + 2 * HEAD_DIM
    dma = pltpu.SemaphoreType.DMA
    vmem = pl.BlockSpec(memory_space=pltpu.VMEM)
    hbm = pl.BlockSpec(memory_space=pl.ANY)
    bf16, f32 = jnp.bfloat16, jnp.float32
    return pl.pallas_call(
        kernel,
        out_shape=(
            jax.ShapeDtypeStruct(prompt.shape, bf16),
            jax.ShapeDtypeStruct((tokens, wq.shape[1]), bf16),
        ),
        in_specs=[vmem, hbm, vmem, hbm, vmem, hbm, hbm, hbm, hbm, hbm],
        out_specs=(hbm, vmem),
        scratch_shapes=[
            pltpu.VMEM(merger_out.shape, bf16),
            pltpu.VMEM(prompt.shape, bf16),
            pltpu.VMEM(prompt.shape, bf16),
            pltpu.VMEM((tokens, wq.shape[1]), bf16),
            pltpu.VMEM(cosine.shape, f32),
            pltpu.VMEM(sine.shape, f32),
            pltpu.VMEM((tokens, wide), f32),
            pltpu.VMEM((groups, tokens, 2 * HEAD_DIM), bf16),
            dma((groups,)),
            dma((groups, 2)),
            dma((PLANE_SENDS,)),
            pltpu.VMEM((heads, tokens, HEAD_DIM), f32),
            pltpu.VMEM((heads, tokens, HEAD_DIM), f32),
            pltpu.VMEM((heads, tokens, HEAD_DIM), f32),
            dma((5,)),
            dma((4, 3)),
            pltpu.VMEM((groups, rows, width + 128), bf16),
            dma((groups,)),
            dma((groups, 2)),
            dma((PLANE_SENDS,)),
            pltpu.VMEM((8, 3, rows, strip), bf16),
            pltpu.VMEM((3, quarter, rows, strip), bf16),
            pltpu.VMEM((quarter, rows, strip), f32),
            dma((8, 3)),
            dma((3, quarter)),
            pltpu.VMEM((quarter * rows, slots), bf16),
            pltpu.VMEM((tokens, 128), f32),
            pltpu.VMEM((slots, strip), bf16),
            pltpu.VMEM((8, slots // 8, strip), bf16),
            dma((groups,)),
            dma((groups,)),
            pltpu.VMEM((4, CHUNKS, tokens, columns // CHUNKS), bf16),
            pltpu.VMEM((4 * columns, wide), bf16),
            pltpu.VMEM((4, 8, tokens), f32),
            dma((3,)),
            dma((3,)),
            dma((3 * CHUNKS,)),
            dma((4, CHUNKS)),
        ],
        compiler_params=pltpu.CompilerParams(
            has_side_effects=True, vmem_limit_bytes=60 << 20, collective_id=0
        ),
    )(hidden, merger_out, position, prompt, gain, wq, wk, wv, cosine, sine)


def body(
    merger_hidden,
    merger_out,
    row_position,
    prompt_embeds,
    norm_gain,
    query_weight,
    key_weight,
    value_weight,
):
    device_rank = lax.axis_index(("role", "seq"))
    tok_count = prompt_embeds.shape[0]
    positions = device_rank * tok_count + jnp.arange(tok_count, dtype=jnp.int32)
    cosine, sine = rotary(positions)
    stream, context = together(
        merger_hidden,
        merger_out,
        row_position[None, :],
        prompt_embeds,
        norm_gain[None, :],
        query_weight,
        key_weight,
        value_weight,
        cosine,
        sine,
    )
    return (stream, context)


def solution(mesh):
    in_specs = (
        P(("role", "seq"), "tp"),
        P("tp", ("role", "seq")),
        P(("role", "seq")),
        P(("role", "seq"), "tp"),
        P("tp"),
        P(None, "tp"),
        P(None, "tp"),
        P(None, "tp"),
    )
    out_specs = (P(("role", "seq"), "tp"), P(("role", "seq"), "tp"))
    return jax.shard_map(body, mesh=mesh, in_specs=in_specs, out_specs=out_specs, check_vma=False)
```

```python
import functools
import math

import jax
import jax.numpy as jnp
from jax import lax
from jax.experimental import pallas as pl
from jax.experimental.pallas import tpu as pltpu
from jax.sharding import PartitionSpec as P

HEAD_DIM = 128


def rotary(positions):
    half_dim = HEAD_DIM // 2
    frequency = 1000000.0 ** (-jnp.arange(half_dim, dtype=jnp.float32) / half_dim)
    angles = positions.astype(jnp.float32)[:, None] * frequency[None, :]
    cosine, sine = jnp.cos(angles), jnp.sin(angles)
    return (
        jnp.concatenate([cosine, cosine], axis=1),
        jnp.concatenate([-sine, sine], axis=1),
    )


MESH = pl.DeviceIdType.MESH
SIDE = 4


def remote(src, dst, send_sem, recv_sem, role, seq, tp):
    return pltpu.make_async_remote_copy(
        src_ref=src,
        dst_ref=dst,
        send_sem=send_sem,
        recv_sem=recv_sem,
        device_id=(role, seq, tp),
        device_id_type=MESH,
    )


def plane_steps(buf, full_sem, half_sem, send_sem):
    role, seq, tp = lax.axis_index("role"), lax.axis_index("seq"), lax.axis_index("tp")
    step_a, step_b = 1 + 3 * role, 4 - 3 * role
    z, x = seq // SIDE, seq % SIDE
    ca = x + role * (z - x)
    cb = z + role * (x - z)
    half = buf.shape[1] // 2
    sent = []

    def seq_of(a, b):
        return ((ca + a + SIDE) % SIDE) * step_a + ((cb + b + SIDE) % SIDE) * step_b

    def slot_of(a, b):
        return role * (SIDE * SIDE) + seq_of(a, b)

    def whole(slot, to_role, to_seq):
        remote(
            buf.at[slot], buf.at[slot], send_sem.at[len(sent)], full_sem.at[slot], to_role, to_seq, tp
        ).start()
        sent.append(2 * half)

    def part(slot, k, to_seq):
        piece = buf.at[slot, pl.ds(k * half, half)]
        remote(
            piece, piece, send_sem.at[len(sent)], half_sem.at[slot, k], role, to_seq, tp
        ).start()
        sent.append(half)

    def wait_whole(slot):
        pltpu.make_async_copy(buf.at[slot], buf.at[slot], full_sem.at[slot]).wait()

    def wait_parts(slot):
        for k in range(2):
            piece = buf.at[slot, pl.ds(k * half, half)]
            pltpu.make_async_copy(piece, piece, half_sem.at[slot, k]).wait()

    def spread_b(slot):
        whole(slot, role, seq_of(0, 1))
        whole(slot, role, seq_of(0, -1))
        whole(slot, 1 - role, seq)

    def pass_b(a):
        for b, k in ((-1, 0), (1, 1)):
            wait_whole(slot_of(a, b))
            part(slot_of(a, b), k, seq_of(0, -b))
            whole(slot_of(a, b), 1 - role, seq)

    def other(b):
        fixed = (ca + b + SIDE) % SIDE
        for k in range(SIDE):
            wait_whole((1 - role) * (SIDE * SIDE) + fixed * step_a + k * step_b)

    def begin():
        own = slot_of(0, 0)
        whole(own, role, seq_of(1, 0))
        whole(own, role, seq_of(-1, 0))
        spread_b(own)
        for a, k in ((-1, 0), (1, 1)):
            wait_whole(slot_of(a, 0))
            part(slot_of(a, 0), k, seq_of(-a, 0))
            spread_b(slot_of(a, 0))
        pass_b(0)
        wait_parts(slot_of(2, 0))
        spread_b(slot_of(2, 0))

    def second():
        pass_b(-1)
        pass_b(1)
        other(0)

    def last():
        for a in (0, -1, 1, 2):
            wait_parts(slot_of(a, 2))
            whole(slot_of(a, 2), 1 - role, seq)
        other(1)

    def mine(b):
        return role, (cb + b + SIDE) % SIDE

    def theirs(b):
        return 1 - role, (ca + b + SIDE) % SIDE

    steps = (
        (begin, mine(0)),
        (second, theirs(0)),
        (lambda: pass_b(2), mine(-1)),
        (lambda: None, mine(1)),
        (lambda: other(-1), theirs(-1)),
        (last, theirs(1)),
        (lambda: None, mine(2)),
        (lambda: other(2), theirs(2)),
    )

    def finish():
        for n, rows in enumerate(sent):
            piece = buf.at[0, pl.ds(0, rows)]
            pltpu.make_async_copy(piece, piece, send_sem.at[n]).wait()

    return steps, finish


PLANE_SENDS = 2 + 3 * 4 + 2 + 8 + 12
CHUNKS = 4


def iota(shape, dim):
    return lax.broadcasted_iota(jnp.int32, shape, dim).astype(jnp.float32)


def greet():
    role, seq, tp = lax.axis_index("role"), lax.axis_index("seq"), lax.axis_index("tp")
    z, x = seq // SIDE, seq % SIDE
    rank = role * (SIDE * SIDE) + seq
    barrier = pltpu.get_barrier_semaphore()

    def tell(to_role, to_seq, to_tp):
        pl.semaphore_signal(
            barrier, inc=1, device_id=(to_role, to_seq, to_tp), device_id_type=MESH
        )

    tell(1 - role, seq, tp)
    for k in (1, 3):
        tell(role, z * SIDE + (x + k) % SIDE, tp)
        tell(role, ((z + k) % SIDE) * SIDE + x, tp)
    for k in (1, 2, 3):
        tell(role, seq, (tp + k) % 4)

    @pl.loop(0, 32)
    def _(i):
        source = tp * 8 + i // 4

        @pl.when((source != rank) | (i % 4 != tp))
        def _():
            tell(source // 16, source % 16, i % 4)

    self_too = jnp.where(rank // 8 == tp, 1, 0)
    pl.semaphore_wait(barrier, 40 - self_too)


def merge_part(
    hidden, weight, position, prompt, stream, weight_here, prompt_here, m
):
    (
        buf,
        full_sem,
        half_sem,
        send_sem,
        partial,
        landed,
        mine,
        y_send,
        y_recv,
        table,
        place,
        packed,
        arrived,
        d_send,
        d_recv,
    ) = m
    role, seq, tp = lax.axis_index("role"), lax.axis_index("seq"), lax.axis_index("tp")
    rank = role * lax.axis_size("seq") + seq
    rows, width = hidden.shape
    tokens = prompt.shape[0]
    groups = buf.shape[0]
    columns = weight.shape[1]
    capacity = 2 * rows // groups
    quarter = groups // 4
    some = SIDE * rows
    copies = []

    def on_line(of_role, fixed):
        n = len(copies) // 3
        if n == 0:
            weight_here.wait()
        step_a, step_b = 1 + 3 * of_role, 4 - 3 * of_role
        pieces, spots = [], []
        for d in (2, 1, 3, 0):
            along = (tp + d + SIDE - fixed) % SIDE
            slot = of_role * (SIDE * SIDE) + along * step_a + fixed * step_b
            pieces.append(buf[slot, :, :width])
            spots.append(of_role * SIDE + fixed + of_role * (along - fixed))
        value = jnp.dot(
            jnp.concatenate(pieces, axis=0), weight[...], preferred_element_type=jnp.float32
        )
        for k, d in enumerate((2, 1, 3)):
            partial[n, k] = value[k * rows : (k + 1) * rows].astype(jnp.bfloat16)
            copy = remote(
                partial.at[n, k],
                landed.at[3 - d, spots[k]],
                y_send.at[n, k],
                y_recv.at[3 - d, spots[k]],
                role,
                seq,
                (tp + d) % 4,
            )
            copy.start()
            copies.append(copy)
        mine[spots[3]] = value[3 * rows :]

    steps, sent = plane_steps(buf, full_sem, half_sem, send_sem)
    for step, (of_role, fixed) in steps:
        step()
        on_line(of_role, fixed)

    r0 = lax.broadcasted_iota(jnp.int32, (some, some), 0)
    r1 = lax.broadcasted_iota(jnp.int32, (some, some), 1)
    lower = jnp.where((r1 < r0) & (r1 // rows == r0 // rows), 1.0, 0.0).astype(jnp.bfloat16)
    source = lax.broadcasted_iota(jnp.int32, (some, 1), 0) // rows

    def decode(got):
        got = got.astype(jnp.float32)
        owner, rest = got[:, 0:1], got[:, 1:2]
        onehot = jnp.where(owner == iota((some, 128), 1), 1.0, 0.0)
        before = jnp.dot(lower, onehot.astype(jnp.bfloat16), preferred_element_type=jnp.float32)
        return owner, rest, jnp.sum(before * onehot, axis=1, keepdims=True)

    for n in range(quarter // SIDE):
        got = jnp.concatenate(
            [buf[n * 16 + z * SIDE + (tp + SIDE - z) % SIDE, :, width:] for z in range(SIDE)],
            axis=0,
        )
        owner, rest, earlier = decode(got)
        spot = (source + n * SIDE).astype(jnp.float32)
        slot = owner * (quarter * capacity) + spot * capacity + earlier
        table[n * some : (n + 1) * some, :] = jnp.where(
            slot == iota((some, table.shape[1]), 1), 1.0, 0.0
        ).astype(jnp.bfloat16)
    place[...] = jnp.zeros_like(place)

    @pl.loop(0, groups // SIDE)
    def _(n):
        got = buf[pl.ds(n * SIDE, SIDE), :, width:].reshape(some, 128)
        owner, rest, earlier = decode(got)
        here = (rest == iota((some, tokens), 1)) & (owner == rank.astype(jnp.float32))
        spot = ((source + n % SIDE) % SIDE) * quarter + n
        slot = spot.astype(jnp.float32) * capacity + earlier
        there = slot == iota((some, 128), 1)
        place[...] += lax.dot_general(
            jnp.where(here, 1.0, 0.0).astype(jnp.bfloat16),
            jnp.where(there, 1.0, 0.0).astype(jnp.bfloat16),
            (((0,), (0,)), ((), ())),
            preferred_element_type=jnp.float32,
        )

    for i in range(quarter):
        for k in range(3):
            got = landed.at[k, i]
            pltpu.make_async_copy(got, got, y_recv.at[k, i]).wait()
            mine[i] += landed[k, i].astype(jnp.float32)
    packed[...] = lax.dot_general(
        table[...],
        mine[...].reshape(quarter * rows, columns).astype(jnp.bfloat16),
        (((0,), (0,)), ((), ())),
        preferred_element_type=jnp.float32,
    ).astype(jnp.bfloat16)

    piece = quarter * capacity
    to_tp = rank // 8
    lane_group = rank % 8

    def sending(i):
        j = (rank + i) % groups
        return remote(
            packed.at[pl.ds(pl.multiple_of(j * piece, piece), piece)],
            arrived.at[lane_group, pl.ds(pl.multiple_of(tp * piece, piece), piece)],
            d_send.at[i],
            d_recv.at[lane_group * 4 + tp],
            j // 16,
            j % 16,
            to_tp,
        )

    def staying():
        return pltpu.make_async_copy(
            packed.at[pl.ds(pl.multiple_of(rank * piece, piece), piece)],
            arrived.at[lane_group, pl.ds(pl.multiple_of(tp * piece, piece), piece)],
            d_recv.at[lane_group * 4 + tp],
        )

    @pl.when(to_tp == tp)
    def _():
        staying().start()

    @pl.when(to_tp != tp)
    def _():
        sending(0).start()

    @pl.loop(1, groups)
    def _(i):
        sending(i).start()

    chosen = place[...].astype(jnp.bfloat16)
    hit = jnp.max(place[...], axis=1, keepdims=True) > 0.5
    prompt_here.wait()
    total = jnp.zeros((tokens, 128), jnp.float32)
    for c in range(8):
        for k in range(4):
            got = arrived.at[c, pl.ds(k * piece, piece)]
            pltpu.make_async_copy(got, got, d_recv.at[c * 4 + k]).wait()
        rows_here = jnp.dot(chosen, arrived[c], preferred_element_type=jnp.float32)
        span = slice(c * columns, (c + 1) * columns)
        x = jnp.where(hit, rows_here, prompt[:, span].astype(jnp.float32))
        stream[:, span] = x.astype(jnp.bfloat16)
        for k in range(0, columns, 128):
            total = total + x[:, k : k + 128] * x[:, k : k + 128]

    def finish():
        sent()
        for copy in copies:
            copy.wait_send()

        @pl.when(to_tp != tp)
        def _():
            sending(0).wait_send()

        @pl.loop(1, groups)
        def _(i):
            sending(i).wait_send()

    return total, finish


def project_part(eps, total, stream, gain, tables_here, acc, m):
    normed, weights, squares, s_send, s_recv, n_send, n_recv = m
    role, seq, tp = lax.axis_index("role"), lax.axis_index("seq"), lax.axis_index("tp")
    rows, columns = stream.shape
    chunk = columns // CHUNKS
    squares[3] = jnp.broadcast_to(
        jnp.sum(jnp.transpose(total), axis=0, keepdims=True), (8, rows)
    )
    sums = []
    for k, off in enumerate((1, 3, 2)):
        copy = remote(
            squares.at[3], squares.at[k], s_send.at[k], s_recv.at[k], role, seq, (tp + off) % 4
        )
        copy.start()
        sums.append(copy)
    for copy in sums:
        copy.wait()
    whole = squares[0] + squares[1] + (squares[2] + squares[3])
    whole = jnp.broadcast_to(whole[0:1], (128, rows))
    inverse = lax.rsqrt(jnp.transpose(whole) / (4 * columns) + eps)[:, 0:1]

    copies = []

    def send(t, c, off):
        copy = remote(
            normed.at[t, c],
            normed.at[t, c],
            n_send.at[len(copies)],
            n_recv.at[t, c],
            role,
            seq,
            (tp + off + 4) % 4,
        )
        copy.start()
        copies.append(copy)

    def arrive(t, c):
        pltpu.make_async_copy(normed.at[t, c], normed.at[t, c], n_recv.at[t, c]).wait()

    def scale(c):
        span = slice(c * chunk, (c + 1) * chunk)
        x = stream[:, span].astype(jnp.float32)
        normed[tp, c] = (x * inverse * gain[:, span].astype(jnp.float32)).astype(jnp.bfloat16)

    scale(0)
    send(tp, 0, 1)
    scale(2)
    send(tp, 2, -1)
    scale(1)
    send(tp, 1, 1)
    scale(3)
    send(tp, 3, -1)
    send(tp, 2, 1)
    send(tp, 0, -1)
    send(tp, 3, 1)
    send(tp, 1, -1)
    before, after, across = (tp + 3) % 4, (tp + 1) % 4, (tp + 2) % 4

    def multiply(t, c, first=False):
        span = pl.ds(pl.multiple_of(t * columns + c * chunk, chunk), chunk)
        value = jnp.dot(normed[t, c], weights[span, :], preferred_element_type=jnp.float32)
        if first:
            acc[...] = value
        else:
            acc[...] += value

    for copy in tables_here:
        copy.wait()
    for c in range(CHUNKS):
        multiply(tp, c, c == 0)
    for c, d in ((0, 2), (1, 3)):
        arrive(before, c)
        send(before, c, 1)
        arrive(after, d)
        send(after, d, -1)
        multiply(before, c)
        multiply(after, d)
    for c, d in ((2, 0), (3, 1)):
        arrive(before, c)
        multiply(before, c)
        arrive(after, d)
        multiply(after, d)
    for c in (0, 2, 1, 3):
        arrive(across, c)
        multiply(across, c)

    def finish():
        for copy in copies:
            copy.wait_send()

    return finish


def attend_part(q_ref, buf, o_ref, acc, top, total, scores, bias, sems):
    heads, rows = q_ref.shape[:2]
    role, seq = lax.axis_index("role"), lax.axis_index("seq")
    z, x = seq // SIDE, seq % SIDE
    rank = role * (SIDE * SIDE) + seq
    factor = math.log2(math.e) / math.sqrt(HEAD_DIM)
    span = SIDE * rows
    acc[...] = jnp.zeros_like(acc)
    total[...] = jnp.zeros_like(total)
    top[...] = jnp.full_like(top, -1e30)

    def block(slots, masked):
        k = jnp.concatenate([buf[slot, :, :HEAD_DIM] for slot in slots], axis=0)
        v = jnp.concatenate([buf[slot, :, HEAD_DIM:] for slot in slots], axis=0)
        if masked:
            ahead = lax.broadcasted_iota(jnp.int32, (rows, rows), 1) - lax.broadcasted_iota(
                jnp.int32, (rows, rows), 0
            )
            for n, slot in enumerate(slots):
                bias[:, n * rows : (n + 1) * rows] = jnp.where(
                    ahead <= (rank - slot) * rows, 0.0, -1e30
                )

        def score(h):
            scores[h % 2] = lax.dot_general(
                q_ref[h], k, (((1,), (1,)), ((), ())), preferred_element_type=jnp.float32
            )

        score(0)
        for h in range(heads):
            if h + 1 < heads:
                score(h + 1)
            s = scores[h % 2]
            if masked:
                s = s + bias[...]
            old = top[h][:, :1]
            new = jnp.maximum(old, jnp.max(s, axis=1, keepdims=True))
            p = jnp.exp2((s - new) * factor)
            alpha = jnp.exp2((old - new) * factor)
            part = p[:, :HEAD_DIM]
            for c in range(HEAD_DIM, span, HEAD_DIM):
                part = part + p[:, c : c + HEAD_DIM]
            total[h] = total[h] * alpha + part
            acc[h] = acc[h] * alpha + jnp.dot(
                p.astype(jnp.bfloat16), v, preferred_element_type=jnp.float32
            )
            top[h] = jnp.broadcast_to(new, (rows, HEAD_DIM))

    steps, sent = plane_steps(buf, *sems)

    @pl.loop(0, len(steps))
    def _(e):
        for n, (step, _) in enumerate(steps):
            pl.when(e == n)(step)
        of_role, fixed = steps[0][1]
        for n, (_, line) in enumerate(steps):
            of_role = jnp.where(e == n, line[0], of_role)
            fixed = jnp.where(e == n, line[1], fixed)
        step_a, step_b = 1 + 3 * of_role, 4 - 3 * of_role
        slots = [
            of_role * (SIDE * SIDE) + along * step_a + fixed * step_b for along in range(SIDE)
        ]
        clear = slots[-1] < rank
        some = slots[0] <= rank
        pl.when(clear)(lambda: block(slots, False))
        pl.when(some & jnp.logical_not(clear))(lambda: block(slots, True))

    for h in range(heads):
        l = jnp.sum(total[h], axis=1, keepdims=True)
        o_ref[:, h * HEAD_DIM : (h + 1) * HEAD_DIM] = (acc[h] / l).astype(o_ref.dtype)
    return sent


MERGE_SCRATCH = 15
PROJECT_SCRATCH = 7


def kernel(
    hidden,
    merger_out,
    position,
    prompt,
    gain,
    query_weight,
    key_weight,
    value_weight,
    cosine,
    sine,
    stream_out,
    context_out,
    merger_here,
    prompt_here,
    stream,
    queries,
    cosine_here,
    sine_here,
    sums,
    keys,
    k_full,
    k_half,
    k_send,
    acc,
    top,
    total,
    scores,
    bias,
    in_sem,
    w_sem,
    *more,
):
    m, p = more[:MERGE_SCRATCH], more[MERGE_SCRATCH:]
    role, seq, tp = lax.axis_index("role"), lax.axis_index("seq"), lax.axis_index("tp")
    rank = role * lax.axis_size("seq") + seq
    rows, width = hidden.shape
    tokens = prompt.shape[0]
    columns = prompt.shape[1]
    heads = query_weight.shape[1] // HEAD_DIM

    fetches = []
    for k, (src, dst) in enumerate(
        (
            (merger_out, merger_here),
            (prompt, prompt_here),
            (cosine, cosine_here),
            (sine, sine_here),
        )
    ):
        copy = pltpu.make_async_copy(src, dst, in_sem.at[k])
        copy.start()
        fetches.append(copy)
    weights = p[1]
    tables_here = []
    for i in range(4):
        for k, (table, spot) in enumerate(
            ((query_weight, 0), (key_weight, heads), (value_weight, heads + 1))
        ):
            span = pl.ds(i * columns, columns)
            lanes = pl.ds(spot * HEAD_DIM, table.shape[1])
            copy = pltpu.make_async_copy(
                table.at[span], weights.at[span, lanes], w_sem.at[i, k]
            )
            copy.start()
            tables_here.append(copy)

    lane = lax.broadcasted_iota(jnp.int32, (rows, 128), 1)
    pos = jnp.transpose(jnp.broadcast_to(position[...], (128, rows)))
    owner = jnp.where(pos >= 0, pos // tokens, -1)
    rest = jnp.where(pos >= 0, pos % tokens, 0)
    code = jnp.where(lane == 0, owner, jnp.where(lane == 1, rest, 0))
    buf = m[0]
    buf[rank, :, :width] = hidden[...]
    buf[rank, :, width:] = code.astype(jnp.float32).astype(jnp.bfloat16)
    greet()
    squares, merged = merge_part(
        hidden, merger_here, position, prompt_here, stream, fetches[0], fetches[1], m
    )
    stream_sent = pltpu.make_async_copy(stream, stream_out, in_sem.at[4])
    stream_sent.start()
    projected = project_part(1e-06, squares, stream, gain, tables_here, sums, p)
    fetches[2].wait()
    fetches[3].wait()

    def turned(h):
        u = sums[:, h * HEAD_DIM : (h + 1) * HEAD_DIM]
        u = u * cosine_here[...] + pltpu.roll(u, HEAD_DIM // 2, 1) * sine_here[...]
        return u.astype(jnp.bfloat16)

    keys[rank, :, :HEAD_DIM] = turned(heads)
    keys[rank, :, HEAD_DIM:] = sums[:, (heads + 1) * HEAD_DIM :].astype(jnp.bfloat16)
    for h in range(heads):
        queries[h] = turned(h)
    k_sent = attend_part(
        queries, keys, context_out, acc, top, total, scores, bias, (k_full, k_half, k_send)
    )
    stream_sent.wait()
    k_sent()
    projected()
    merged()


def together(hidden, merger_out, position, prompt, gain, wq, wk, wv, cosine, sine):
    rows, width = hidden.shape
    groups = lax.axis_size("role") * lax.axis_size("seq")
    tokens, columns = prompt.shape
    strip = merger_out.shape[1]
    quarter = groups // 4
    slots = groups * quarter * (2 * rows // groups)
    heads = wq.shape[1] // HEAD_DIM
    wide = wq.shape[1] + 2 * HEAD_DIM
    dma = pltpu.SemaphoreType.DMA
    vmem = pl.BlockSpec(memory_space=pltpu.VMEM)
    hbm = pl.BlockSpec(memory_space=pl.ANY)
    bf16, f32 = jnp.bfloat16, jnp.float32
    return pl.pallas_call(
        kernel,
        out_shape=(
            jax.ShapeDtypeStruct(prompt.shape, bf16),
            jax.ShapeDtypeStruct((tokens, wq.shape[1]), bf16),
        ),
        in_specs=[vmem, hbm, vmem, hbm, vmem, hbm, hbm, hbm, hbm, hbm],
        out_specs=(hbm, vmem),
        scratch_shapes=[
            pltpu.VMEM(merger_out.shape, bf16),
            pltpu.VMEM(prompt.shape, bf16),
            pltpu.VMEM(prompt.shape, bf16),
            pltpu.VMEM((heads, tokens, HEAD_DIM), bf16),
            pltpu.VMEM(cosine.shape, f32),
            pltpu.VMEM(sine.shape, f32),
            pltpu.VMEM((tokens, wide), f32),
            pltpu.VMEM((groups, tokens, 2 * HEAD_DIM), bf16),
            dma((groups,)),
            dma((groups, 2)),
            dma((PLANE_SENDS,)),
            pltpu.VMEM((heads, tokens, HEAD_DIM), f32),
            pltpu.VMEM((heads, tokens, HEAD_DIM), f32),
            pltpu.VMEM((heads, tokens, HEAD_DIM), f32),
            pltpu.VMEM((2, tokens, SIDE * tokens), f32),
            pltpu.VMEM((tokens, SIDE * tokens), f32),
            dma((5,)),
            dma((4, 3)),
            pltpu.VMEM((groups, rows, width + 128), bf16),
            dma((groups,)),
            dma((groups, 2)),
            dma((PLANE_SENDS,)),
            pltpu.VMEM((8, 3, rows, strip), bf16),
            pltpu.VMEM((3, quarter, rows, strip), bf16),
            pltpu.VMEM((quarter, rows, strip), f32),
            dma((8, 3)),
            dma((3, quarter)),
            pltpu.VMEM((quarter * rows, slots), bf16),
            pltpu.VMEM((tokens, 128), f32),
            pltpu.VMEM((slots, strip), bf16),
            pltpu.VMEM((8, slots // 8, strip), bf16),
            dma((groups,)),
            dma((groups,)),
            pltpu.VMEM((4, CHUNKS, tokens, columns // CHUNKS), bf16),
            pltpu.VMEM((4 * columns, wide), bf16),
            pltpu.VMEM((4, 8, tokens), f32),
            dma((3,)),
            dma((3,)),
            dma((3 * CHUNKS,)),
            dma((4, CHUNKS)),
        ],
        compiler_params=pltpu.CompilerParams(
            has_side_effects=True, vmem_limit_bytes=60 << 20, collective_id=0
        ),
    )(hidden, merger_out, position, prompt, gain, wq, wk, wv, cosine, sine)


def body(
    merger_hidden,
    merger_out,
    row_position,
    prompt_embeds,
    norm_gain,
    query_weight,
    key_weight,
    value_weight,
):
    device_rank = lax.axis_index(("role", "seq"))
    tok_count = prompt_embeds.shape[0]
    positions = device_rank * tok_count + jnp.arange(tok_count, dtype=jnp.int32)
    cosine, sine = rotary(positions)
    stream, context = together(
        merger_hidden,
        merger_out,
        row_position[None, :],
        prompt_embeds,
        norm_gain[None, :],
        query_weight,
        key_weight,
        value_weight,
        cosine,
        sine,
    )
    return (stream, context)


def solution(mesh):
    in_specs = (
        P(("role", "seq"), "tp"),
        P("tp", ("role", "seq")),
        P(("role", "seq")),
        P(("role", "seq"), "tp"),
        P("tp"),
        P(None, "tp"),
        P(None, "tp"),
        P(None, "tp"),
    )
    out_specs = (P(("role", "seq"), "tp"), P(("role", "seq"), "tp"))
    return jax.shard_map(body, mesh=mesh, in_specs=in_specs, out_specs=out_specs, check_vma=False)
```

```python
import functools
import math

import jax
import jax.numpy as jnp
from jax import lax
from jax.experimental import pallas as pl
from jax.experimental.pallas import tpu as pltpu
from jax.sharding import PartitionSpec as P

HEAD_DIM = 128


def rotary(positions):
    half_dim = HEAD_DIM // 2
    frequency = 1000000.0 ** (-jnp.arange(half_dim, dtype=jnp.float32) / half_dim)
    angles = positions.astype(jnp.float32)[:, None] * frequency[None, :]
    cosine, sine = jnp.cos(angles), jnp.sin(angles)
    return (
        jnp.concatenate([cosine, cosine], axis=1),
        jnp.concatenate([-sine, sine], axis=1),
    )


MESH = pl.DeviceIdType.MESH
SIDE = 4


def remote(src, dst, send_sem, recv_sem, role, seq, tp):
    return pltpu.make_async_remote_copy(
        src_ref=src,
        dst_ref=dst,
        send_sem=send_sem,
        recv_sem=recv_sem,
        device_id=(role, seq, tp),
        device_id_type=MESH,
    )


def plane_steps(buf, full_sem, half_sem, send_sem):
    role, seq, tp = lax.axis_index("role"), lax.axis_index("seq"), lax.axis_index("tp")
    step_a, step_b = 1 + 3 * role, 4 - 3 * role
    z, x = seq // SIDE, seq % SIDE
    ca = x + role * (z - x)
    cb = z + role * (x - z)
    half = buf.shape[1] // 2
    sent = []

    def seq_of(a, b):
        return ((ca + a + SIDE) % SIDE) * step_a + ((cb + b + SIDE) % SIDE) * step_b

    def slot_of(a, b):
        return role * (SIDE * SIDE) + seq_of(a, b)

    def whole(slot, to_role, to_seq):
        remote(
            buf.at[slot], buf.at[slot], send_sem.at[len(sent)], full_sem.at[slot], to_role, to_seq, tp
        ).start()
        sent.append(2 * half)

    def part(slot, k, to_seq):
        piece = buf.at[slot, pl.ds(k * half, half)]
        remote(
            piece, piece, send_sem.at[len(sent)], half_sem.at[slot, k], role, to_seq, tp
        ).start()
        sent.append(half)

    def wait_whole(slot):
        pltpu.make_async_copy(buf.at[slot], buf.at[slot], full_sem.at[slot]).wait()

    def wait_parts(slot):
        for k in range(2):
            piece = buf.at[slot, pl.ds(k * half, half)]
            pltpu.make_async_copy(piece, piece, half_sem.at[slot, k]).wait()

    def spread_b(slot):
        whole(slot, role, seq_of(0, 1))
        whole(slot, role, seq_of(0, -1))
        whole(slot, 1 - role, seq)

    def pass_b(a):
        for b, k in ((-1, 0), (1, 1)):
            wait_whole(slot_of(a, b))
            part(slot_of(a, b), k, seq_of(0, -b))
            whole(slot_of(a, b), 1 - role, seq)

    def other(b):
        fixed = (ca + b + SIDE) % SIDE
        for k in range(SIDE):
            wait_whole((1 - role) * (SIDE * SIDE) + fixed * step_a + k * step_b)

    def begin():
        own = slot_of(0, 0)
        whole(own, role, seq_of(1, 0))
        whole(own, role, seq_of(-1, 0))
        spread_b(own)
        for a, k in ((-1, 0), (1, 1)):
            wait_whole(slot_of(a, 0))
            part(slot_of(a, 0), k, seq_of(-a, 0))
            spread_b(slot_of(a, 0))
        pass_b(0)
        wait_parts(slot_of(2, 0))
        spread_b(slot_of(2, 0))

    def second():
        pass_b(-1)
        pass_b(1)
        other(0)

    def last():
        for a in (0, -1, 1, 2):
            wait_parts(slot_of(a, 2))
            whole(slot_of(a, 2), 1 - role, seq)
        other(1)

    def mine(b):
        return role, (cb + b + SIDE) % SIDE

    def theirs(b):
        return 1 - role, (ca + b + SIDE) % SIDE

    steps = (
        (begin, mine(0)),
        (second, theirs(0)),
        (lambda: pass_b(2), mine(-1)),
        (lambda: None, mine(1)),
        (lambda: other(-1), theirs(-1)),
        (last, theirs(1)),
        (lambda: None, mine(2)),
        (lambda: other(2), theirs(2)),
    )

    def finish():
        for n, rows in enumerate(sent):
            piece = buf.at[0, pl.ds(0, rows)]
            pltpu.make_async_copy(piece, piece, send_sem.at[n]).wait()

    return steps, finish


PLANE_SENDS = 2 + 3 * 4 + 2 + 8 + 12
CHUNKS = 4


def iota(shape, dim):
    return lax.broadcasted_iota(jnp.int32, shape, dim).astype(jnp.float32)


def greet():
    role, seq, tp = lax.axis_index("role"), lax.axis_index("seq"), lax.axis_index("tp")
    z, x = seq // SIDE, seq % SIDE
    barrier = pltpu.get_barrier_semaphore()

    def tell(to_role, to_seq, to_tp):
        pl.semaphore_signal(
            barrier, inc=1, device_id=(to_role, to_seq, to_tp), device_id_type=MESH
        )

    tell(1 - role, seq, tp)
    for k in (1, 3):
        tell(role, z * SIDE + (x + k) % SIDE, tp)
        tell(role, ((z + k) % SIDE) * SIDE + x, tp)
    for k in (1, 2, 3):
        tell(role, seq, (tp + k) % 4)

    pl.semaphore_wait(barrier, 8)


def merge_part(
    hidden, weight, position, prompt, stream, weight_here, prompt_here, m
):
    (
        buf,
        full_sem,
        half_sem,
        send_sem,
        partial,
        landed,
        mine,
        y_send,
        y_recv,
        table,
        place,
        packed,
        arrived,
        d_send,
        d_recv,
    ) = m
    role, seq, tp = lax.axis_index("role"), lax.axis_index("seq"), lax.axis_index("tp")
    rank = role * lax.axis_size("seq") + seq
    rows, width = hidden.shape
    tokens = prompt.shape[0]
    groups = buf.shape[0]
    columns = weight.shape[1]
    capacity = 2 * rows // groups
    quarter = groups // 4
    some = SIDE * rows
    copies = []

    def on_line(of_role, fixed):
        n = len(copies) // 3
        if n == 0:
            weight_here.wait()
        step_a, step_b = 1 + 3 * of_role, 4 - 3 * of_role
        pieces, spots = [], []
        for d in (2, 1, 3, 0):
            along = (tp + d + SIDE - fixed) % SIDE
            slot = of_role * (SIDE * SIDE) + along * step_a + fixed * step_b
            pieces.append(buf[slot, :, :width])
            spots.append(of_role * SIDE + fixed + of_role * (along - fixed))
        value = jnp.dot(
            jnp.concatenate(pieces, axis=0), weight[...], preferred_element_type=jnp.float32
        )
        for k, d in enumerate((2, 1, 3)):
            partial[n, k] = value[k * rows : (k + 1) * rows].astype(jnp.bfloat16)
            copy = remote(
                partial.at[n, k],
                landed.at[3 - d, spots[k]],
                y_send.at[n, k],
                y_recv.at[3 - d, spots[k]],
                role,
                seq,
                (tp + d) % 4,
            )
            copy.start()
            copies.append(copy)
        mine[spots[3]] = value[3 * rows :]

    steps, sent = plane_steps(buf, full_sem, half_sem, send_sem)
    for step, (of_role, fixed) in steps:
        step()
        on_line(of_role, fixed)

    r0 = lax.broadcasted_iota(jnp.int32, (some, some), 0)
    r1 = lax.broadcasted_iota(jnp.int32, (some, some), 1)
    lower = jnp.where((r1 < r0) & (r1 // rows == r0 // rows), 1.0, 0.0).astype(jnp.bfloat16)
    source = lax.broadcasted_iota(jnp.int32, (some, 1), 0) // rows

    def decode(got):
        got = got.astype(jnp.float32)
        owner, rest = got[:, 0:1], got[:, 1:2]
        onehot = jnp.where(owner == iota((some, 128), 1), 1.0, 0.0)
        before = jnp.dot(lower, onehot.astype(jnp.bfloat16), preferred_element_type=jnp.float32)
        return owner, rest, jnp.sum(before * onehot, axis=1, keepdims=True)

    for n in range(quarter // SIDE):
        got = jnp.concatenate(
            [buf[n * 16 + z * SIDE + (tp + SIDE - z) % SIDE, :, width:] for z in range(SIDE)],
            axis=0,
        )
        owner, rest, earlier = decode(got)
        spot = (source + n * SIDE).astype(jnp.float32)
        slot = owner * (quarter * capacity) + spot * capacity + earlier
        table[n * some : (n + 1) * some, :] = jnp.where(
            slot == iota((some, table.shape[1]), 1), 1.0, 0.0
        ).astype(jnp.bfloat16)
    place[...] = jnp.zeros_like(place)

    @pl.loop(0, groups // SIDE)
    def _(n):
        got = buf[pl.ds(n * SIDE, SIDE), :, width:].reshape(some, 128)
        owner, rest, earlier = decode(got)
        here = (rest == iota((some, tokens), 1)) & (owner == rank.astype(jnp.float32))
        spot = ((source + n % SIDE) % SIDE) * quarter + n
        slot = spot.astype(jnp.float32) * capacity + earlier
        there = slot == iota((some, 128), 1)
        place[...] += lax.dot_general(
            jnp.where(here, 1.0, 0.0).astype(jnp.bfloat16),
            jnp.where(there, 1.0, 0.0).astype(jnp.bfloat16),
            (((0,), (0,)), ((), ())),
            preferred_element_type=jnp.float32,
        )

    for i in range(quarter):
        for k in range(3):
            got = landed.at[k, i]
            pltpu.make_async_copy(got, got, y_recv.at[k, i]).wait()
            mine[i] += landed[k, i].astype(jnp.float32)
    packed[...] = lax.dot_general(
        table[...],
        mine[...].reshape(quarter * rows, columns).astype(jnp.bfloat16),
        (((0,), (0,)), ((), ())),
        preferred_element_type=jnp.float32,
    ).astype(jnp.bfloat16)

    piece = quarter * capacity
    to_tp = rank // 8
    lane_group = rank % 8

    def sending(i):
        j = (rank + i) % groups
        return remote(
            packed.at[pl.ds(pl.multiple_of(j * piece, piece), piece)],
            arrived.at[lane_group, pl.ds(pl.multiple_of(tp * piece, piece), piece)],
            d_send.at[i],
            d_recv.at[lane_group * 4 + tp],
            j // 16,
            j % 16,
            to_tp,
        )

    def staying():
        return pltpu.make_async_copy(
            packed.at[pl.ds(pl.multiple_of(rank * piece, piece), piece)],
            arrived.at[lane_group, pl.ds(pl.multiple_of(tp * piece, piece), piece)],
            d_recv.at[lane_group * 4 + tp],
        )

    @pl.when(to_tp == tp)
    def _():
        staying().start()

    @pl.when(to_tp != tp)
    def _():
        sending(0).start()

    @pl.loop(1, groups)
    def _(i):
        sending(i).start()

    chosen = place[...].astype(jnp.bfloat16)
    hit = jnp.max(place[...], axis=1, keepdims=True) > 0.5
    prompt_here.wait()
    total = jnp.zeros((tokens, 128), jnp.float32)
    for c in range(8):
        for k in range(4):
            got = arrived.at[c, pl.ds(k * piece, piece)]
            pltpu.make_async_copy(got, got, d_recv.at[c * 4 + k]).wait()
        rows_here = jnp.dot(chosen, arrived[c], preferred_element_type=jnp.float32)
        span = slice(c * columns, (c + 1) * columns)
        x = jnp.where(hit, rows_here, prompt[:, span].astype(jnp.float32))
        stream[:, span] = x.astype(jnp.bfloat16)
        for k in range(0, columns, 128):
            total = total + x[:, k : k + 128] * x[:, k : k + 128]

    def finish():
        sent()
        for copy in copies:
            copy.wait_send()

        @pl.when(to_tp != tp)
        def _():
            sending(0).wait_send()

        @pl.loop(1, groups)
        def _(i):
            sending(i).wait_send()

    return total, finish


def project_part(eps, total, stream, gain, tables_here, acc, m):
    normed, weights, squares, s_send, s_recv, n_send, n_recv = m
    role, seq, tp = lax.axis_index("role"), lax.axis_index("seq"), lax.axis_index("tp")
    rows, columns = stream.shape
    chunk = columns // CHUNKS
    squares[3] = jnp.broadcast_to(
        jnp.sum(jnp.transpose(total), axis=0, keepdims=True), (8, rows)
    )
    sums = []
    for k, off in enumerate((1, 3, 2)):
        copy = remote(
            squares.at[3], squares.at[k], s_send.at[k], s_recv.at[k], role, seq, (tp + off) % 4
        )
        copy.start()
        sums.append(copy)
    for copy in sums:
        copy.wait()
    whole = squares[0] + squares[1] + (squares[2] + squares[3])
    whole = jnp.broadcast_to(whole[0:1], (128, rows))
    inverse = lax.rsqrt(jnp.transpose(whole) / (4 * columns) + eps)[:, 0:1]

    copies = []

    def send(t, c, off):
        copy = remote(
            normed.at[t, c],
            normed.at[t, c],
            n_send.at[len(copies)],
            n_recv.at[t, c],
            role,
            seq,
            (tp + off + 4) % 4,
        )
        copy.start()
        copies.append(copy)

    def arrive(t, c):
        pltpu.make_async_copy(normed.at[t, c], normed.at[t, c], n_recv.at[t, c]).wait()

    def scale(c):
        span = slice(c * chunk, (c + 1) * chunk)
        x = stream[:, span].astype(jnp.float32)
        normed[tp, c] = (x * inverse * gain[:, span].astype(jnp.float32)).astype(jnp.bfloat16)

    scale(0)
    send(tp, 0, 1)
    scale(2)
    send(tp, 2, -1)
    scale(1)
    send(tp, 1, 1)
    scale(3)
    send(tp, 3, -1)
    send(tp, 2, 1)
    send(tp, 0, -1)
    send(tp, 3, 1)
    send(tp, 1, -1)
    before, after, across = (tp + 3) % 4, (tp + 1) % 4, (tp + 2) % 4

    def multiply(t, c, first=False):
        span = pl.ds(pl.multiple_of(t * columns + c * chunk, chunk), chunk)
        value = jnp.dot(normed[t, c], weights[span, :], preferred_element_type=jnp.float32)
        if first:
            acc[...] = value
        else:
            acc[...] += value

    for copy in tables_here:
        copy.wait()
    for c in range(CHUNKS):
        multiply(tp, c, c == 0)
    for c, d in ((0, 2), (1, 3)):
        arrive(before, c)
        send(before, c, 1)
        arrive(after, d)
        send(after, d, -1)
        multiply(before, c)
        multiply(after, d)
    for c, d in ((2, 0), (3, 1)):
        arrive(before, c)
        multiply(before, c)
        arrive(after, d)
        multiply(after, d)
    for c in (0, 2, 1, 3):
        arrive(across, c)
        multiply(across, c)

    def finish():
        for copy in copies:
            copy.wait_send()

    return finish


def attend_part(q_ref, buf, o_ref, acc, top, total, scores, bias, sems):
    heads, rows = q_ref.shape[:2]
    role, seq = lax.axis_index("role"), lax.axis_index("seq")
    z, x = seq // SIDE, seq % SIDE
    rank = role * (SIDE * SIDE) + seq
    factor = math.log2(math.e) / math.sqrt(HEAD_DIM)
    span = SIDE * rows
    acc[...] = jnp.zeros_like(acc)
    total[...] = jnp.zeros_like(total)
    top[...] = jnp.full_like(top, -1e30)

    def block(slots, masked):
        k = jnp.concatenate([buf[slot, :, :HEAD_DIM] for slot in slots], axis=0)
        v = jnp.concatenate([buf[slot, :, HEAD_DIM:] for slot in slots], axis=0)
        if masked:
            ahead = lax.broadcasted_iota(jnp.int32, (rows, rows), 1) - lax.broadcasted_iota(
                jnp.int32, (rows, rows), 0
            )
            for n, slot in enumerate(slots):
                bias[:, n * rows : (n + 1) * rows] = jnp.where(
                    ahead <= (rank - slot) * rows, 0.0, -1e30
                )

        def score(h):
            scores[h % 2] = lax.dot_general(
                q_ref[h], k, (((1,), (1,)), ((), ())), preferred_element_type=jnp.float32
            )

        score(0)
        for h in range(heads):
            if h + 1 < heads:
                score(h + 1)
            s = scores[h % 2]
            if masked:
                s = s + bias[...]
            old = top[h][:, :1]
            new = jnp.maximum(old, jnp.max(s, axis=1, keepdims=True))
            p = jnp.exp2((s - new) * factor)
            alpha = jnp.exp2((old - new) * factor)
            part = p[:, :HEAD_DIM]
            for c in range(HEAD_DIM, span, HEAD_DIM):
                part = part + p[:, c : c + HEAD_DIM]
            total[h] = total[h] * alpha + part
            acc[h] = acc[h] * alpha + jnp.dot(
                p.astype(jnp.bfloat16), v, preferred_element_type=jnp.float32
            )
            top[h] = jnp.broadcast_to(new, (rows, HEAD_DIM))

    steps, sent = plane_steps(buf, *sems)

    @pl.loop(0, len(steps))
    def _(e):
        for n, (step, _) in enumerate(steps):
            pl.when(e == n)(step)
        of_role, fixed = steps[0][1]
        for n, (_, line) in enumerate(steps):
            of_role = jnp.where(e == n, line[0], of_role)
            fixed = jnp.where(e == n, line[1], fixed)
        step_a, step_b = 1 + 3 * of_role, 4 - 3 * of_role
        slots = [
            of_role * (SIDE * SIDE) + along * step_a + fixed * step_b for along in range(SIDE)
        ]
        clear = slots[-1] < rank
        some = slots[0] <= rank
        pl.when(clear)(lambda: block(slots, False))
        pl.when(some & jnp.logical_not(clear))(lambda: block(slots, True))

    for h in range(heads):
        l = jnp.sum(total[h], axis=1, keepdims=True)
        o_ref[:, h * HEAD_DIM : (h + 1) * HEAD_DIM] = (acc[h] / l).astype(o_ref.dtype)
    return sent


MERGE_SCRATCH = 15
PROJECT_SCRATCH = 7


def kernel(
    hidden,
    merger_out,
    position,
    prompt,
    gain,
    query_weight,
    key_weight,
    value_weight,
    cosine,
    sine,
    stream,
    context_out,
    merger_here,
    prompt_here,
    queries,
    cosine_here,
    sine_here,
    sums,
    keys,
    k_full,
    k_half,
    k_send,
    acc,
    top,
    total,
    scores,
    bias,
    in_sem,
    w_sem,
    *more,
):
    m, p = more[:MERGE_SCRATCH], more[MERGE_SCRATCH:]
    role, seq, tp = lax.axis_index("role"), lax.axis_index("seq"), lax.axis_index("tp")
    rank = role * lax.axis_size("seq") + seq
    rows, width = hidden.shape
    tokens = prompt.shape[0]
    columns = prompt.shape[1]
    heads = query_weight.shape[1] // HEAD_DIM

    fetches = []
    for k, (src, dst) in enumerate(
        (
            (merger_out, merger_here),
            (prompt, prompt_here),
            (cosine, cosine_here),
            (sine, sine_here),
        )
    ):
        copy = pltpu.make_async_copy(src, dst, in_sem.at[k])
        copy.start()
        fetches.append(copy)
    weights = p[1]
    tables_here = []
    for i in range(4):
        for k, (table, spot) in enumerate(
            ((query_weight, 0), (key_weight, heads), (value_weight, heads + 1))
        ):
            span = pl.ds(i * columns, columns)
            lanes = pl.ds(spot * HEAD_DIM, table.shape[1])
            copy = pltpu.make_async_copy(
                table.at[span], weights.at[span, lanes], w_sem.at[i, k]
            )
            copy.start()
            tables_here.append(copy)

    lane = lax.broadcasted_iota(jnp.int32, (rows, 128), 1)
    pos = jnp.transpose(jnp.broadcast_to(position[...], (128, rows)))
    owner = jnp.where(pos >= 0, pos // tokens, -1)
    rest = jnp.where(pos >= 0, pos % tokens, 0)
    code = jnp.where(lane == 0, owner, jnp.where(lane == 1, rest, 0))
    buf = m[0]
    buf[rank, :, :width] = hidden[...]
    buf[rank, :, width:] = code.astype(jnp.float32).astype(jnp.bfloat16)
    greet()
    squares, merged = merge_part(
        hidden, merger_here, position, prompt_here, stream, fetches[0], fetches[1], m
    )
    projected = project_part(1e-06, squares, stream, gain, tables_here, sums, p)
    fetches[2].wait()
    fetches[3].wait()

    def turned(h):
        u = sums[:, h * HEAD_DIM : (h + 1) * HEAD_DIM]
        u = u * cosine_here[...] + pltpu.roll(u, HEAD_DIM // 2, 1) * sine_here[...]
        return u.astype(jnp.bfloat16)

    keys[rank, :, :HEAD_DIM] = turned(heads)
    keys[rank, :, HEAD_DIM:] = sums[:, (heads + 1) * HEAD_DIM :].astype(jnp.bfloat16)
    for h in range(heads):
        queries[h] = turned(h)
    k_sent = attend_part(
        queries, keys, context_out, acc, top, total, scores, bias, (k_full, k_half, k_send)
    )
    k_sent()
    projected()
    merged()


def together(hidden, merger_out, position, prompt, gain, wq, wk, wv, cosine, sine):
    rows, width = hidden.shape
    groups = lax.axis_size("role") * lax.axis_size("seq")
    tokens, columns = prompt.shape
    strip = merger_out.shape[1]
    quarter = groups // 4
    slots = groups * quarter * (2 * rows // groups)
    heads = wq.shape[1] // HEAD_DIM
    wide = wq.shape[1] + 2 * HEAD_DIM
    dma = pltpu.SemaphoreType.DMA
    vmem = pl.BlockSpec(memory_space=pltpu.VMEM)
    hbm = pl.BlockSpec(memory_space=pl.ANY)
    bf16, f32 = jnp.bfloat16, jnp.float32
    return pl.pallas_call(
        kernel,
        out_shape=(
            jax.ShapeDtypeStruct(prompt.shape, bf16),
            jax.ShapeDtypeStruct((tokens, wq.shape[1]), bf16),
        ),
        in_specs=[vmem, hbm, vmem, hbm, vmem, hbm, hbm, hbm, hbm, hbm],
        out_specs=(vmem, vmem),
        scratch_shapes=[
            pltpu.VMEM(merger_out.shape, bf16),
            pltpu.VMEM(prompt.shape, bf16),
            pltpu.VMEM((heads, tokens, HEAD_DIM), bf16),
            pltpu.VMEM(cosine.shape, f32),
            pltpu.VMEM(sine.shape, f32),
            pltpu.VMEM((tokens, wide), f32),
            pltpu.VMEM((groups, tokens, 2 * HEAD_DIM), bf16),
            dma((groups,)),
            dma((groups, 2)),
            dma((PLANE_SENDS,)),
            pltpu.VMEM((heads, tokens, HEAD_DIM), f32),
            pltpu.VMEM((heads, tokens, HEAD_DIM), f32),
            pltpu.VMEM((heads, tokens, HEAD_DIM), f32),
            pltpu.VMEM((2, tokens, SIDE * tokens), f32),
            pltpu.VMEM((tokens, SIDE * tokens), f32),
            dma((4,)),
            dma((4, 3)),
            pltpu.VMEM((groups, rows, width + 128), bf16),
            dma((groups,)),
            dma((groups, 2)),
            dma((PLANE_SENDS,)),
            pltpu.VMEM((8, 3, rows, strip), bf16),
            pltpu.VMEM((3, quarter, rows, strip), bf16),
            pltpu.VMEM((quarter, rows, strip), f32),
            dma((8, 3)),
            dma((3, quarter)),
            pltpu.VMEM((quarter * rows, slots), bf16),
            pltpu.VMEM((tokens, 128), f32),
            pltpu.VMEM((slots, strip), bf16),
            pltpu.VMEM((8, slots // 8, strip), bf16),
            dma((groups,)),
            dma((groups,)),
            pltpu.VMEM((4, CHUNKS, tokens, columns // CHUNKS), bf16),
            pltpu.VMEM((4 * columns, wide), bf16),
            pltpu.VMEM((4, 8, tokens), f32),
            dma((3,)),
            dma((3,)),
            dma((3 * CHUNKS,)),
            dma((4, CHUNKS)),
        ],
        compiler_params=pltpu.CompilerParams(
            has_side_effects=True, vmem_limit_bytes=60 << 20, collective_id=0
        ),
    )(hidden, merger_out, position, prompt, gain, wq, wk, wv, cosine, sine)


def body(
    merger_hidden,
    merger_out,
    row_position,
    prompt_embeds,
    norm_gain,
    query_weight,
    key_weight,
    value_weight,
):
    device_rank = lax.axis_index(("role", "seq"))
    tok_count = prompt_embeds.shape[0]
    positions = device_rank * tok_count + jnp.arange(tok_count, dtype=jnp.int32)
    cosine, sine = rotary(positions)
    stream, context = together(
        merger_hidden,
        merger_out,
        row_position[None, :],
        prompt_embeds,
        norm_gain[None, :],
        query_weight,
        key_weight,
        value_weight,
        cosine,
        sine,
    )
    return (stream, context)


def solution(mesh):
    in_specs = (
        P(("role", "seq"), "tp"),
        P("tp", ("role", "seq")),
        P(("role", "seq")),
        P(("role", "seq"), "tp"),
        P("tp"),
        P(None, "tp"),
        P(None, "tp"),
        P(None, "tp"),
    )
    out_specs = (P(("role", "seq"), "tp"), P(("role", "seq"), "tp"))
    return jax.shard_map(body, mesh=mesh, in_specs=in_specs, out_specs=out_specs, check_vma=False)
```

```python
import functools
import math

import jax
import jax.numpy as jnp
from jax import lax
from jax.experimental import pallas as pl
from jax.experimental.pallas import tpu as pltpu
from jax.sharding import PartitionSpec as P

HEAD_DIM = 128


def rotary(positions):
    half_dim = HEAD_DIM // 2
    frequency = 1000000.0 ** (-jnp.arange(half_dim, dtype=jnp.float32) / half_dim)
    angles = positions.astype(jnp.float32)[:, None] * frequency[None, :]
    cosine, sine = jnp.cos(angles), jnp.sin(angles)
    return (
        jnp.concatenate([cosine, cosine], axis=1),
        jnp.concatenate([-sine, sine], axis=1),
    )


MESH = pl.DeviceIdType.MESH
SIDE = 4


def remote(src, dst, send_sem, recv_sem, role, seq, tp):
    return pltpu.make_async_remote_copy(
        src_ref=src,
        dst_ref=dst,
        send_sem=send_sem,
        recv_sem=recv_sem,
        device_id=(role, seq, tp),
        device_id_type=MESH,
    )


def plane_steps(buf, full_sem, half_sem, send_sem):
    role, seq, tp = lax.axis_index("role"), lax.axis_index("seq"), lax.axis_index("tp")
    step_a, step_b = 1 + 3 * role, 4 - 3 * role
    z, x = seq // SIDE, seq % SIDE
    ca = x + role * (z - x)
    cb = z + role * (x - z)
    half = buf.shape[1] // 2
    sent = []

    def seq_of(a, b):
        return ((ca + a + SIDE) % SIDE) * step_a + ((cb + b + SIDE) % SIDE) * step_b

    def slot_of(a, b):
        return role * (SIDE * SIDE) + seq_of(a, b)

    def whole(slot, to_role, to_seq):
        remote(
            buf.at[slot], buf.at[slot], send_sem.at[len(sent)], full_sem.at[slot], to_role, to_seq, tp
        ).start()
        sent.append(2 * half)

    def part(slot, k, to_seq):
        piece = buf.at[slot, pl.ds(k * half, half)]
        remote(
            piece, piece, send_sem.at[len(sent)], half_sem.at[slot, k], role, to_seq, tp
        ).start()
        sent.append(half)

    def wait_whole(slot):
        pltpu.make_async_copy(buf.at[slot], buf.at[slot], full_sem.at[slot]).wait()

    def wait_parts(slot):
        for k in range(2):
            piece = buf.at[slot, pl.ds(k * half, half)]
            pltpu.make_async_copy(piece, piece, half_sem.at[slot, k]).wait()

    def spread_b(slot):
        whole(slot, role, seq_of(0, 1))
        whole(slot, role, seq_of(0, -1))
        whole(slot, 1 - role, seq)

    def pass_b(a):
        for b, k in ((-1, 0), (1, 1)):
            wait_whole(slot_of(a, b))
            part(slot_of(a, b), k, seq_of(0, -b))
            whole(slot_of(a, b), 1 - role, seq)

    def other(b):
        fixed = (ca + b + SIDE) % SIDE
        for k in range(SIDE):
            wait_whole((1 - role) * (SIDE * SIDE) + fixed * step_a + k * step_b)

    def start():
        own = slot_of(0, 0)
        whole(own, role, seq_of(1, 0))
        whole(own, role, seq_of(-1, 0))
        spread_b(own)

    def along():
        for a, k in ((-1, 0), (1, 1)):
            wait_whole(slot_of(a, 0))
            part(slot_of(a, 0), k, seq_of(-a, 0))
            spread_b(slot_of(a, 0))

    def first():
        pass_b(0)
        wait_parts(slot_of(2, 0))
        spread_b(slot_of(2, 0))

    def second():
        pass_b(-1)
        pass_b(1)
        other(0)

    def last():
        for a in (0, -1, 1, 2):
            wait_parts(slot_of(a, 2))
            whole(slot_of(a, 2), 1 - role, seq)
        other(1)

    def mine(b):
        return role, (cb + b + SIDE) % SIDE

    def theirs(b):
        return 1 - role, (ca + b + SIDE) % SIDE

    steps = (
        (start, None),
        (along, None),
        (first, mine(0)),
        (second, theirs(0)),
        (lambda: pass_b(2), mine(-1)),
        (lambda: None, mine(1)),
        (lambda: other(-1), theirs(-1)),
        (last, theirs(1)),
        (lambda: None, mine(2)),
        (lambda: other(2), theirs(2)),
    )

    def finish():
        for n, rows in enumerate(sent):
            piece = buf.at[0, pl.ds(0, rows)]
            pltpu.make_async_copy(piece, piece, send_sem.at[n]).wait()

    return steps, finish


PLANE_SENDS = 2 + 3 * 4 + 2 + 8 + 12
CHUNKS = 4


def iota(shape, dim):
    return lax.broadcasted_iota(jnp.int32, shape, dim).astype(jnp.float32)


def greet():
    role, seq, tp = lax.axis_index("role"), lax.axis_index("seq"), lax.axis_index("tp")
    z, x = seq // SIDE, seq % SIDE
    barrier = pltpu.get_barrier_semaphore()

    def tell(to_role, to_seq, to_tp):
        pl.semaphore_signal(
            barrier, inc=1, device_id=(to_role, to_seq, to_tp), device_id_type=MESH
        )

    tell(1 - role, seq, tp)
    for k in (1, 3):
        tell(role, z * SIDE + (x + k) % SIDE, tp)
        tell(role, ((z + k) % SIDE) * SIDE + x, tp)
    for k in (1, 2, 3):
        tell(role, seq, (tp + k) % 4)

    pl.semaphore_wait(barrier, 8)


def merge_part(
    hidden, weight, position, prompt, stream, weight_here, prompt_here, m
):
    (
        buf,
        full_sem,
        half_sem,
        send_sem,
        partial,
        landed,
        mine,
        y_send,
        y_recv,
        table,
        place,
        packed,
        arrived,
        d_send,
        d_recv,
    ) = m
    role, seq, tp = lax.axis_index("role"), lax.axis_index("seq"), lax.axis_index("tp")
    rank = role * lax.axis_size("seq") + seq
    rows, width = hidden.shape
    tokens = prompt.shape[0]
    groups = buf.shape[0]
    columns = weight.shape[1]
    capacity = 2 * rows // groups
    quarter = groups // 4
    some = SIDE * rows
    copies = []

    def on_line(of_role, fixed):
        n = len(copies) // 3
        if n == 0:
            weight_here.wait()
        step_a, step_b = 1 + 3 * of_role, 4 - 3 * of_role
        pieces, spots = [], []
        for d in (2, 1, 3, 0):
            along = (tp + d + SIDE - fixed) % SIDE
            slot = of_role * (SIDE * SIDE) + along * step_a + fixed * step_b
            pieces.append(buf[slot, :, :width])
            spots.append(of_role * SIDE + fixed + of_role * (along - fixed))
        value = jnp.dot(
            jnp.concatenate(pieces, axis=0), weight[...], preferred_element_type=jnp.float32
        )
        for k, d in enumerate((2, 1, 3)):
            partial[n, k] = value[k * rows : (k + 1) * rows].astype(jnp.bfloat16)
            copy = remote(
                partial.at[n, k],
                landed.at[3 - d, spots[k]],
                y_send.at[n, k],
                y_recv.at[3 - d, spots[k]],
                role,
                seq,
                (tp + d) % 4,
            )
            copy.start()
            copies.append(copy)
        mine[spots[3]] = value[3 * rows :]

    steps, sent = plane_steps(buf, full_sem, half_sem, send_sem)
    for step, line in steps:
        step()
        if line is not None:
            on_line(*line)

    r0 = lax.broadcasted_iota(jnp.int32, (some, some), 0)
    r1 = lax.broadcasted_iota(jnp.int32, (some, some), 1)
    lower = jnp.where((r1 < r0) & (r1 // rows == r0 // rows), 1.0, 0.0).astype(jnp.bfloat16)
    source = lax.broadcasted_iota(jnp.int32, (some, 1), 0) // rows

    def decode(got):
        got = got.astype(jnp.float32)
        owner, rest = got[:, 0:1], got[:, 1:2]
        onehot = jnp.where(owner == iota((some, 128), 1), 1.0, 0.0)
        before = jnp.dot(lower, onehot.astype(jnp.bfloat16), preferred_element_type=jnp.float32)
        return owner, rest, jnp.sum(before * onehot, axis=1, keepdims=True)

    for n in range(quarter // SIDE):
        got = jnp.concatenate(
            [buf[n * 16 + z * SIDE + (tp + SIDE - z) % SIDE, :, width:] for z in range(SIDE)],
            axis=0,
        )
        owner, rest, earlier = decode(got)
        spot = (source + n * SIDE).astype(jnp.float32)
        slot = owner * (quarter * capacity) + spot * capacity + earlier
        table[n * some : (n + 1) * some, :] = jnp.where(
            slot == iota((some, table.shape[1]), 1), 1.0, 0.0
        ).astype(jnp.bfloat16)
    place[...] = jnp.zeros_like(place)

    @pl.loop(0, groups // SIDE)
    def _(n):
        got = buf[pl.ds(n * SIDE, SIDE), :, width:].reshape(some, 128)
        owner, rest, earlier = decode(got)
        here = (rest == iota((some, tokens), 1)) & (owner == rank.astype(jnp.float32))
        spot = ((source + n % SIDE) % SIDE) * quarter + n
        slot = spot.astype(jnp.float32) * capacity + earlier
        there = slot == iota((some, 128), 1)
        place[...] += lax.dot_general(
            jnp.where(here, 1.0, 0.0).astype(jnp.bfloat16),
            jnp.where(there, 1.0, 0.0).astype(jnp.bfloat16),
            (((0,), (0,)), ((), ())),
            preferred_element_type=jnp.float32,
        )

    for i in range(quarter):
        for k in range(3):
            got = landed.at[k, i]
            pltpu.make_async_copy(got, got, y_recv.at[k, i]).wait()
            mine[i] += landed[k, i].astype(jnp.float32)
    packed[...] = lax.dot_general(
        table[...],
        mine[...].reshape(quarter * rows, columns).astype(jnp.bfloat16),
        (((0,), (0,)), ((), ())),
        preferred_element_type=jnp.float32,
    ).astype(jnp.bfloat16)

    piece = quarter * capacity
    to_tp = rank // 8
    lane_group = rank % 8

    def sending(i):
        j = (rank + i) % groups
        return remote(
            packed.at[pl.ds(pl.multiple_of(j * piece, piece), piece)],
            arrived.at[lane_group, pl.ds(pl.multiple_of(tp * piece, piece), piece)],
            d_send.at[i],
            d_recv.at[lane_group * 4 + tp],
            j // 16,
            j % 16,
            to_tp,
        )

    def staying():
        return pltpu.make_async_copy(
            packed.at[pl.ds(pl.multiple_of(rank * piece, piece), piece)],
            arrived.at[lane_group, pl.ds(pl.multiple_of(tp * piece, piece), piece)],
            d_recv.at[lane_group * 4 + tp],
        )

    @pl.when(to_tp == tp)
    def _():
        staying().start()

    @pl.when(to_tp != tp)
    def _():
        sending(0).start()

    @pl.loop(1, groups)
    def _(i):
        sending(i).start()

    chosen = place[...].astype(jnp.bfloat16)
    hit = jnp.max(place[...], axis=1, keepdims=True) > 0.5
    prompt_here.wait()
    total = jnp.zeros((tokens, 128), jnp.float32)
    for c in range(8):
        for k in range(4):
            got = arrived.at[c, pl.ds(k * piece, piece)]
            pltpu.make_async_copy(got, got, d_recv.at[c * 4 + k]).wait()
        rows_here = jnp.dot(chosen, arrived[c], preferred_element_type=jnp.float32)
        span = slice(c * columns, (c + 1) * columns)
        x = jnp.where(hit, rows_here, prompt[:, span].astype(jnp.float32))
        stream[:, span] = x.astype(jnp.bfloat16)
        for k in range(0, columns, 128):
            total = total + x[:, k : k + 128] * x[:, k : k + 128]

    def finish():
        sent()
        for copy in copies:
            copy.wait_send()

        @pl.when(to_tp != tp)
        def _():
            sending(0).wait_send()

        @pl.loop(1, groups)
        def _(i):
            sending(i).wait_send()

    return total, finish


def project_part(eps, total, stream, gain, tables_here, acc, m):
    normed, weights, squares, s_send, s_recv, n_send, n_recv = m
    role, seq, tp = lax.axis_index("role"), lax.axis_index("seq"), lax.axis_index("tp")
    rows, columns = stream.shape
    chunk = columns // 2
    few = rows // 2
    squares[3] = jnp.broadcast_to(
        jnp.sum(jnp.transpose(total), axis=0, keepdims=True), (8, rows)
    )
    sums = []
    for k, off in enumerate((1, 3, 2)):
        copy = remote(
            squares.at[3], squares.at[k], s_send.at[k], s_recv.at[k], role, seq, (tp + off) % 4
        )
        copy.start()
        sums.append(copy)
    for copy in sums:
        copy.wait()
    whole = squares[0] + squares[1] + (squares[2] + squares[3])
    whole = jnp.broadcast_to(whole[0:1], (128, rows))
    inverse = lax.rsqrt(jnp.transpose(whole) / (4 * columns) + eps)[:, 0:1]

    sent = []

    def send(t, hf, c, off):
        remote(
            normed.at[t, hf, c],
            normed.at[t, hf, c],
            n_send.at[len(sent)],
            n_recv.at[t, 2 * hf + c],
            role,
            seq,
            (tp + off + 4) % 4,
        ).start()
        sent.append(off)

    def arrive(t, hf, c):
        got = normed.at[t, hf, c]
        pltpu.make_async_copy(got, got, n_recv.at[t, 2 * hf + c]).wait()

    def scale(hf, c):
        span = slice(c * chunk, (c + 1) * chunk)
        part = slice(hf * few, (hf + 1) * few)
        x = stream[part, span].astype(jnp.float32)
        normed[tp, hf, c] = (
            x * inverse[part] * gain[:, span].astype(jnp.float32)
        ).astype(jnp.bfloat16)

    before, after, across = (tp + 3) % 4, (tp + 1) % 4, (tp + 2) % 4

    def multiply(t, hf, c, first=False):
        span = pl.ds(pl.multiple_of(t * columns + c * chunk, chunk), chunk)
        part = slice(hf * few, (hf + 1) * few)
        value = jnp.dot(normed[t, hf, c], weights[span, :], preferred_element_type=jnp.float32)
        if first:
            acc[part, :] = value
        else:
            acc[part, :] += value

    def send_own(hf):
        send(tp, hf, 0, 1)
        send(tp, hf, 1, -1)
        send(tp, hf, 1, 1)
        send(tp, hf, 0, -1)

    def near(hf):
        arrive(before, hf, 0)
        send(before, hf, 0, 1)
        arrive(after, hf, 1)
        send(after, hf, 1, -1)
        if hf == 0:
            send_own(1)
        multiply(before, hf, 0)
        multiply(after, hf, 1)

    def rest(hf):
        arrive(before, hf, 1)
        multiply(before, hf, 1)
        arrive(after, hf, 0)
        multiply(after, hf, 0)
        for c in range(2):
            arrive(across, hf, c)
            multiply(across, hf, c)

    scale(0, 0)
    scale(0, 1)
    send_own(0)
    scale(1, 0)
    scale(1, 1)
    for copy in tables_here:
        copy.wait()
    for hf in range(2):
        for c in range(2):
            multiply(tp, hf, c, c == 0)
    near(0)
    rest(0)

    def finish():
        for n in range(len(sent)):
            piece = normed.at[0, 0, 0]
            pltpu.make_async_copy(piece, piece, n_send.at[n]).wait()

    return near, rest, finish


def line_slots(of_role, fixed):
    step_a, step_b = 1 + 3 * of_role, 4 - 3 * of_role
    return [of_role * (SIDE * SIDE) + n * step_a + fixed * step_b for n in range(SIDE)]


def attend_to(q_ref, buf, hf, slots, part, acc, top, total, scores, bias, rank):
    heads, rows = q_ref.shape[:2]
    few = buf.shape[1]
    count = part.stop - part.start
    span = len(slots) * few
    factor = math.log2(math.e) / math.sqrt(HEAD_DIM)
    low, high = slots[0], slots[0]
    for slot in slots[1:]:
        low, high = jnp.minimum(low, slot), jnp.maximum(high, slot)

    def block(masked):
        k = jnp.concatenate([buf[slot, :, :HEAD_DIM] for slot in slots], axis=0)
        v = jnp.concatenate([buf[slot, :, HEAD_DIM:] for slot in slots], axis=0)
        if masked:
            ahead = lax.broadcasted_iota(jnp.int32, (count, few), 1) - lax.broadcasted_iota(
                jnp.int32, (count, few), 0
            )
            for n, slot in enumerate(slots):
                bias[:count, n * few : (n + 1) * few] = jnp.where(
                    ahead <= (rank - slot) * rows + part.start - hf * few, 0.0, -1e30
                )

        def score(h):
            scores[h % 2, :count] = lax.dot_general(
                q_ref[h, part], k, (((1,), (1,)), ((), ())), preferred_element_type=jnp.float32
            )

        score(0)
        for h in range(heads):
            if h + 1 < heads:
                score(h + 1)
            s = scores[h % 2, :count]
            if masked:
                s = s + bias[:count]
            old = top[h, part][:, :1]
            new = jnp.maximum(old, jnp.max(s, axis=1, keepdims=True))
            p = jnp.exp2((s - new) * factor)
            alpha = jnp.exp2((old - new) * factor)
            some = p[:, :HEAD_DIM]
            for c in range(HEAD_DIM, span, HEAD_DIM):
                some = some + p[:, c : c + HEAD_DIM]
            total[h, part] = total[h, part] * alpha + some
            acc[h, part] = acc[h, part] * alpha + jnp.dot(
                p.astype(jnp.bfloat16), v, preferred_element_type=jnp.float32
            )
            top[h, part] = jnp.broadcast_to(new, (count, HEAD_DIM))

    pl.when(high < rank)(lambda: block(False))
    pl.when((low <= rank) & (high >= rank))(lambda: block(True))


def in_steps(steps, visit, extra=()):
    @pl.loop(0, len(steps))
    def _(e):
        for n, (step, _) in enumerate(steps):
            pl.when(e == n)(step)
        of_role, fixed = steps[2][1]
        for n, (_, line) in enumerate(steps[2:]):
            of_role = jnp.where(e == n + 2, line[0], of_role)
            fixed = jnp.where(e == n + 2, line[1], fixed)
        visit(e, of_role, fixed)
        for n, act in extra:
            pl.when(e == n)(act)


MERGE_SCRATCH = 15
PROJECT_SCRATCH = 7


def kernel(
    hidden,
    merger_out,
    position,
    prompt,
    gain,
    query_weight,
    key_weight,
    value_weight,
    cosine,
    sine,
    stream,
    context_out,
    merger_here,
    prompt_here,
    queries,
    cosine_here,
    sine_here,
    sums,
    keys_0,
    keys_1,
    k_full,
    k_half,
    k_send,
    acc,
    top,
    total,
    scores,
    bias,
    long_scores,
    long_bias,
    in_sem,
    w_sem,
    *more,
):
    m, p = more[:MERGE_SCRATCH], more[MERGE_SCRATCH:]
    role, seq, tp = lax.axis_index("role"), lax.axis_index("seq"), lax.axis_index("tp")
    rank = role * lax.axis_size("seq") + seq
    rows, width = hidden.shape
    tokens = prompt.shape[0]
    columns = prompt.shape[1]
    heads = query_weight.shape[1] // HEAD_DIM

    fetches = []
    for k, (src, dst) in enumerate(
        (
            (merger_out, merger_here),
            (prompt, prompt_here),
            (cosine, cosine_here),
            (sine, sine_here),
        )
    ):
        copy = pltpu.make_async_copy(src, dst, in_sem.at[k])
        copy.start()
        fetches.append(copy)
    weights = p[1]
    tables_here = []
    for i in range(4):
        for k, (table, spot) in enumerate(
            ((query_weight, 0), (key_weight, heads), (value_weight, heads + 1))
        ):
            span = pl.ds(i * columns, columns)
            lanes = pl.ds(spot * HEAD_DIM, table.shape[1])
            copy = pltpu.make_async_copy(
                table.at[span], weights.at[span, lanes], w_sem.at[i, k]
            )
            copy.start()
            tables_here.append(copy)

    lane = lax.broadcasted_iota(jnp.int32, (rows, 128), 1)
    pos = jnp.transpose(jnp.broadcast_to(position[...], (128, rows)))
    owner = jnp.where(pos >= 0, pos // tokens, -1)
    rest = jnp.where(pos >= 0, pos % tokens, 0)
    code = jnp.where(lane == 0, owner, jnp.where(lane == 1, rest, 0))
    buf = m[0]
    buf[rank, :, :width] = hidden[...]
    buf[rank, :, width:] = code.astype(jnp.float32).astype(jnp.bfloat16)
    greet()
    squares, merged = merge_part(
        hidden, merger_here, position, prompt_here, stream, fetches[0], fetches[1], m
    )
    near, rest, projected = project_part(1e-06, squares, stream, gain, tables_here, sums, p)
    fetches[2].wait()
    fetches[3].wait()

    few = tokens // 2
    state = (acc, top, total)
    acc[...] = jnp.zeros_like(acc)
    total[...] = jnp.zeros_like(total)
    top[...] = jnp.full_like(top, -1e30)
    halves = (slice(0, few), slice(few, tokens))

    def rotated(hf):
        part = halves[hf]

        def turned(h):
            u = sums[part, h * HEAD_DIM : (h + 1) * HEAD_DIM]
            u = u * cosine_here[part] + pltpu.roll(u, HEAD_DIM // 2, 1) * sine_here[part]
            return u.astype(jnp.bfloat16)

        keys[hf][rank, :, :HEAD_DIM] = turned(heads)
        keys[hf][rank, :, HEAD_DIM:] = sums[part, (heads + 1) * HEAD_DIM :].astype(jnp.bfloat16)
        for h in range(heads):
            queries[h, part] = turned(h)

    keys = (keys_0, keys_1)
    rotated(0)
    steps, sent_0 = plane_steps(keys_0, k_full.at[0], k_half.at[0], k_send.at[0])

    def visit_0(e, of_role, fixed):
        @pl.when(e >= 2)
        def _():
            attend_to(
                queries, keys_0, 0, line_slots(of_role, fixed), halves[0], *state, scores, bias, rank
            )

    in_steps(steps, visit_0, ((2, lambda: near(1)),))
    rest(1)
    rotated(1)
    steps, sent_1 = plane_steps(keys_1, k_full.at[1], k_half.at[1], k_send.at[1])
    everyone = slice(0, tokens)

    def visit_1(e, of_role, fixed):
        @pl.when(e < 4)
        def _():
            slots = line_slots(e // 2, 2 * (e % 2)) + line_slots(e // 2, 2 * (e % 2) + 1)
            attend_to(
                queries, keys_0, 0, slots, halves[1], *state, long_scores, long_bias, rank
            )

        @pl.when(e >= 2)
        def _():
            attend_to(
                queries, keys_1, 1, line_slots(of_role, fixed), everyone, *state, scores, bias, rank
            )

    in_steps(steps, visit_1)
    for h in range(heads):
        l = jnp.sum(total[h], axis=1, keepdims=True)
        context_out[:, h * HEAD_DIM : (h + 1) * HEAD_DIM] = (acc[h] / l).astype(context_out.dtype)
    sent_0()
    sent_1()
    projected()
    merged()


def together(hidden, merger_out, position, prompt, gain, wq, wk, wv, cosine, sine):
    rows, width = hidden.shape
    groups = lax.axis_size("role") * lax.axis_size("seq")
    tokens, columns = prompt.shape
    strip = merger_out.shape[1]
    quarter = groups // 4
    slots = groups * quarter * (2 * rows // groups)
    heads = wq.shape[1] // HEAD_DIM
    wide = wq.shape[1] + 2 * HEAD_DIM
    dma = pltpu.SemaphoreType.DMA
    vmem = pl.BlockSpec(memory_space=pltpu.VMEM)
    hbm = pl.BlockSpec(memory_space=pl.ANY)
    bf16, f32 = jnp.bfloat16, jnp.float32
    return pl.pallas_call(
        kernel,
        out_shape=(
            jax.ShapeDtypeStruct(prompt.shape, bf16),
            jax.ShapeDtypeStruct((tokens, wq.shape[1]), bf16),
        ),
        in_specs=[vmem, hbm, vmem, hbm, vmem, hbm, hbm, hbm, hbm, hbm],
        out_specs=(vmem, vmem),
        scratch_shapes=[
            pltpu.VMEM(merger_out.shape, bf16),
            pltpu.VMEM(prompt.shape, bf16),
            pltpu.VMEM((heads, tokens, HEAD_DIM), bf16),
            pltpu.VMEM(cosine.shape, f32),
            pltpu.VMEM(sine.shape, f32),
            pltpu.VMEM((tokens, wide), f32),
            pltpu.VMEM((groups, tokens // 2, 2 * HEAD_DIM), bf16),
            pltpu.VMEM((groups, tokens // 2, 2 * HEAD_DIM), bf16),
            dma((2, groups)),
            dma((2, groups, 2)),
            dma((2, PLANE_SENDS)),
            pltpu.VMEM((heads, tokens, HEAD_DIM), f32),
            pltpu.VMEM((heads, tokens, HEAD_DIM), f32),
            pltpu.VMEM((heads, tokens, HEAD_DIM), f32),
            pltpu.VMEM((2, tokens, SIDE * tokens // 2), f32),
            pltpu.VMEM((tokens, SIDE * tokens // 2), f32),
            pltpu.VMEM((2, tokens // 2, SIDE * tokens), f32),
            pltpu.VMEM((tokens // 2, SIDE * tokens), f32),
            dma((4,)),
            dma((4, 3)),
            pltpu.VMEM((groups, rows, width + 128), bf16),
            dma((groups,)),
            dma((groups, 2)),
            dma((PLANE_SENDS,)),
            pltpu.VMEM((8, 3, rows, strip), bf16),
            pltpu.VMEM((3, quarter, rows, strip), bf16),
            pltpu.VMEM((quarter, rows, strip), f32),
            dma((8, 3)),
            dma((3, quarter)),
            pltpu.VMEM((quarter * rows, slots), bf16),
            pltpu.VMEM((tokens, 128), f32),
            pltpu.VMEM((slots, strip), bf16),
            pltpu.VMEM((8, slots // 8, strip), bf16),
            dma((groups,)),
            dma((groups,)),
            pltpu.VMEM((4, 2, 2, tokens // 2, columns // 2), bf16),
            pltpu.VMEM((4 * columns, wide), bf16),
            pltpu.VMEM((4, 8, tokens), f32),
            dma((3,)),
            dma((3,)),
            dma((3 * CHUNKS,)),
            dma((4, CHUNKS)),
        ],
        compiler_params=pltpu.CompilerParams(
            has_side_effects=True, vmem_limit_bytes=60 << 20, collective_id=0
        ),
    )(hidden, merger_out, position, prompt, gain, wq, wk, wv, cosine, sine)


def body(
    merger_hidden,
    merger_out,
    row_position,
    prompt_embeds,
    norm_gain,
    query_weight,
    key_weight,
    value_weight,
):
    device_rank = lax.axis_index(("role", "seq"))
    tok_count = prompt_embeds.shape[0]
    positions = device_rank * tok_count + jnp.arange(tok_count, dtype=jnp.int32)
    cosine, sine = rotary(positions)
    stream, context = together(
        merger_hidden,
        merger_out,
        row_position[None, :],
        prompt_embeds,
        norm_gain[None, :],
        query_weight,
        key_weight,
        value_weight,
        cosine,
        sine,
    )
    return (stream, context)


def solution(mesh):
    in_specs = (
        P(("role", "seq"), "tp"),
        P("tp", ("role", "seq")),
        P(("role", "seq")),
        P(("role", "seq"), "tp"),
        P("tp"),
        P(None, "tp"),
        P(None, "tp"),
        P(None, "tp"),
    )
    out_specs = (P(("role", "seq"), "tp"), P(("role", "seq"), "tp"))
    return jax.shard_map(body, mesh=mesh, in_specs=in_specs, out_specs=out_specs, check_vma=False)
```

```python
import functools
import math

import jax
import jax.numpy as jnp
from jax import lax
from jax.experimental import pallas as pl
from jax.experimental.pallas import tpu as pltpu
from jax.sharding import PartitionSpec as P

HEAD_DIM = 128


def rotary(positions):
    half_dim = HEAD_DIM // 2
    frequency = 1000000.0 ** (-jnp.arange(half_dim, dtype=jnp.float32) / half_dim)
    angles = positions.astype(jnp.float32)[:, None] * frequency[None, :]
    cosine, sine = jnp.cos(angles), jnp.sin(angles)
    return cosine, sine


MESH = pl.DeviceIdType.MESH
SIDE = 4


def remote(src, dst, send_sem, recv_sem, role, seq, tp):
    return pltpu.make_async_remote_copy(
        src_ref=src,
        dst_ref=dst,
        send_sem=send_sem,
        recv_sem=recv_sem,
        device_id=(role, seq, tp),
        device_id_type=MESH,
    )


def plane_steps(buf, full_sem, half_sem, send_sem):
    role, seq, tp = lax.axis_index("role"), lax.axis_index("seq"), lax.axis_index("tp")
    step_a, step_b = 1 + 3 * role, 4 - 3 * role
    z, x = seq // SIDE, seq % SIDE
    ca = x + role * (z - x)
    cb = z + role * (x - z)
    half = buf.shape[1] // 2
    sent = []

    def seq_of(a, b):
        return ((ca + a + SIDE) % SIDE) * step_a + ((cb + b + SIDE) % SIDE) * step_b

    def slot_of(a, b):
        return role * (SIDE * SIDE) + seq_of(a, b)

    def whole(slot, to_role, to_seq):
        remote(
            buf.at[slot], buf.at[slot], send_sem.at[len(sent)], full_sem.at[slot], to_role, to_seq, tp
        ).start()
        sent.append(2 * half)

    def part(slot, k, to_seq):
        piece = buf.at[slot, pl.ds(k * half, half)]
        remote(
            piece, piece, send_sem.at[len(sent)], half_sem.at[slot, k], role, to_seq, tp
        ).start()
        sent.append(half)

    def wait_whole(slot):
        pltpu.make_async_copy(buf.at[slot], buf.at[slot], full_sem.at[slot]).wait()

    def wait_parts(slot):
        for k in range(2):
            piece = buf.at[slot, pl.ds(k * half, half)]
            pltpu.make_async_copy(piece, piece, half_sem.at[slot, k]).wait()

    def spread_b(slot):
        whole(slot, role, seq_of(0, 1))
        whole(slot, role, seq_of(0, -1))
        whole(slot, 1 - role, seq)

    def pass_b(a):
        for b, k in ((-1, 0), (1, 1)):
            wait_whole(slot_of(a, b))
            part(slot_of(a, b), k, seq_of(0, -b))
            whole(slot_of(a, b), 1 - role, seq)

    def other(b):
        fixed = (ca + b + SIDE) % SIDE
        for k in range(SIDE):
            wait_whole((1 - role) * (SIDE * SIDE) + fixed * step_a + k * step_b)

    def start():
        own = slot_of(0, 0)
        whole(own, role, seq_of(1, 0))
        whole(own, role, seq_of(-1, 0))
        spread_b(own)

    def along():
        for a, k in ((-1, 0), (1, 1)):
            wait_whole(slot_of(a, 0))
            part(slot_of(a, 0), k, seq_of(-a, 0))
            spread_b(slot_of(a, 0))

    def first():
        pass_b(0)
        wait_parts(slot_of(2, 0))
        spread_b(slot_of(2, 0))

    def second():
        pass_b(-1)
        pass_b(1)
        other(0)

    def last():
        for a in (0, -1, 1, 2):
            wait_parts(slot_of(a, 2))
            whole(slot_of(a, 2), 1 - role, seq)
        other(1)

    def mine(b):
        return role, (cb + b + SIDE) % SIDE

    def theirs(b):
        return 1 - role, (ca + b + SIDE) % SIDE

    steps = (
        (start, None),
        (along, None),
        (first, mine(0)),
        (second, theirs(0)),
        (lambda: pass_b(2), mine(-1)),
        (lambda: None, mine(1)),
        (lambda: other(-1), theirs(-1)),
        (last, theirs(1)),
        (lambda: None, mine(2)),
        (lambda: other(2), theirs(2)),
    )

    def finish():
        for n, rows in enumerate(sent):
            piece = buf.at[0, pl.ds(0, rows)]
            pltpu.make_async_copy(piece, piece, send_sem.at[n]).wait()

    return steps, finish


PLANE_SENDS = 2 + 3 * 4 + 2 + 8 + 12
CHUNKS = 4


def iota(shape, dim):
    return lax.broadcasted_iota(jnp.int32, shape, dim).astype(jnp.float32)


def greet():
    role, seq, tp = lax.axis_index("role"), lax.axis_index("seq"), lax.axis_index("tp")
    z, x = seq // SIDE, seq % SIDE
    barrier = pltpu.get_barrier_semaphore()

    def tell(to_role, to_seq, to_tp):
        pl.semaphore_signal(
            barrier, inc=1, device_id=(to_role, to_seq, to_tp), device_id_type=MESH
        )

    tell(1 - role, seq, tp)
    for k in (1, 3):
        tell(role, z * SIDE + (x + k) % SIDE, tp)
        tell(role, ((z + k) % SIDE) * SIDE + x, tp)
    for k in (1, 2, 3):
        tell(role, seq, (tp + k) % 4)

    pl.semaphore_wait(barrier, 8)


def merge_part(
    hidden, weight, position, prompt, stream, weight_here, prompt_here, m
):
    (
        buf,
        full_sem,
        half_sem,
        send_sem,
        partial,
        landed,
        mine,
        y_send,
        y_recv,
        table,
        place,
        packed,
        arrived,
        d_send,
        d_recv,
    ) = m
    role, seq, tp = lax.axis_index("role"), lax.axis_index("seq"), lax.axis_index("tp")
    rank = role * lax.axis_size("seq") + seq
    rows, width = hidden.shape
    tokens = prompt.shape[0]
    groups = buf.shape[0]
    columns = weight.shape[1]
    capacity = 2 * rows // groups
    quarter = groups // 4
    some = SIDE * rows
    copies = []

    def on_line(of_role, fixed):
        n = len(copies) // 3
        if n == 0:
            weight_here.wait()
        step_a, step_b = 1 + 3 * of_role, 4 - 3 * of_role
        pieces, spots = [], []
        for d in (2, 1, 3, 0):
            along = (tp + d + SIDE - fixed) % SIDE
            slot = of_role * (SIDE * SIDE) + along * step_a + fixed * step_b
            pieces.append(buf[slot, :, :width])
            spots.append(of_role * SIDE + fixed + of_role * (along - fixed))
        value = jnp.dot(
            jnp.concatenate(pieces, axis=0), weight[...], preferred_element_type=jnp.float32
        )
        for k, d in enumerate((2, 1, 3)):
            partial[n, k] = value[k * rows : (k + 1) * rows].astype(jnp.bfloat16)
            copy = remote(
                partial.at[n, k],
                landed.at[3 - d, spots[k]],
                y_send.at[n, k],
                y_recv.at[3 - d, spots[k]],
                role,
                seq,
                (tp + d) % 4,
            )
            copy.start()
            copies.append(copy)
        mine[spots[3]] = value[3 * rows :]

    steps, sent = plane_steps(buf, full_sem, half_sem, send_sem)
    for step, line in steps:
        step()
        if line is not None:
            on_line(*line)

    r0 = lax.broadcasted_iota(jnp.int32, (some, some), 0)
    r1 = lax.broadcasted_iota(jnp.int32, (some, some), 1)
    lower = jnp.where((r1 < r0) & (r1 // rows == r0 // rows), 1.0, 0.0).astype(jnp.bfloat16)
    source = lax.broadcasted_iota(jnp.int32, (some, 1), 0) // rows

    def decode(got):
        got = got.astype(jnp.float32)
        owner, rest = got[:, 0:1], got[:, 1:2]
        onehot = jnp.where(owner == iota((some, 128), 1), 1.0, 0.0)
        before = jnp.dot(lower, onehot.astype(jnp.bfloat16), preferred_element_type=jnp.float32)
        return owner, rest, jnp.sum(before * onehot, axis=1, keepdims=True)

    for n in range(quarter // SIDE):
        got = jnp.concatenate(
            [buf[n * 16 + z * SIDE + (tp + SIDE - z) % SIDE, :, width:] for z in range(SIDE)],
            axis=0,
        )
        owner, rest, earlier = decode(got)
        spot = (source + n * SIDE).astype(jnp.float32)
        slot = owner * (quarter * capacity) + spot * capacity + earlier
        table[n * some : (n + 1) * some, :] = jnp.where(
            slot == iota((some, table.shape[1]), 1), 1.0, 0.0
        ).astype(jnp.bfloat16)
    place[...] = jnp.zeros_like(place)

    @pl.loop(0, groups // SIDE)
    def _(n):
        got = buf[pl.ds(n * SIDE, SIDE), :, width:].reshape(some, 128)
        owner, rest, earlier = decode(got)
        here = (rest == iota((some, tokens), 1)) & (owner == rank.astype(jnp.float32))
        spot = ((source + n % SIDE) % SIDE) * quarter + n
        slot = spot.astype(jnp.float32) * capacity + earlier
        there = slot == iota((some, 128), 1)
        place[...] += lax.dot_general(
            jnp.where(here, 1.0, 0.0).astype(jnp.bfloat16),
            jnp.where(there, 1.0, 0.0).astype(jnp.bfloat16),
            (((0,), (0,)), ((), ())),
            preferred_element_type=jnp.float32,
        )

    for i in range(quarter):
        for k in range(3):
            got = landed.at[k, i]
            pltpu.make_async_copy(got, got, y_recv.at[k, i]).wait()
            mine[i] += landed[k, i].astype(jnp.float32)
    packed[...] = lax.dot_general(
        table[...],
        mine[...].reshape(quarter * rows, columns).astype(jnp.bfloat16),
        (((0,), (0,)), ((), ())),
        preferred_element_type=jnp.float32,
    ).astype(jnp.bfloat16)

    piece = quarter * capacity
    to_tp = rank // 8
    lane_group = rank % 8

    def sending(i):
        j = (rank + i) % groups
        return remote(
            packed.at[pl.ds(pl.multiple_of(j * piece, piece), piece)],
            arrived.at[lane_group, pl.ds(pl.multiple_of(tp * piece, piece), piece)],
            d_send.at[i],
            d_recv.at[lane_group * 4 + tp],
            j // 16,
            j % 16,
            to_tp,
        )

    def staying():
        return pltpu.make_async_copy(
            packed.at[pl.ds(pl.multiple_of(rank * piece, piece), piece)],
            arrived.at[lane_group, pl.ds(pl.multiple_of(tp * piece, piece), piece)],
            d_recv.at[lane_group * 4 + tp],
        )

    @pl.when(to_tp == tp)
    def _():
        staying().start()

    @pl.when(to_tp != tp)
    def _():
        sending(0).start()

    @pl.loop(1, groups)
    def _(i):
        sending(i).start()

    chosen = place[...].astype(jnp.bfloat16)
    hit = jnp.max(place[...], axis=1, keepdims=True) > 0.5
    prompt_here.wait()
    total = jnp.zeros((tokens, 128), jnp.float32)
    for c in range(8):
        for k in range(4):
            got = arrived.at[c, pl.ds(k * piece, piece)]
            pltpu.make_async_copy(got, got, d_recv.at[c * 4 + k]).wait()
        rows_here = jnp.dot(chosen, arrived[c], preferred_element_type=jnp.float32)
        span = slice(c * columns, (c + 1) * columns)
        x = jnp.where(hit, rows_here, prompt[:, span].astype(jnp.float32))
        stream[:, span] = x.astype(jnp.bfloat16)
        for k in range(0, columns, 128):
            total = total + x[:, k : k + 128] * x[:, k : k + 128]

    def finish():
        sent()
        for copy in copies:
            copy.wait_send()

        @pl.when(to_tp != tp)
        def _():
            sending(0).wait_send()

        @pl.loop(1, groups)
        def _(i):
            sending(i).wait_send()

    return total, finish


def project_part(eps, total, stream, gain, tables_here, acc, meanwhile, m):
    normed, weights, squares, s_send, s_recv, n_send, n_recv = m
    role, seq, tp = lax.axis_index("role"), lax.axis_index("seq"), lax.axis_index("tp")
    rows, columns = stream.shape
    chunk = columns // CHUNKS
    squares[3] = jnp.broadcast_to(
        jnp.sum(jnp.transpose(total), axis=0, keepdims=True), (8, rows)
    )
    sums = []
    for k, off in enumerate((1, 3, 2)):
        copy = remote(
            squares.at[3], squares.at[k], s_send.at[k], s_recv.at[k], role, seq, (tp + off) % 4
        )
        copy.start()
        sums.append(copy)
    meanwhile()
    for copy in sums:
        copy.wait()
    whole = squares[0] + squares[1] + (squares[2] + squares[3])
    whole = jnp.broadcast_to(whole[0:1], (128, rows))
    inverse = lax.rsqrt(jnp.transpose(whole) / (4 * columns) + eps)[:, 0:1]

    copies = []

    def send(t, c, off):
        copy = remote(
            normed.at[t, c],
            normed.at[t, c],
            n_send.at[len(copies)],
            n_recv.at[t, c],
            role,
            seq,
            (tp + off + 4) % 4,
        )
        copy.start()
        copies.append(copy)

    def arrive(t, c):
        pltpu.make_async_copy(normed.at[t, c], normed.at[t, c], n_recv.at[t, c]).wait()

    def scale(c):
        span = slice(c * chunk, (c + 1) * chunk)
        x = stream[:, span].astype(jnp.float32)
        normed[tp, c] = (x * inverse * gain[span].astype(jnp.float32).reshape(1, chunk)).astype(jnp.bfloat16)

    scale(0)
    send(tp, 0, 1)
    scale(2)
    send(tp, 2, -1)
    scale(1)
    send(tp, 1, 1)
    scale(3)
    send(tp, 3, -1)
    send(tp, 2, 1)
    send(tp, 0, -1)
    send(tp, 3, 1)
    send(tp, 1, -1)
    before, after, across = (tp + 3) % 4, (tp + 1) % 4, (tp + 2) % 4

    def multiply(t, c, first=False):
        span = pl.ds(pl.multiple_of(t * columns + c * chunk, chunk), chunk)
        value = jnp.dot(normed[t, c], weights[span, :], preferred_element_type=jnp.float32)
        if first:
            acc[...] = value
        else:
            acc[...] += value

    for copy in tables_here:
        copy.wait()
    for c in range(CHUNKS):
        multiply(tp, c, c == 0)
    for c, d in ((0, 2), (1, 3)):
        arrive(before, c)
        send(before, c, 1)
        arrive(after, d)
        send(after, d, -1)
        multiply(before, c)
        multiply(after, d)
    for c, d in ((2, 0), (3, 1)):
        arrive(before, c)
        multiply(before, c)
        arrive(after, d)
        multiply(after, d)
    for c in (0, 2, 1, 3):
        arrive(across, c)
        multiply(across, c)

    def finish():
        for copy in copies:
            copy.wait_send()

    return finish


def attend_part(q_ref, buf, o_ref, acc, top, total, scores, bias, steps):
    heads, rows = q_ref.shape[:2]
    role, seq = lax.axis_index("role"), lax.axis_index("seq")
    z, x = seq // SIDE, seq % SIDE
    rank = role * (SIDE * SIDE) + seq
    factor = math.log2(math.e) / math.sqrt(HEAD_DIM)
    span = SIDE * rows

    def block(slots, masked):
        k = jnp.concatenate([buf[slot, :, :HEAD_DIM] for slot in slots], axis=0)
        v = jnp.concatenate([buf[slot, :, HEAD_DIM:] for slot in slots], axis=0)
        if masked:
            ahead = lax.broadcasted_iota(jnp.int32, (rows, rows), 1) - lax.broadcasted_iota(
                jnp.int32, (rows, rows), 0
            )
            for n, slot in enumerate(slots):
                bias[:, n * rows : (n + 1) * rows] = jnp.where(
                    ahead <= (rank - slot) * rows, 0.0, -1e30
                )

        def score(h):
            scores[h % 2] = lax.dot_general(
                q_ref[h], k, (((1,), (1,)), ((), ())), preferred_element_type=jnp.float32
            )

        score(0)
        for h in range(heads):
            if h + 1 < heads:
                score(h + 1)
            s = scores[h % 2]
            if masked:
                s = s + bias[...]
            old = top[h][:, :1]
            new = jnp.maximum(old, jnp.max(s, axis=1, keepdims=True))
            p = jnp.exp2((s - new) * factor)
            alpha = jnp.exp2((old - new) * factor)
            part = p[:, :HEAD_DIM]
            for c in range(HEAD_DIM, span, HEAD_DIM):
                part = part + p[:, c : c + HEAD_DIM]
            total[h] = total[h] * alpha + part
            acc[h] = acc[h] * alpha + jnp.dot(
                p.astype(jnp.bfloat16), v, preferred_element_type=jnp.float32
            )
            top[h] = jnp.broadcast_to(new, (rows, HEAD_DIM))

    @pl.loop(0, len(steps))
    def _(e):
        for n, (step, _) in enumerate(steps):
            pl.when(e == n)(step)
        of_role, fixed = steps[0][1]
        for n, (_, line) in enumerate(steps):
            of_role = jnp.where(e == n, line[0], of_role)
            fixed = jnp.where(e == n, line[1], fixed)
        step_a, step_b = 1 + 3 * of_role, 4 - 3 * of_role
        slots = [
            of_role * (SIDE * SIDE) + along * step_a + fixed * step_b for along in range(SIDE)
        ]
        clear = slots[-1] < rank
        some = slots[0] <= rank
        pl.when(clear)(lambda: block(slots, False))
        pl.when(some & jnp.logical_not(clear))(lambda: block(slots, True))

    for h in range(heads):
        l = jnp.sum(total[h], axis=1, keepdims=True)
        o_ref[:, h * HEAD_DIM : (h + 1) * HEAD_DIM] = (acc[h] / l).astype(o_ref.dtype)


MERGE_SCRATCH = 15
PROJECT_SCRATCH = 7


def kernel(
    hidden,
    merger_out,
    position,
    prompt,
    gain,
    query_weight,
    key_weight,
    value_weight,
    cosine,
    sine,
    stream,
    context_out,
    merger_here,
    prompt_here,
    queries,
    cosine_here,
    sine_here,
    sums,
    keys,
    k_full,
    k_half,
    k_send,
    acc,
    top,
    total,
    scores,
    bias,
    in_sem,
    w_sem,
    *more,
):
    m, p = more[:MERGE_SCRATCH], more[MERGE_SCRATCH:]
    role, seq, tp = lax.axis_index("role"), lax.axis_index("seq"), lax.axis_index("tp")
    rank = role * lax.axis_size("seq") + seq
    rows, width = hidden.shape
    tokens = prompt.shape[0]
    columns = prompt.shape[1]
    heads = query_weight.shape[1] // HEAD_DIM

    fetches = []
    for k, (src, dst) in enumerate(
        (
            (merger_out, merger_here),
            (prompt, prompt_here),
            (cosine, cosine_here),
            (sine, sine_here),
        )
    ):
        copy = pltpu.make_async_copy(src, dst, in_sem.at[k])
        copy.start()
        fetches.append(copy)
    weights = p[1]
    tables_here = []
    for i in range(4):
        for k, (table, spot) in enumerate(
            ((query_weight, 0), (key_weight, heads), (value_weight, heads + 1))
        ):
            span = pl.ds(i * columns, columns)
            lanes = pl.ds(spot * HEAD_DIM, table.shape[1])
            copy = pltpu.make_async_copy(
                table.at[span], weights.at[span, lanes], w_sem.at[i, k]
            )
            copy.start()
            tables_here.append(copy)

    lane = lax.broadcasted_iota(jnp.int32, (rows, 128), 1)
    pos = jnp.transpose(jnp.broadcast_to(position[...], (128, rows)))
    owner = jnp.where(pos >= 0, pos // tokens, -1)
    rest = jnp.where(pos >= 0, pos % tokens, 0)
    code = jnp.where(lane == 0, owner, jnp.where(lane == 1, rest, 0))
    buf = m[0]
    buf[rank, :, :width] = hidden[...]
    buf[rank, :, width:] = code.astype(jnp.float32).astype(jnp.bfloat16)
    greet()
    squares, merged = merge_part(
        hidden, merger_here, position, prompt_here, stream, fetches[0], fetches[1], m
    )

    def clear():
        acc[...] = jnp.zeros_like(acc)
        total[...] = jnp.zeros_like(total)
        top[...] = jnp.full_like(top, -1e30)

    projected = project_part(1e-06, squares, stream, gain, tables_here, sums, clear, p)
    fetches[2].wait()
    fetches[3].wait()

    cosine_wide = jnp.concatenate([cosine_here[...], cosine_here[...]], axis=1)
    sine_wide = jnp.concatenate([-sine_here[...], sine_here[...]], axis=1)

    def turned(h):
        u = sums[:, h * HEAD_DIM : (h + 1) * HEAD_DIM]
        u = u * cosine_wide + pltpu.roll(u, HEAD_DIM // 2, 1) * sine_wide
        return u.astype(jnp.bfloat16)

    keys[rank, :, :HEAD_DIM] = turned(heads)
    keys[rank, :, HEAD_DIM:] = sums[:, (heads + 1) * HEAD_DIM :].astype(jnp.bfloat16)
    steps, k_sent = plane_steps(keys, k_full, k_half, k_send)
    steps[0][0]()
    for h in range(heads):
        queries[h] = turned(h)
    steps[1][0]()
    attend_part(queries, keys, context_out, acc, top, total, scores, bias, steps[2:])
    k_sent()
    projected()
    merged()


def together(hidden, merger_out, position, prompt, gain, wq, wk, wv, cosine, sine):
    rows, width = hidden.shape
    groups = lax.axis_size("role") * lax.axis_size("seq")
    tokens, columns = prompt.shape
    strip = merger_out.shape[1]
    quarter = groups // 4
    slots = groups * quarter * (2 * rows // groups)
    heads = wq.shape[1] // HEAD_DIM
    wide = wq.shape[1] + 2 * HEAD_DIM
    dma = pltpu.SemaphoreType.DMA
    vmem = pl.BlockSpec(memory_space=pltpu.VMEM)
    hbm = pl.BlockSpec(memory_space=pl.ANY)
    bf16, f32 = jnp.bfloat16, jnp.float32
    return pl.pallas_call(
        kernel,
        out_shape=(
            jax.ShapeDtypeStruct(prompt.shape, bf16),
            jax.ShapeDtypeStruct((tokens, wq.shape[1]), bf16),
        ),
        in_specs=[vmem, hbm, vmem, hbm, vmem, hbm, hbm, hbm, hbm, hbm],
        out_specs=(vmem, vmem),
        scratch_shapes=[
            pltpu.VMEM(merger_out.shape, bf16),
            pltpu.VMEM(prompt.shape, bf16),
            pltpu.VMEM((heads, tokens, HEAD_DIM), bf16),
            pltpu.VMEM(cosine.shape, f32),
            pltpu.VMEM(sine.shape, f32),
            pltpu.VMEM((tokens, wide), f32),
            pltpu.VMEM((groups, tokens, 2 * HEAD_DIM), bf16),
            dma((groups,)),
            dma((groups, 2)),
            dma((PLANE_SENDS,)),
            pltpu.VMEM((heads, tokens, HEAD_DIM), f32),
            pltpu.VMEM((heads, tokens, HEAD_DIM), f32),
            pltpu.VMEM((heads, tokens, HEAD_DIM), f32),
            pltpu.VMEM((2, tokens, SIDE * tokens), f32),
            pltpu.VMEM((tokens, SIDE * tokens), f32),
            dma((4,)),
            dma((4, 3)),
            pltpu.VMEM((groups, rows, width + 128), bf16),
            dma((groups,)),
            dma((groups, 2)),
            dma((PLANE_SENDS,)),
            pltpu.VMEM((8, 3, rows, strip), bf16),
            pltpu.VMEM((3, quarter, rows, strip), bf16),
            pltpu.VMEM((quarter, rows, strip), f32),
            dma((8, 3)),
            dma((3, quarter)),
            pltpu.VMEM((quarter * rows, slots), bf16),
            pltpu.VMEM((tokens, 128), f32),
            pltpu.VMEM((slots, strip), bf16),
            pltpu.VMEM((8, slots // 8, strip), bf16),
            dma((groups,)),
            dma((groups,)),
            pltpu.VMEM((4, CHUNKS, tokens, columns // CHUNKS), bf16),
            pltpu.VMEM((4 * columns, wide), bf16),
            pltpu.VMEM((4, 8, tokens), f32),
            dma((3,)),
            dma((3,)),
            dma((3 * CHUNKS,)),
            dma((4, CHUNKS)),
        ],
        compiler_params=pltpu.CompilerParams(
            has_side_effects=True, vmem_limit_bytes=60 << 20, collective_id=0
        ),
    )(hidden, merger_out, position, prompt, gain, wq, wk, wv, cosine, sine)


def body(
    merger_hidden,
    merger_out,
    row_position,
    prompt_embeds,
    norm_gain,
    query_weight,
    key_weight,
    value_weight,
):
    device_rank = lax.axis_index(("role", "seq"))
    tok_count = prompt_embeds.shape[0]
    positions = device_rank * tok_count + jnp.arange(tok_count, dtype=jnp.int32)
    cosine, sine = rotary(positions)
    stream, context = together(
        merger_hidden,
        merger_out,
        row_position[None, :],
        prompt_embeds,
        norm_gain,
        query_weight,
        key_weight,
        value_weight,
        cosine,
        sine,
    )
    return (stream, context)


def solution(mesh):
    in_specs = (
        P(("role", "seq"), "tp"),
        P("tp", ("role", "seq")),
        P(("role", "seq")),
        P(("role", "seq"), "tp"),
        P("tp"),
        P(None, "tp"),
        P(None, "tp"),
        P(None, "tp"),
    )
    out_specs = (P(("role", "seq"), "tp"), P(("role", "seq"), "tp"))
    return jax.shard_map(body, mesh=mesh, in_specs=in_specs, out_specs=out_specs, check_vma=False)
```

```python
import functools
import math

import jax
import jax.numpy as jnp
from jax import lax
from jax.experimental import pallas as pl
from jax.experimental.pallas import tpu as pltpu
from jax.sharding import PartitionSpec as P

HEAD_DIM = 128


def rotary(positions):
    half_dim = HEAD_DIM // 2
    frequency = 1000000.0 ** (-jnp.arange(half_dim, dtype=jnp.float32) / half_dim)
    angles = positions.astype(jnp.float32)[:, None] * frequency[None, :]
    cosine, sine = jnp.cos(angles), jnp.sin(angles)
    return cosine, sine


MESH = pl.DeviceIdType.MESH
SIDE = 4


def remote(src, dst, send_sem, recv_sem, role, seq, tp):
    return pltpu.make_async_remote_copy(
        src_ref=src,
        dst_ref=dst,
        send_sem=send_sem,
        recv_sem=recv_sem,
        device_id=(role, seq, tp),
        device_id_type=MESH,
    )


def plane_steps(buf, full_sem, half_sem, send_sem, upward=False):
    role, seq, tp = lax.axis_index("role"), lax.axis_index("seq"), lax.axis_index("tp")
    step_a, step_b = 1 + 3 * role, 4 - 3 * role
    z, x = seq // SIDE, seq % SIDE
    ca = x + role * (z - x)
    cb = z + role * (x - z)
    half = buf.shape[1] // 2
    sent = []

    def seq_of(a, b):
        return ((ca + a + SIDE) % SIDE) * step_a + ((cb + b + SIDE) % SIDE) * step_b

    def slot_of(a, b):
        return role * (SIDE * SIDE) + seq_of(a, b)

    def whole(slot, to_role, to_seq):
        remote(
            buf.at[slot], buf.at[slot], send_sem.at[len(sent)], full_sem.at[slot], to_role, to_seq, tp
        ).start()
        sent.append((2 * half, False))

    def mate(slot):
        copy = remote(
            buf.at[slot], buf.at[slot], send_sem.at[len(sent)], full_sem.at[slot], 1 - role, seq, tp
        )
        if upward:
            pl.when(role == 0)(copy.start)
        else:
            copy.start()
        sent.append((2 * half, upward))

    def part(slot, k, to_seq):
        piece = buf.at[slot, pl.ds(k * half, half)]
        remote(
            piece, piece, send_sem.at[len(sent)], half_sem.at[slot, k], role, to_seq, tp
        ).start()
        sent.append((half, False))

    def wait_whole(slot):
        pltpu.make_async_copy(buf.at[slot], buf.at[slot], full_sem.at[slot]).wait()

    def wait_parts(slot):
        for k in range(2):
            piece = buf.at[slot, pl.ds(k * half, half)]
            pltpu.make_async_copy(piece, piece, half_sem.at[slot, k]).wait()

    def spread_b(slot):
        whole(slot, role, seq_of(0, 1))
        whole(slot, role, seq_of(0, -1))
        mate(slot)

    def pass_b(a):
        for b, k in ((-1, 0), (1, 1)):
            wait_whole(slot_of(a, b))
            part(slot_of(a, b), k, seq_of(0, -b))
            mate(slot_of(a, b))

    def other(b):
        fixed = (ca + b + SIDE) % SIDE

        def wait_all():
            for k in range(SIDE):
                wait_whole((1 - role) * (SIDE * SIDE) + fixed * step_a + k * step_b)

        if upward:
            pl.when(role == 1)(wait_all)
        else:
            wait_all()

    def start():
        own = slot_of(0, 0)
        whole(own, role, seq_of(1, 0))
        whole(own, role, seq_of(-1, 0))
        spread_b(own)

    def along():
        for a, k in ((-1, 0), (1, 1)):
            wait_whole(slot_of(a, 0))
            part(slot_of(a, 0), k, seq_of(-a, 0))
            spread_b(slot_of(a, 0))

    def first():
        pass_b(0)
        wait_parts(slot_of(2, 0))
        spread_b(slot_of(2, 0))

    def second():
        pass_b(-1)
        pass_b(1)
        other(0)

    def last():
        for a in (0, -1, 1, 2):
            wait_parts(slot_of(a, 2))
            mate(slot_of(a, 2))
        other(1)

    def mine(b):
        return role, (cb + b + SIDE) % SIDE

    def theirs(b):
        return 1 - role, (ca + b + SIDE) % SIDE

    steps = (
        (start, None),
        (along, None),
        (first, mine(0)),
        (second, theirs(0)),
        (lambda: pass_b(2), mine(-1)),
        (lambda: None, mine(1)),
        (lambda: other(-1), theirs(-1)),
        (last, theirs(1)),
        (lambda: None, mine(2)),
        (lambda: other(2), theirs(2)),
    )

    def finish():
        for n, (rows, only_lower) in enumerate(sent):
            piece = buf.at[0, pl.ds(0, rows)]
            done = pltpu.make_async_copy(piece, piece, send_sem.at[n])
            if only_lower:
                pl.when(role == 0)(done.wait)
            else:
                done.wait()

    return steps, finish


PLANE_SENDS = 2 + 3 * 4 + 2 + 8 + 12
CHUNKS = 4


def iota(shape, dim):
    return lax.broadcasted_iota(jnp.int32, shape, dim).astype(jnp.float32)


def greet():
    role, seq, tp = lax.axis_index("role"), lax.axis_index("seq"), lax.axis_index("tp")
    z, x = seq // SIDE, seq % SIDE
    barrier = pltpu.get_barrier_semaphore()

    def tell(to_role, to_seq, to_tp):
        pl.semaphore_signal(
            barrier, inc=1, device_id=(to_role, to_seq, to_tp), device_id_type=MESH
        )

    tell(1 - role, seq, tp)
    for k in (1, 3):
        tell(role, z * SIDE + (x + k) % SIDE, tp)
        tell(role, ((z + k) % SIDE) * SIDE + x, tp)
    for k in (1, 2, 3):
        tell(role, seq, (tp + k) % 4)

    pl.semaphore_wait(barrier, 8)


def merge_part(
    hidden, weight, position, prompt, stream, weight_here, prompt_here, m
):
    (
        buf,
        full_sem,
        half_sem,
        send_sem,
        partial,
        landed,
        mine,
        y_send,
        y_recv,
        table,
        place,
        packed,
        arrived,
        d_send,
        d_recv,
    ) = m
    role, seq, tp = lax.axis_index("role"), lax.axis_index("seq"), lax.axis_index("tp")
    rank = role * lax.axis_size("seq") + seq
    rows, width = hidden.shape
    tokens = prompt.shape[0]
    groups = buf.shape[0]
    columns = weight.shape[1]
    capacity = 2 * rows // groups
    quarter = groups // 4
    some = SIDE * rows
    copies = []

    def on_line(of_role, fixed):
        n = len(copies) // 3
        if n == 0:
            weight_here.wait()
        step_a, step_b = 1 + 3 * of_role, 4 - 3 * of_role
        pieces, spots = [], []
        for d in (2, 1, 3, 0):
            along = (tp + d + SIDE - fixed) % SIDE
            slot = of_role * (SIDE * SIDE) + along * step_a + fixed * step_b
            pieces.append(buf[slot, :, :width])
            spots.append(of_role * SIDE + fixed + of_role * (along - fixed))
        value = jnp.dot(
            jnp.concatenate(pieces, axis=0), weight[...], preferred_element_type=jnp.float32
        )
        for k, d in enumerate((2, 1, 3)):
            partial[n, k] = value[k * rows : (k + 1) * rows].astype(jnp.bfloat16)
            copy = remote(
                partial.at[n, k],
                landed.at[3 - d, spots[k]],
                y_send.at[n, k],
                y_recv.at[3 - d, spots[k]],
                role,
                seq,
                (tp + d) % 4,
            )
            copy.start()
            copies.append(copy)
        mine[spots[3]] = value[3 * rows :]

    steps, sent = plane_steps(buf, full_sem, half_sem, send_sem)
    for step, line in steps:
        step()
        if line is not None:
            on_line(*line)

    r0 = lax.broadcasted_iota(jnp.int32, (some, some), 0)
    r1 = lax.broadcasted_iota(jnp.int32, (some, some), 1)
    lower = jnp.where((r1 < r0) & (r1 // rows == r0 // rows), 1.0, 0.0).astype(jnp.bfloat16)
    source = lax.broadcasted_iota(jnp.int32, (some, 1), 0) // rows

    def decode(got):
        got = got.astype(jnp.float32)
        owner, rest = got[:, 0:1], got[:, 1:2]
        onehot = jnp.where(owner == iota((some, 128), 1), 1.0, 0.0)
        before = jnp.dot(lower, onehot.astype(jnp.bfloat16), preferred_element_type=jnp.float32)
        return owner, rest, jnp.sum(before * onehot, axis=1, keepdims=True)

    for n in range(quarter // SIDE):
        got = jnp.concatenate(
            [buf[n * 16 + z * SIDE + (tp + SIDE - z) % SIDE, :, width:] for z in range(SIDE)],
            axis=0,
        )
        owner, rest, earlier = decode(got)
        spot = (source + n * SIDE).astype(jnp.float32)
        slot = owner * (quarter * capacity) + spot * capacity + earlier
        table[n * some : (n + 1) * some, :] = jnp.where(
            slot == iota((some, table.shape[1]), 1), 1.0, 0.0
        ).astype(jnp.bfloat16)
    place[...] = jnp.zeros_like(place)

    @pl.loop(0, groups // SIDE)
    def _(n):
        got = buf[pl.ds(n * SIDE, SIDE), :, width:].reshape(some, 128)
        owner, rest, earlier = decode(got)
        here = (rest == iota((some, tokens), 1)) & (owner == rank.astype(jnp.float32))
        spot = ((source + n % SIDE) % SIDE) * quarter + n
        slot = spot.astype(jnp.float32) * capacity + earlier
        there = slot == iota((some, 128), 1)
        place[...] += lax.dot_general(
            jnp.where(here, 1.0, 0.0).astype(jnp.bfloat16),
            jnp.where(there, 1.0, 0.0).astype(jnp.bfloat16),
            (((0,), (0,)), ((), ())),
            preferred_element_type=jnp.float32,
        )

    for i in range(quarter):
        for k in range(3):
            got = landed.at[k, i]
            pltpu.make_async_copy(got, got, y_recv.at[k, i]).wait()
            mine[i] += landed[k, i].astype(jnp.float32)
    packed[...] = lax.dot_general(
        table[...],
        mine[...].reshape(quarter * rows, columns).astype(jnp.bfloat16),
        (((0,), (0,)), ((), ())),
        preferred_element_type=jnp.float32,
    ).astype(jnp.bfloat16)

    piece = quarter * capacity
    to_tp = rank // 8
    lane_group = rank % 8

    def sending(i):
        j = (rank + i) % groups
        return remote(
            packed.at[pl.ds(pl.multiple_of(j * piece, piece), piece)],
            arrived.at[lane_group, pl.ds(pl.multiple_of(tp * piece, piece), piece)],
            d_send.at[i],
            d_recv.at[lane_group * 4 + tp],
            j // 16,
            j % 16,
            to_tp,
        )

    def staying():
        return pltpu.make_async_copy(
            packed.at[pl.ds(pl.multiple_of(rank * piece, piece), piece)],
            arrived.at[lane_group, pl.ds(pl.multiple_of(tp * piece, piece), piece)],
            d_recv.at[lane_group * 4 + tp],
        )

    @pl.when(to_tp == tp)
    def _():
        staying().start()

    @pl.when(to_tp != tp)
    def _():
        sending(0).start()

    @pl.loop(1, groups)
    def _(i):
        sending(i).start()

    chosen = place[...].astype(jnp.bfloat16)
    hit = jnp.max(place[...], axis=1, keepdims=True) > 0.5
    prompt_here.wait()
    total = jnp.zeros((tokens, 128), jnp.float32)
    for c in range(8):
        for k in range(4):
            got = arrived.at[c, pl.ds(k * piece, piece)]
            pltpu.make_async_copy(got, got, d_recv.at[c * 4 + k]).wait()
        rows_here = jnp.dot(chosen, arrived[c], preferred_element_type=jnp.float32)
        span = slice(c * columns, (c + 1) * columns)
        x = jnp.where(hit, rows_here, prompt[:, span].astype(jnp.float32))
        stream[:, span] = x.astype(jnp.bfloat16)
        for k in range(0, columns, 128):
            total = total + x[:, k : k + 128] * x[:, k : k + 128]

    def finish():
        sent()
        for copy in copies:
            copy.wait_send()

        @pl.when(to_tp != tp)
        def _():
            sending(0).wait_send()

        @pl.loop(1, groups)
        def _(i):
            sending(i).wait_send()

    return total, finish


def project_part(eps, total, stream, gain, tables_here, acc, meanwhile, m):
    normed, weights, squares, s_send, s_recv, n_send, n_recv = m
    role, seq, tp = lax.axis_index("role"), lax.axis_index("seq"), lax.axis_index("tp")
    rows, columns = stream.shape
    chunk = columns // CHUNKS
    squares[3] = jnp.broadcast_to(
        jnp.sum(jnp.transpose(total), axis=0, keepdims=True), (8, rows)
    )
    sums = []
    for k, off in enumerate((1, 3, 2)):
        copy = remote(
            squares.at[3], squares.at[k], s_send.at[k], s_recv.at[k], role, seq, (tp + off) % 4
        )
        copy.start()
        sums.append(copy)
    meanwhile()
    for copy in sums:
        copy.wait()
    whole = squares[0] + squares[1] + (squares[2] + squares[3])
    whole = jnp.broadcast_to(whole[0:1], (128, rows))
    inverse = lax.rsqrt(jnp.transpose(whole) / (4 * columns) + eps)[:, 0:1]

    copies = []

    def send(t, c, off):
        copy = remote(
            normed.at[t, c],
            normed.at[t, c],
            n_send.at[len(copies)],
            n_recv.at[t, c],
            role,
            seq,
            (tp + off + 4) % 4,
        )
        copy.start()
        copies.append(copy)

    def arrive(t, c):
        pltpu.make_async_copy(normed.at[t, c], normed.at[t, c], n_recv.at[t, c]).wait()

    def scale(c):
        span = slice(c * chunk, (c + 1) * chunk)
        x = stream[:, span].astype(jnp.float32)
        normed[tp, c] = (x * inverse * gain[span].astype(jnp.float32).reshape(1, chunk)).astype(jnp.bfloat16)

    scale(0)
    send(tp, 0, 1)
    scale(2)
    send(tp, 2, -1)
    scale(1)
    send(tp, 1, 1)
    scale(3)
    send(tp, 3, -1)
    send(tp, 2, 1)
    send(tp, 0, -1)
    send(tp, 3, 1)
    send(tp, 1, -1)
    before, after, across = (tp + 3) % 4, (tp + 1) % 4, (tp + 2) % 4

    def multiply(t, c, first=False):
        span = pl.ds(pl.multiple_of(t * columns + c * chunk, chunk), chunk)
        value = jnp.dot(normed[t, c], weights[span, :], preferred_element_type=jnp.float32)
        if first:
            acc[...] = value
        else:
            acc[...] += value

    for copy in tables_here:
        copy.wait()
    for c in range(CHUNKS):
        multiply(tp, c, c == 0)
    for c, d in ((0, 2), (1, 3)):
        arrive(before, c)
        send(before, c, 1)
        arrive(after, d)
        send(after, d, -1)
        multiply(before, c)
        multiply(after, d)
    for c, d in ((2, 0), (3, 1)):
        arrive(before, c)
        multiply(before, c)
        arrive(after, d)
        multiply(after, d)
    for c in (0, 2, 1, 3):
        arrive(across, c)
        multiply(across, c)

    def finish():
        for copy in copies:
            copy.wait_send()

    return finish


def attend_part(q_ref, buf, o_ref, acc, top, total, scores, bias, steps):
    heads, rows = q_ref.shape[:2]
    role, seq = lax.axis_index("role"), lax.axis_index("seq")
    z, x = seq // SIDE, seq % SIDE
    rank = role * (SIDE * SIDE) + seq
    factor = math.log2(math.e) / math.sqrt(HEAD_DIM)
    span = SIDE * rows

    def block(slots, masked):
        k = jnp.concatenate([buf[slot, :, :HEAD_DIM] for slot in slots], axis=0)
        v = jnp.concatenate([buf[slot, :, HEAD_DIM:] for slot in slots], axis=0)
        if masked:
            ahead = lax.broadcasted_iota(jnp.int32, (rows, rows), 1) - lax.broadcasted_iota(
                jnp.int32, (rows, rows), 0
            )
            for n, slot in enumerate(slots):
                bias[:, n * rows : (n + 1) * rows] = jnp.where(
                    ahead <= (rank - slot) * rows, 0.0, -1e30
                )

        def score(h):
            scores[h % 2] = lax.dot_general(
                q_ref[h], k, (((1,), (1,)), ((), ())), preferred_element_type=jnp.float32
            )

        score(0)
        for h in range(heads):
            if h + 1 < heads:
                score(h + 1)
            s = scores[h % 2]
            if masked:
                s = s + bias[...]
            old = top[h][:, :1]
            new = jnp.maximum(old, jnp.max(s, axis=1, keepdims=True))
            p = jnp.exp2((s - new) * factor)
            alpha = jnp.exp2((old - new) * factor)
            part = p[:, :HEAD_DIM]
            for c in range(HEAD_DIM, span, HEAD_DIM):
                part = part + p[:, c : c + HEAD_DIM]
            total[h] = total[h] * alpha + part
            acc[h] = acc[h] * alpha + jnp.dot(
                p.astype(jnp.bfloat16), v, preferred_element_type=jnp.float32
            )
            top[h] = jnp.broadcast_to(new, (rows, HEAD_DIM))

    @pl.loop(0, len(steps))
    def _(e):
        for n, (step, _) in enumerate(steps):
            pl.when(e == n)(step)
        of_role, fixed = steps[0][1]
        for n, (_, line) in enumerate(steps):
            of_role = jnp.where(e == n, line[0], of_role)
            fixed = jnp.where(e == n, line[1], fixed)
        step_a, step_b = 1 + 3 * of_role, 4 - 3 * of_role
        slots = [
            of_role * (SIDE * SIDE) + along * step_a + fixed * step_b for along in range(SIDE)
        ]
        clear = slots[-1] < rank
        some = slots[0] <= rank
        pl.when(clear)(lambda: block(slots, False))
        pl.when(some & jnp.logical_not(clear))(lambda: block(slots, True))

    for h in range(heads):
        l = jnp.sum(total[h], axis=1, keepdims=True)
        o_ref[:, h * HEAD_DIM : (h + 1) * HEAD_DIM] = (acc[h] / l).astype(o_ref.dtype)


MERGE_SCRATCH = 15
PROJECT_SCRATCH = 7


def kernel(
    hidden,
    merger_out,
    position,
    prompt,
    gain,
    query_weight,
    key_weight,
    value_weight,
    cosine,
    sine,
    stream,
    context_out,
    merger_here,
    prompt_here,
    queries,
    cosine_here,
    sine_here,
    sums,
    keys,
    k_full,
    k_half,
    k_send,
    acc,
    top,
    total,
    scores,
    bias,
    in_sem,
    w_sem,
    *more,
):
    m, p = more[:MERGE_SCRATCH], more[MERGE_SCRATCH:]
    role, seq, tp = lax.axis_index("role"), lax.axis_index("seq"), lax.axis_index("tp")
    rank = role * lax.axis_size("seq") + seq
    rows, width = hidden.shape
    tokens = prompt.shape[0]
    columns = prompt.shape[1]
    heads = query_weight.shape[1] // HEAD_DIM

    fetches = []
    for k, (src, dst) in enumerate(
        (
            (merger_out, merger_here),
            (prompt, prompt_here),
            (cosine, cosine_here),
            (sine, sine_here),
        )
    ):
        copy = pltpu.make_async_copy(src, dst, in_sem.at[k])
        copy.start()
        fetches.append(copy)
    weights = p[1]
    tables_here = []
    for i in range(4):
        for k, (table, spot) in enumerate(
            ((query_weight, 0), (key_weight, heads), (value_weight, heads + 1))
        ):
            span = pl.ds(i * columns, columns)
            lanes = pl.ds(spot * HEAD_DIM, table.shape[1])
            copy = pltpu.make_async_copy(
                table.at[span], weights.at[span, lanes], w_sem.at[i, k]
            )
            copy.start()
            tables_here.append(copy)

    lane = lax.broadcasted_iota(jnp.int32, (rows, 128), 1)
    pos = jnp.transpose(jnp.broadcast_to(position[...], (128, rows)))
    owner = jnp.where(pos >= 0, pos // tokens, -1)
    rest = jnp.where(pos >= 0, pos % tokens, 0)
    code = jnp.where(lane == 0, owner, jnp.where(lane == 1, rest, 0))
    buf = m[0]
    buf[rank, :, :width] = hidden[...]
    buf[rank, :, width:] = code.astype(jnp.float32).astype(jnp.bfloat16)
    greet()
    squares, merged = merge_part(
        hidden, merger_here, position, prompt_here, stream, fetches[0], fetches[1], m
    )

    def clear():
        acc[...] = jnp.zeros_like(acc)
        total[...] = jnp.zeros_like(total)
        top[...] = jnp.full_like(top, -1e30)

    projected = project_part(1e-06, squares, stream, gain, tables_here, sums, clear, p)
    fetches[2].wait()
    fetches[3].wait()

    cosine_wide = jnp.concatenate([cosine_here[...], cosine_here[...]], axis=1)
    sine_wide = jnp.concatenate([-sine_here[...], sine_here[...]], axis=1)

    def turned(h):
        u = sums[:, h * HEAD_DIM : (h + 1) * HEAD_DIM]
        u = u * cosine_wide + pltpu.roll(u, HEAD_DIM // 2, 1) * sine_wide
        return u.astype(jnp.bfloat16)

    keys[rank, :, :HEAD_DIM] = turned(heads)
    keys[rank, :, HEAD_DIM:] = sums[:, (heads + 1) * HEAD_DIM :].astype(jnp.bfloat16)
    steps, k_sent = plane_steps(keys, k_full, k_half, k_send, upward=True)
    steps[0][0]()
    for h in range(heads):
        queries[h] = turned(h)
    steps[1][0]()
    attend_part(queries, keys, context_out, acc, top, total, scores, bias, steps[2:])
    k_sent()
    projected()
    merged()


def together(hidden, merger_out, position, prompt, gain, wq, wk, wv, cosine, sine):
    rows, width = hidden.shape
    groups = lax.axis_size("role") * lax.axis_size("seq")
    tokens, columns = prompt.shape
    strip = merger_out.shape[1]
    quarter = groups // 4
    slots = groups * quarter * (2 * rows // groups)
    heads = wq.shape[1] // HEAD_DIM
    wide = wq.shape[1] + 2 * HEAD_DIM
    dma = pltpu.SemaphoreType.DMA
    vmem = pl.BlockSpec(memory_space=pltpu.VMEM)
    hbm = pl.BlockSpec(memory_space=pl.ANY)
    bf16, f32 = jnp.bfloat16, jnp.float32
    return pl.pallas_call(
        kernel,
        out_shape=(
            jax.ShapeDtypeStruct(prompt.shape, bf16),
            jax.ShapeDtypeStruct((tokens, wq.shape[1]), bf16),
        ),
        in_specs=[vmem, hbm, vmem, hbm, vmem, hbm, hbm, hbm, hbm, hbm],
        out_specs=(vmem, vmem),
        scratch_shapes=[
            pltpu.VMEM(merger_out.shape, bf16),
            pltpu.VMEM(prompt.shape, bf16),
            pltpu.VMEM((heads, tokens, HEAD_DIM), bf16),
            pltpu.VMEM(cosine.shape, f32),
            pltpu.VMEM(sine.shape, f32),
            pltpu.VMEM((tokens, wide), f32),
            pltpu.VMEM((groups, tokens, 2 * HEAD_DIM), bf16),
            dma((groups,)),
            dma((groups, 2)),
            dma((PLANE_SENDS,)),
            pltpu.VMEM((heads, tokens, HEAD_DIM), f32),
            pltpu.VMEM((heads, tokens, HEAD_DIM), f32),
            pltpu.VMEM((heads, tokens, HEAD_DIM), f32),
            pltpu.VMEM((2, tokens, SIDE * tokens), f32),
            pltpu.VMEM((tokens, SIDE * tokens), f32),
            dma((4,)),
            dma((4, 3)),
            pltpu.VMEM((groups, rows, width + 128), bf16),
            dma((groups,)),
            dma((groups, 2)),
            dma((PLANE_SENDS,)),
            pltpu.VMEM((8, 3, rows, strip), bf16),
            pltpu.VMEM((3, quarter, rows, strip), bf16),
            pltpu.VMEM((quarter, rows, strip), f32),
            dma((8, 3)),
            dma((3, quarter)),
            pltpu.VMEM((quarter * rows, slots), bf16),
            pltpu.VMEM((tokens, 128), f32),
            pltpu.VMEM((slots, strip), bf16),
            pltpu.VMEM((8, slots // 8, strip), bf16),
            dma((groups,)),
            dma((groups,)),
            pltpu.VMEM((4, CHUNKS, tokens, columns // CHUNKS), bf16),
            pltpu.VMEM((4 * columns, wide), bf16),
            pltpu.VMEM((4, 8, tokens), f32),
            dma((3,)),
            dma((3,)),
            dma((3 * CHUNKS,)),
            dma((4, CHUNKS)),
        ],
        compiler_params=pltpu.CompilerParams(
            has_side_effects=True, vmem_limit_bytes=60 << 20, collective_id=0
        ),
    )(hidden, merger_out, position, prompt, gain, wq, wk, wv, cosine, sine)


def body(
    merger_hidden,
    merger_out,
    row_position,
    prompt_embeds,
    norm_gain,
    query_weight,
    key_weight,
    value_weight,
):
    device_rank = lax.axis_index(("role", "seq"))
    tok_count = prompt_embeds.shape[0]
    positions = device_rank * tok_count + jnp.arange(tok_count, dtype=jnp.int32)
    cosine, sine = rotary(positions)
    stream, context = together(
        merger_hidden,
        merger_out,
        row_position[None, :],
        prompt_embeds,
        norm_gain,
        query_weight,
        key_weight,
        value_weight,
        cosine,
        sine,
    )
    return (stream, context)


def solution(mesh):
    in_specs = (
        P(("role", "seq"), "tp"),
        P("tp", ("role", "seq")),
        P(("role", "seq")),
        P(("role", "seq"), "tp"),
        P("tp"),
        P(None, "tp"),
        P(None, "tp"),
        P(None, "tp"),
    )
    out_specs = (P(("role", "seq"), "tp"), P(("role", "seq"), "tp"))
    return jax.shard_map(body, mesh=mesh, in_specs=in_specs, out_specs=out_specs, check_vma=False)
```
